32 devices in a mesh: row: 8 (over z, y), col: 4 (over x, core).
Axes of the slice: x: 2, y: 2, z: 4, core: 2. Of those that a mesh axis runs over, the one named last changes fastest.
Arguments:
- inputs: float32 [16384, 768], P(('row', 'col')), may hold values from -25 to 25, as said below
- cotangent: float32 [16384, 768], P(('row', 'col')), may hold values from -6 to 6
- token_order: int32 [16384], P('row'), may hold values from 0 to 16383, as said below
- token_place: int32 [16384], P('row'), may hold values from 0 to 16383, as said below
- seq_lengths: int32 [8, 8], P('row'), may hold values from 1 to 512, 2048 in all within a row
- query_weight: bfloat16 [768, 768], P('row', 'col'), may hold values from -0.21875 to 0.21875
- key_weight: bfloat16 [768, 768], P('row', 'col'), may hold values from -0.21875 to 0.21875
- value_weight: bfloat16 [768, 768], P('row', 'col'), may hold values from -0.21875 to 0.21875
- output_weight: bfloat16 [768, 768], P('col', 'row'), may hold values from -0.875 to 0.875
- inner_weight: bfloat16 [768, 3072], P('row', 'col'), may hold values from -0.21875 to 0.21875
- outer_weight: bfloat16 [3072, 768], P('col', 'row'), may hold values from -0.109375 to 0.109375
- query_bias: bfloat16 [768], P(('col', 'row')), may hold values from -3 to 3
- value_bias: bfloat16 [768], P(('col', 'row')), may hold values from -3 to 3
- output_bias: bfloat16 [768], P(('col', 'row')), may hold values from -2 to 2
- inner_bias: bfloat16 [3072], P(('col', 'row')), may hold values from -3 to 3
- outer_bias: bfloat16 [768], P(('col', 'row')), may hold values from -2 to 2
- first_gain: bfloat16 [768], P(('col', 'row')), may hold values from 0.5 to 1.5
- first_shift: bfloat16 [768], P(('col', 'row')), may hold values from -2 to 2
- second_gain: bfloat16 [768], P(('col', 'row')), may hold values from 0.5 to 1.5
- second_shift: bfloat16 [768], P(('col', 'row')), may hold values from -2 to 2
Outputs:
- output: float32 [16384, 768], P(('row', 'col'))
- input_grad: float32 [16384, 768], P(('row', 'col'))
- query_weight_grad: float32 [768, 768], P('row', 'col')
- key_weight_grad: float32 [768, 768], P('row', 'col')
- value_weight_grad: float32 [768, 768], P('row', 'col')
- output_weight_grad: float32 [768, 768], P('col', 'row')
- inner_weight_grad: float32 [768, 3072], P('row', 'col')
- outer_weight_grad: float32 [3072, 768], P('col', 'row')
- query_bias_grad: float32 [768], P(('col', 'row'))
- value_bias_grad: float32 [768], P(('col', 'row'))
- output_bias_grad: float32 [768], P(('col', 'row'))
- inner_bias_grad: float32 [3072], P(('col', 'row'))
- outer_bias_grad: float32 [768], P(('col', 'row'))
- first_gain_grad: float32 [768], P(('col', 'row'))
- first_shift_grad: float32 [768], P(('col', 'row'))
- second_gain_grad: float32 [768], P(('col', 'row'))
- second_shift_grad: float32 [768], P(('col', 'row'))
The draws below stay inside these ranges and needn't reach their ends.
Inputs may be any that keep to these rules, and one draw needn't show every extreme that they name: `inputs`: drawn from a normal or uniform law times independent row and feature scales. `token_order`: A permutation of all tokens. Every work block of 2048 rows takes exactly 256 tokens from each block of 2048 given rows. The inverse permutation of token_order: token_order[token_place[i]] = i. `seq_lengths`: each row sums to 2048; its sequences lie one after another in that work block.
All inputs are finite; a program needn't handle non-finite values.
Results may differ from the reference program's by a relative error of at most 0.013.
The reference program's roundings to bfloat16 on the way count: a program that leaves them out, or rounds other values in their place, can miss the bound.
Values may be sent and summed in bfloat16 or wider, within the bound.
A program may use at most 128 MiB of HBM per device.

```python
import math
import jax
import jax.numpy as jnp
import numpy as np
from jax import lax

D = 768
H = 12
HD = 64
FF = 3072
TOK_GRP = 2048
SEQS = 8
QBLOCK = 512
LONGEST = 512
GROUPS = 8
TOKENS = 16384
SLICE_TOK = 256


def draw_inputs(key, part):
    key_parts = jax.random.split(jax.random.fold_in(key, 11), 3)
    columns = (jnp.arange(D, dtype=jnp.float32) + jax.random.uniform(key_parts[0], (D,))) / D
    col_scale = 0.3 * jnp.exp(columns * 2.302585092994046)
    row_scale = jnp.exp(jax.random.uniform(key_parts[1], (TOKENS, 1), minval=-0.5, maxval=0.7))
    base_vals = jax.random.normal(key_parts[2], (TOKENS, D))
    base_vals = jnp.clip(base_vals, -4.0, 4.0)
    return (base_vals * row_scale * col_scale).astype(jnp.float32)


def deal_tables(key):
    groups_all = TOKENS // TOK_GRP
    block_key, source_key = jax.random.split(jax.random.fold_in(key, 29))
    shuffles = jax.vmap(lambda sub_key: jax.random.permutation(sub_key, TOK_GRP))(jax.random.split(block_key, groups_all)).astype(jnp.int32)
    sources = shuffles // SLICE_TOK
    within = shuffles % SLICE_TOK
    slot_index = jnp.arange(groups_all, dtype=jnp.int32)[:, None] * SLICE_TOK + within
    scrambles = jax.vmap(lambda sub_key: jax.random.permutation(sub_key, TOK_GRP))(jax.random.split(source_key, groups_all)).astype(jnp.int32)
    local_rows = scrambles[sources, slot_index]
    token_order = (sources * TOK_GRP + local_rows).reshape(TOKENS).astype(jnp.int32)
    token_place = jnp.zeros((TOKENS,), jnp.int32).at[token_order].set(jnp.arange(TOKENS, dtype=jnp.int32))
    return (token_order, token_place)


def draw_token_order(key, part):
    return deal_tables(key)[0]


def draw_token_place(key, part):
    return deal_tables(key)[1]


def level_of(key, extent, shards, least, largest):
    loudness = 1.0
    for position, blocks in shards:
        steps = jax.random.uniform(jax.random.fold_in(jax.random.fold_in(key, 6), position), (blocks,), jnp.float32, least / len(shards), largest / len(shards))
        loudness = loudness * jnp.repeat(jnp.exp(steps), extent[position] // blocks).reshape((-1,) + (1,) * (len(extent) - 1 - position))
    return loudness


def profile(number_of, total, reach, lean):
    loads = [(1 << 20) // math.isqrt(rank ** lean) + 1 for rank in range(2, number_of + 1)]
    surplus, given = total - reach - (number_of - 1), [1] * (number_of - 1)
    while surplus > 0:
        movable = [i for i in range(number_of - 1) if given[i] < reach]
        mass, left = sum([loads[i] for i in movable]), surplus
        for i in movable:
            extra = min(reach - given[i], max(1, left * loads[i] // mass), surplus)
            given[i] = given[i] + extra
            surplus = surplus - extra
    return np.array([reach] + given)


def uneven_parts(stream_key, amount, total, most, lean):
    if amount == 2:
        one = jax.random.randint(stream_key, (), max(1, total - most), min(most, total - 1) + 1)
        return jnp.stack([one, total - one])
    lengths = jnp.asarray(profile(amount, total, most, lean), jnp.int32)
    twos = (amount - 1) // 2
    donor, receiver = lengths[1:1 + 2 * twos:2], lengths[2:2 + 2 * twos:2]
    margin = jnp.minimum(donor - 1, most - receiver)
    shifted = jax.random.randint(jax.random.fold_in(stream_key, 1), (twos,), 0, 1 << 20) % (margin + 1)
    lengths = lengths.at[1:1 + 2 * twos:2].set(donor - shifted).at[2:2 + 2 * twos:2].set(receiver + shifted)
    return lengths[jax.random.permutation(jax.random.fold_in(stream_key, 2), amount)]


def gaussian(own_key, dims, width, limit, cuts=(), kind=jnp.bfloat16):
    array = jax.random.normal(own_key, dims, jnp.float32) * width
    if len(cuts) > 0:
        array = level_of(own_key, dims, cuts, -0.22, 0.18) * array
    return jnp.clip(array, min=-limit, max=limit).astype(kind)


def setup_inputs(seed: int = 0) -> dict:
    splits = jax.random.split(jax.random.key(seed), 21)
    return {
        "inputs": draw_inputs(jax.random.fold_in(splits[20], 71), 0),
        "cotangent": gaussian(splits[1], (TOKENS, D), 1.0, 6.0, ((0, 32),), jnp.float32),
        "token_order": draw_token_order(jax.random.fold_in(splits[20], 71), 0),
        "token_place": draw_token_place(jax.random.fold_in(splits[20], 71), 0),
        "seq_lengths": jax.vmap(lambda own: uneven_parts(own, SEQS, TOK_GRP, LONGEST, 2))(jax.random.split(splits[4], GROUPS)).reshape((GROUPS, SEQS)).astype(jnp.int32),
        "query_weight": gaussian(splits[5], (D, D), D ** -0.5, 0.21875, ((0, 8), (1, 4))),
        "key_weight": gaussian(splits[6], (D, D), D ** -0.5, 0.21875, ((0, 8), (1, 4))),
        "value_weight": gaussian(splits[7], (D, D), D ** -0.5, 0.21875, ((0, 8), (1, 4))),
        "output_weight": gaussian(splits[8], (D, D), (D // 16) ** -0.5, 0.875, ((0, 4), (1, 8))),
        "inner_weight": gaussian(splits[9], (D, FF), D ** -0.5, 0.21875, ((0, 8), (1, 4))),
        "outer_weight": gaussian(splits[10], (FF, D), FF ** -0.5, 0.109375, ((0, 4), (1, 8))),
        "query_bias": gaussian(splits[11], (D,), 0.5, 3.0, ((0, 32),)),
        "value_bias": gaussian(splits[12], (D,), 0.5, 3.0, ((0, 32),)),
        "output_bias": gaussian(splits[13], (D,), 0.3, 2.0, ((0, 32),)),
        "inner_bias": gaussian(splits[14], (FF,), 0.5, 3.0, ((0, 32),)),
        "outer_bias": gaussian(splits[15], (D,), 0.3, 2.0, ((0, 32),)),
        "first_gain": jnp.clip(1.0 + 0.1 * jax.random.normal(splits[16], (D,), jnp.float32), 0.5, 1.5).astype(jnp.bfloat16),
        "first_shift": gaussian(splits[17], (D,), 0.3, 2.0, ((0, 32),)),
        "second_gain": jnp.clip(1.0 + 0.1 * jax.random.normal(splits[18], (D,), jnp.float32), 0.5, 1.5).astype(jnp.bfloat16),
        "second_shift": gaussian(splits[19], (D,), 0.3, 2.0, ((0, 32),)),
    }


@jax.custom_vjp
def low(v):
    return lax.optimization_barrier(v.astype(jnp.bfloat16)).astype(jnp.float32)

@jax.custom_vjp
def low_back(v):
    return v

def low_keep(v):
    return (low(v), None)

def low_pass(kept, grad):
    return (grad,)

def back_keep(v):
    return (v, None)

def back_low(kept, grad):
    return (low(grad),)
low.defvjp(low_keep, low_pass)
low_back.defvjp(back_keep, back_low)
norm_eps = 1e-12
high_mode = lax.Precision.HIGHEST
root_half = 0.7071067811865476

def round_both(value):
    return low(low_back(value))

def matmul(left, right):
    return jnp.dot(left, right, precision=high_mode, preferred_element_type=jnp.float32)

def layer_norm(resid_in, gain_vec, shift_vec):
    center = resid_in - lax.optimization_barrier(jnp.mean(resid_in, axis=-1, keepdims=True))
    spread = lax.optimization_barrier(jnp.mean(center * center, axis=-1, keepdims=True))
    return center * lax.rsqrt(spread + norm_eps) * gain_vec + shift_vec

def segment_ids(group_lengths):
    seq_ends = jnp.cumsum(group_lengths).astype(jnp.int32)
    places = jnp.arange(TOK_GRP, dtype=jnp.int32)
    return lax.optimization_barrier(jnp.sum((places[:, None] >= seq_ends[None, :]).astype(jnp.int32), axis=1)).astype(jnp.int32)

def attend(queries, keys_all, values_all, seg_ids):
    key_heads = keys_all.reshape(TOK_GRP, H, HD)
    value_heads = values_all.reshape(TOK_GRP, H, HD)
    score_scale = HD ** (-0.5)

    @jax.checkpoint
    def one_block(block_args):
        query_block, seg_block = block_args
        scores = jnp.einsum('qhd,khd->hqk', query_block, key_heads, precision=high_mode) * score_scale
        scores = low_back(scores)
        allowed = seg_block[:, None] == seg_ids[None, :]
        scores = jnp.where(allowed[None], scores, -1e+30)
        row_top = lax.optimization_barrier(jnp.max(scores, axis=2, keepdims=True))
        weights = jnp.exp(scores - row_top)
        prob_vals = low(weights / lax.optimization_barrier(jnp.sum(weights, axis=2, keepdims=True)))
        mixed_out = jnp.einsum('hqk,khd->qhd', prob_vals, value_heads, precision=high_mode)
        return mixed_out.reshape(QBLOCK, H * HD)
    block_count = TOK_GRP // QBLOCK
    mixed_all = lax.map(one_block, (queries.reshape(block_count, QBLOCK, H, HD), seg_ids.reshape(block_count, QBLOCK)))
    return mixed_all.reshape(TOK_GRP, H * HD)

def one_layer(tokens, seg_ids, param_set):
    query_w, key_w, value_w, output_w, inner_w, outer_w, query_b, value_b, output_b, inner_b, outer_b, first_g, first_s, second_g, second_s = param_set
    token_low = low(tokens)
    queries = round_both(matmul(token_low, query_w) + query_b)
    keys_all = round_both(matmul(token_low, key_w))
    values_all = round_both(matmul(token_low, value_w) + value_b)
    mixed = round_both(attend(queries, keys_all, values_all, seg_ids))
    branch = low_back(matmul(mixed, output_w)) + output_b
    normed = layer_norm(tokens + branch, first_g, first_s)
    normed_low = low(normed)
    inner_pre = low_back(matmul(normed_low, inner_w)) + inner_b
    hidden = low(0.5 * inner_pre * (1.0 + jax.scipy.special.erf(inner_pre * root_half)))
    outer_out = low_back(matmul(hidden, outer_w)) + outer_b
    return layer_norm(normed + outer_out, second_g, second_s)

def reference(inputs, cotangent, token_order, token_place, seq_lengths, query_weight, key_weight, value_weight, output_weight, inner_weight, outer_weight, query_bias, value_bias, output_bias, inner_bias, outer_bias, first_gain, first_shift, second_gain, second_shift):
    work_tokens = inputs[token_order].reshape(GROUPS, TOK_GRP, D)
    work_grads = cotangent[token_order].reshape(GROUPS, TOK_GRP, D)
    seg_table = jax.vmap(segment_ids)(seq_lengths)
    params = tuple((param_item.astype(jnp.float32) for param_item in (query_weight, key_weight, value_weight, output_weight, inner_weight, outer_weight, query_bias, value_bias, output_bias, inner_bias, outer_bias, first_gain, first_shift, second_gain, second_shift)))

    def forward(tokens_all, param_set):

        def group_step(running, group_args):
            group_tokens, group_segs = group_args
            return (running, one_layer(group_tokens, group_segs, param_set))
        unused, outputs = lax.scan(group_step, jnp.zeros((), jnp.float32), (tokens_all, seg_table))
        return outputs
    work_out, pull_back = jax.vjp(forward, work_tokens, params)
    token_grads, param_grads = pull_back(work_grads)
    output = work_out.reshape(TOKENS, D)[token_place]
    input_grad = token_grads.reshape(TOKENS, D)[token_place]
    return (output, input_grad, param_grads[0], param_grads[1], param_grads[2], param_grads[3], param_grads[4], param_grads[5], param_grads[6], param_grads[7], param_grads[8], param_grads[9], param_grads[10], param_grads[11], param_grads[12], param_grads[13], param_grads[14])
```

```python
import functools

import jax
import jax.numpy as jnp
from jax import lax
from jax.experimental import pallas as pl
from jax.experimental.pallas import tpu as pltpu
from jax.sharding import PartitionSpec as P

D = 768
HD = 64
FEAT = 192
HEADS = 3
QB = 256
KB = 256

norm_eps = 1e-12
root_half = 0.7071067811865476
inv_root_two_pi = 0.3989422804014327
NN = (((1,), (0,)), ((), ()))
NT = (((1,), (1,)), ((), ()))
TN = (((0,), (0,)), ((), ()))
MESH = pl.DeviceIdType.MESH
f32 = jnp.float32
bf16 = jnp.bfloat16
VM = pl.BlockSpec(memory_space=pltpu.VMEM)
SM = pl.BlockSpec(memory_space=pltpu.SMEM)


def mm(a, b, dims):
    return lax.dot_general(a, b, dims, preferred_element_type=f32)


def lane_head(rows):
    return lax.broadcasted_iota(jnp.int32, (rows, FEAT), 1) // HD


def attend_fwd_body(lo_ref, hi_ref, start_ref, end_ref, q_ref, k_ref, v_ref, mix_ref, lse_ref, s_buf):
    scale = HD ** (-0.5)
    blocks = q_ref.shape[0] // QB
    heads = lane_head(QB)

    @pl.loop(0, blocks)
    def _(qb):
        rows = pl.ds(qb * QB, QB)
        qv = q_ref[rows, :]
        qs = [jnp.where(heads == h, qv, jnp.zeros_like(qv)) for h in range(HEADS)]
        q_start = start_ref[:, rows]
        q_end = end_ref[:, rows]
        lo, hi = lo_ref[qb], hi_ref[qb]

        def scores(kb, tops):
            keys = pl.ds(pl.multiple_of(kb * KB, KB), KB)
            kv = k_ref[keys, :]
            pos = lax.broadcasted_iota(jnp.int32, (KB, QB), 0) + kb * KB
            allowed = (pos >= q_start) & (pos < q_end)
            out = []
            for h in range(HEADS):
                s = jnp.where(allowed, mm(kv, qs[h], NT) * scale, -1e30)
                s_buf[h, keys, :] = s
                out.append(jnp.maximum(tops[h], jnp.max(s, axis=0, keepdims=True)))
            return tuple(out)

        tops = lax.fori_loop(lo, hi, scores, tuple(jnp.full((1, QB), -1e30, f32) for _ in range(HEADS)))

        def weigh(kb, sums):
            keys = pl.ds(pl.multiple_of(kb * KB, KB), KB)
            out = []
            for h in range(HEADS):
                e = jnp.exp(s_buf[h, keys, :] - tops[h])
                s_buf[h, keys, :] = e
                out.append(sums[h] + jnp.sum(e, axis=0, keepdims=True))
            return tuple(out)

        sums = lax.fori_loop(lo, hi, weigh, tuple(jnp.zeros((1, QB), f32) for _ in range(HEADS)))
        inv = [1.0 / s for s in sums]

        def mix(kb, acc):
            keys = pl.ds(pl.multiple_of(kb * KB, KB), KB)
            vv = v_ref[keys, :]
            for h in range(HEADS):
                p = (s_buf[h, keys, :] * inv[h]).astype(bf16)
                acc = acc + jnp.where(heads == h, mm(p, vv, TN), 0.0)
            return acc

        acc = lax.fori_loop(lo, hi, mix, jnp.zeros((QB, FEAT), f32))
        mix_ref[rows, :] = acc.astype(bf16)
        for h in range(HEADS):
            lse_ref[pl.ds(h, 1), rows] = tops[h] + jnp.log(sums[h])


def attend_fwd(lo, hi, start, end, q, k, v):
    rows = q.shape[0]
    return pl.pallas_call(
        attend_fwd_body,
        out_shape=(
            jax.ShapeDtypeStruct((rows, FEAT), bf16),
            jax.ShapeDtypeStruct((8, rows), f32),
        ),
        in_specs=[SM, SM, VM, VM, VM, VM, VM],
        out_specs=(VM, VM),
        scratch_shapes=[pltpu.VMEM((HEADS, rows, QB), f32)],
        name="attend_fwd",
        compiler_params=pltpu.CompilerParams(vmem_limit_bytes=40 << 20),
        cost_estimate=pl.CostEstimate(flops=8_000_000_000, bytes_accessed=4_000_000, transcendentals=4_000_000),
    )(lo, hi, start, end, q, k, v)


def attend_bwd_body(
    lo_ref, hi_ref, start_ref, end_ref, q_ref, k_ref, v_ref, do_ref, lse_ref,
    dq_ref, dk_ref, dv_ref, p_buf, dp_buf, dk_acc, dv_acc,
):
    scale = HD ** (-0.5)
    blocks = q_ref.shape[0] // QB
    heads = lane_head(QB)
    key_heads = lane_head(KB)
    dk_acc[...] = jnp.zeros_like(dk_acc)
    dv_acc[...] = jnp.zeros_like(dv_acc)

    @pl.loop(0, blocks)
    def _(qb):
        rows = pl.ds(qb * QB, QB)
        qv = q_ref[rows, :]
        dv_in = do_ref[rows, :]
        qs = [jnp.where(heads == h, qv, jnp.zeros_like(qv)) for h in range(HEADS)]
        dos = [jnp.where(heads == h, dv_in, jnp.zeros_like(dv_in)) for h in range(HEADS)]
        q_start = start_ref[:, rows]
        q_end = end_ref[:, rows]
        lse = [lse_ref[pl.ds(h, 1), rows] for h in range(HEADS)]
        lo, hi = lo_ref[qb], hi_ref[qb]

        def first(kb, sums):
            keys = pl.ds(pl.multiple_of(kb * KB, KB), KB)
            kv, vv = k_ref[keys, :], v_ref[keys, :]
            pos = lax.broadcasted_iota(jnp.int32, (KB, QB), 0) + kb * KB
            allowed = (pos >= q_start) & (pos < q_end)
            out = []
            grad_v = dv_acc[keys, :]
            for h in range(HEADS):
                p = jnp.where(allowed, jnp.exp(mm(kv, qs[h], NT) * scale - lse[h]), 0.0)
                dp = mm(vv, dos[h], NT)
                p_buf[h, keys, :] = p
                dp_buf[h, keys, :] = dp
                out.append(sums[h] + jnp.sum(p * dp, axis=0, keepdims=True))
                grad_v = grad_v + mm(p.astype(bf16), dos[h], NN)
            dv_acc[keys, :] = grad_v
            return tuple(out)

        sums = lax.fori_loop(lo, hi, first, tuple(jnp.zeros((1, QB), f32) for _ in range(HEADS)))

        def second(kb, acc):
            keys = pl.ds(pl.multiple_of(kb * KB, KB), KB)
            kv = k_ref[keys, :]
            grad_k = dk_acc[keys, :]
            for h in range(HEADS):
                ds = (p_buf[h, keys, :] * (dp_buf[h, keys, :] - sums[h])).astype(bf16)
                grad_k = grad_k + mm(ds, qs[h], NN)
                acc = acc + jnp.where(heads == h, mm(ds, kv, TN), 0.0)
            dk_acc[keys, :] = grad_k
            return acc

        acc = lax.fori_loop(lo, hi, second, jnp.zeros((QB, FEAT), f32))
        dq_ref[rows, :] = (acc * scale).astype(bf16)

    dk_ref[...] = (dk_acc[...] * scale).astype(bf16)
    dv_ref[...] = dv_acc[...].astype(bf16)


def attend_bwd(lo, hi, start, end, q, k, v, do, lse):
    rows = q.shape[0]
    shape = jax.ShapeDtypeStruct((rows, FEAT), bf16)
    return pl.pallas_call(
        attend_bwd_body,
        out_shape=(shape, shape, shape),
        in_specs=[SM, SM] + [VM] * 7,
        out_specs=(VM, VM, VM),
        scratch_shapes=[
            pltpu.VMEM((HEADS, rows, QB), f32),
            pltpu.VMEM((HEADS, rows, QB), f32),
            pltpu.VMEM((rows, FEAT), f32),
            pltpu.VMEM((rows, FEAT), f32),
        ],
        name="attend_bwd",
        compiler_params=pltpu.CompilerParams(vmem_limit_bytes=48 << 20),
        cost_estimate=pl.CostEstimate(flops=20_000_000_000, bytes_accessed=6_000_000, transcendentals=4_000_000),
    )(lo, hi, start, end, q, k, v, do, lse)


def remote(src, dst, send_sem, recv_sem, device):
    return pltpu.make_async_remote_copy(
        src_ref=src, dst_ref=dst, send_sem=send_sem, recv_sem=recv_sem,
        device_id=device, device_id_type=MESH,
    )


def col_peers():
    r, c = lax.axis_index("row"), lax.axis_index("col")
    sib, nbr, diag = c + 1 - 2 * (c % 2), (c + 2) % 4, 3 - c
    return r, c, sib, nbr, diag


def norm_rows(x):
    mean = jnp.mean(x, axis=1, keepdims=True)
    center = x - mean
    var = jnp.mean(center * center, axis=1, keepdims=True)
    inv = lax.rsqrt(var + norm_eps)
    return center * inv, inv


def norm_back(grad, gain, hat, inv):
    e = grad * gain
    mean_e = jnp.mean(e, axis=1, keepdims=True)
    mean_c = jnp.mean(e * hat, axis=1, keepdims=True)
    return inv * (e - mean_e - hat * mean_c)


CH = 128


def middle_body(
    mixed_ref, tok_ref, cot_ref, wo_ref, win_ref, wout_ref, vec_ref, bin_ref,
    out_ref, g1_ref, gmix_ref, dwo_ref, dwin_ref, dwout_ref, dvec_ref, dbin_ref,
    nfull, hidden, slope, g2full, own, d2ds, d2dr, xs, xr, normed, hat1, inv1, grad2,
    ds_s, ds_r, x_s, x_r, asib_s, asib_r, anbr_s, anbr_r, afwd_s, afwd_r,
):
    r, c, sib, nbr, diag = col_peers()
    chunks = tok_ref.shape[0] // CH

    barrier = pltpu.get_barrier_semaphore()
    for peer in (sib, nbr):
        pl.semaphore_signal(barrier, inc=1, device_id=(r, peer), device_id_type=MESH)
    pl.semaphore_wait(barrier, 2)

    bo, g1, s1, b2, g2, s2 = [vec_ref[pl.ds(i, 1), :] for i in range(6)]

    def d2d(st, k):
        return remote(d2ds.at[st, k], d2dr.at[st, k], ds_s.at[st, k], ds_r.at[st, k], (r, sib))

    def xcopy(st, k):
        return remote(xs.at[st, k], xr.at[st, k], x_s.at[st, k], x_r.at[st, k], (r, nbr))

    def rs_start(st, k, part):
        d2ds[st, k, 0] = part(sib).astype(bf16)
        d2ds[st, k, 1] = part(diag).astype(bf16)
        d2d(st, k).start()
        mine = part(c)
        other = part(nbr)
        d2d(st, k).wait_recv()
        xs[st, k] = (other + d2dr[st, k, 1].astype(f32)).astype(bf16)
        xcopy(st, k).start()
        own[st, k] = mine + d2dr[st, k, 0].astype(f32)

    def rs_end(st, k):
        xcopy(st, k).wait_recv()
        return own[st, k] + xr[st, k].astype(f32)

    gathered = (nfull, g2full, g1_ref)

    def piece(st, q, k):
        return gathered[st].at[q, pl.ds(pl.multiple_of(k * CH, CH), CH), :]

    def ag_copy(st, k, q, sems, target):
        return remote(piece(st, q, k), piece(st, q, k), sems[0].at[st, k], sems[1].at[st, k], (r, target))

    to_sib = functools.partial(ag_copy, sems=(asib_s, asib_r), target=sib)
    to_nbr = functools.partial(ag_copy, sems=(anbr_s, anbr_r), target=nbr)
    fwd = functools.partial(ag_copy, sems=(afwd_s, afwd_r), target=sib)

    def ag_start(st, k, value):
        gathered[st][c, pl.ds(pl.multiple_of(k * CH, CH), CH), :] = value
        to_nbr(st, k, c).start()
        to_sib(st, k, c).start()

    def ag_end(st, k):
        to_nbr(st, k, c).wait_recv()
        fwd(st, k, nbr).start()
        to_sib(st, k, c).wait_recv()
        fwd(st, k, nbr).wait_recv()

    def rows_of(k):
        return pl.ds(pl.multiple_of(k * CH, CH), CH)

    def all_rows(ref, k):
        return ref[:, rows_of(k), :].reshape(4 * CH, ref.shape[2])

    @pl.loop(0, chunks)
    def _(k):
        rs_start(0, k, lambda q: mm(mixed_ref[q, rows_of(k), :], wo_ref[...], NT))

    @pl.loop(0, chunks)
    def _(k):
        resid = rs_end(0, k) + tok_ref[rows_of(k), :].astype(f32) + bo
        hat, inv = norm_rows(resid)
        hat1[k] = hat
        inv1[k] = inv
        val = hat * g1 + s1
        normed[k] = val
        ag_start(0, k, val.astype(bf16))

    @pl.loop(0, chunks)
    def _(k):
        ag_end(0, k)
        pre = mm(all_rows(nfull, k), win_ref[...], NN) + bin_ref[...]
        cum = 0.5 * (1.0 + lax.erf(pre * root_half))
        dens = jnp.exp(-0.5 * pre * pre) * inv_root_two_pi
        hidden[:, rows_of(k), :] = (pre * cum).astype(bf16).reshape(4, CH, D)
        slope[:, rows_of(k), :] = (cum + pre * dens).reshape(4, CH, D)
        rs_start(1, k, lambda q: mm(hidden[q, rows_of(k), :], wout_ref[...], NT))

    dvec_ref[...] = jnp.zeros_like(dvec_ref)

    @pl.loop(0, chunks)
    def _(k):
        resid = rs_end(1, k) + normed[k] + b2
        hat, inv = norm_rows(resid)
        out_ref[rows_of(k), :] = (hat * g2 + s2).astype(out_ref.dtype)
        cot = cot_ref[rows_of(k), :].astype(f32)
        grad = norm_back(cot, g2, hat, inv)
        grad2[k] = grad
        ag_start(1, k, grad.astype(bf16))
        dvec_ref[pl.ds(2, 1), :] += jnp.sum(grad, axis=0, keepdims=True)
        dvec_ref[pl.ds(5, 1), :] += jnp.sum(cot * hat, axis=0, keepdims=True)
        dvec_ref[pl.ds(6, 1), :] += jnp.sum(cot, axis=0, keepdims=True)

    dwin_ref[...] = jnp.zeros_like(dwin_ref)
    dwout_ref[...] = jnp.zeros_like(dwout_ref)
    dwo_ref[...] = jnp.zeros_like(dwo_ref)
    dbin_ref[...] = jnp.zeros_like(dbin_ref)

    @pl.loop(0, chunks)
    def _(k):
        ag_end(1, k)
        g2c = all_rows(g2full, k)
        grad_pre = mm(g2c, wout_ref[...], NN) * all_rows(slope, k)
        dbin_ref[...] += jnp.sum(grad_pre, axis=0, keepdims=True)
        low = grad_pre.astype(bf16)
        hid = all_rows(hidden, k)
        hidden[:, rows_of(k), :] = low.reshape(4, CH, D)
        rs_start(2, k, lambda q: mm(hidden[q, rows_of(k), :], win_ref[...], NT))
        dwout_ref[...] += mm(g2c, hid, TN)
        dwin_ref[...] += mm(all_rows(nfull, k), low, TN)

    @pl.loop(0, chunks)
    def _(k):
        grad_normed = rs_end(2, k) + grad2[k]
        hat = hat1[k]
        grad = norm_back(grad_normed, g1, hat, inv1[k])
        ag_start(2, k, grad.astype(bf16))
        dvec_ref[pl.ds(1, 1), :] += jnp.sum(grad, axis=0, keepdims=True)
        dvec_ref[pl.ds(3, 1), :] += jnp.sum(grad_normed * hat, axis=0, keepdims=True)
        dvec_ref[pl.ds(4, 1), :] += jnp.sum(grad_normed, axis=0, keepdims=True)

    @pl.loop(0, chunks)
    def _(k):
        ag_end(2, k)
        g1c = all_rows(g1_ref, k)
        gmix_ref[:, rows_of(k), :] = mm(g1c, wo_ref[...], NN).astype(bf16).reshape(4, CH, FEAT)
        dwo_ref[...] += mm(g1c, all_rows(mixed_ref, k), TN)

    @pl.loop(0, chunks)
    def _(k):
        for st in range(3):
            d2d(st, k).wait_send()
            xcopy(st, k).wait_send()
            to_sib(st, k, c).wait_send()
            to_nbr(st, k, c).wait_send()
            fwd(st, k, nbr).wait_send()


def middle(mixed, tok, cot, wo, win, wout, vec, b_in):
    own_rows = tok.shape[0]
    chunks = own_rows // CH
    sem = pltpu.SemaphoreType.DMA((3, chunks))
    S = jax.ShapeDtypeStruct
    return pl.pallas_call(
        middle_body,
        out_shape=(
            S((own_rows, D), bf16),
            S((4, own_rows, D), bf16),
            S((4, own_rows, FEAT), bf16),
            S((D, FEAT), f32),
            S((D, D), f32),
            S((D, D), f32),
            S((8, D), f32),
            S((1, D), f32),
        ),
        in_specs=[VM] * 8,
        out_specs=(VM,) * 8,
        scratch_shapes=[
            pltpu.VMEM((4, own_rows, D), bf16),
            pltpu.VMEM((4, own_rows, D), bf16),
            pltpu.VMEM((4, own_rows, D), f32),
            pltpu.VMEM((4, own_rows, D), bf16),
            pltpu.VMEM((3, chunks, CH, D), f32),
            pltpu.VMEM((3, chunks, 2, CH, D), bf16),
            pltpu.VMEM((3, chunks, 2, CH, D), bf16),
            pltpu.VMEM((3, chunks, CH, D), bf16),
            pltpu.VMEM((3, chunks, CH, D), bf16),
            pltpu.VMEM((chunks, CH, D), f32),
            pltpu.VMEM((chunks, CH, D), f32),
            pltpu.VMEM((chunks, CH, 1), f32),
            pltpu.VMEM((chunks, CH, D), f32),
        ]
        + [sem] * 10,
        name="middle",
        compiler_params=pltpu.CompilerParams(collective_id=2, has_side_effects=True, vmem_limit_bytes=60 << 20),
        cost_estimate=pl.CostEstimate(flops=80_000_000_000, bytes_accessed=20_000_000, transcendentals=4_000_000),
    )(mixed, tok, cot, wo, win, wout, vec, b_in)


def sent_and_summed(value, dim):
    size = lax.axis_size("row")
    before, after = value.shape[:dim], value.shape[dim + 1 :]
    pieces = jnp.moveaxis(value.reshape(*before, size, -1, *after), dim, 0)
    return jnp.sum(lax.all_to_all(pieces, "row", 0, 0, tiled=True).astype(f32), axis=0)


def per_device(
    inputs, cotangent, token_order, token_place, seq_lengths,
    query_weight, key_weight, value_weight, output_weight, inner_weight, outer_weight,
    query_bias, value_bias, output_bias, inner_bias, outer_bias,
    first_gain, first_shift, second_gain, second_shift,
):
    rows = lax.axis_size("row")
    col = lax.axis_index("col")
    given = lax.all_to_all(inputs.astype(bf16), "col", split_axis=1, concat_axis=0, tiled=True)
    given_g = lax.all_to_all(cotangent.astype(bf16), "col", split_axis=1, concat_axis=0, tiled=True)
    tok_rows = given.shape[0]
    send_order = jnp.argsort(token_place // tok_rows, stable=True)
    arrive_order = jnp.argsort(token_order, stable=True)
    got = lax.all_to_all(given[send_order], "row", split_axis=0, concat_axis=0, tiled=True)
    got_g = lax.all_to_all(given_g[send_order], "row", split_axis=0, concat_axis=0, tiled=True)
    dealt = jnp.zeros_like(got).at[arrive_order].set(got)
    dealt_g = jnp.zeros_like(got_g).at[arrive_order].set(got_g)
    own_rows = tok_rows // 4

    pack = jnp.concatenate(
        [query_weight, key_weight, value_weight, output_weight.T, inner_weight, outer_weight.T], axis=1
    )
    pack = lax.all_gather(pack, "row", axis=0, tiled=True)
    w_qkv, wo, win, wout = pack[:, :576], pack[:, 576:768], pack[:, 768:1536], pack[:, 1536:]
    vecs = jnp.concatenate(
        [query_bias, value_bias, output_bias, first_gain, first_shift, outer_bias, second_gain, second_shift, inner_bias]
    )[None]
    vecs = lax.all_gather(vecs, "row", axis=0, tiled=True)
    small = query_bias.shape[0]
    mine = vecs[:, : 8 * small].reshape(rows, 8, small).transpose(1, 0, 2).reshape(8, FEAT)
    b_in = vecs[:, 8 * small :].reshape(1, D).astype(f32)
    full = lax.all_gather(mine[2:], "col", axis=1, tiled=True).astype(f32)
    vec = jnp.concatenate([full, jnp.zeros((2, D), f32)], axis=0)

    seq_ends = jnp.cumsum(seq_lengths[0])
    seq_starts = seq_ends - seq_lengths[0]
    positions = jnp.arange(tok_rows, dtype=jnp.int32)
    seg = jnp.sum((positions[:, None] >= seq_ends[None, :]).astype(jnp.int32), axis=1)
    hot = (seg[:, None] == jnp.arange(seq_ends.shape[0])[None, :]).astype(jnp.int32)
    start = jnp.sum(hot * seq_starts[None], axis=1)
    end = jnp.sum(hot * seq_ends[None], axis=1)
    lo = start[::QB] // KB
    hi = (end[QB - 1 :: QB] + KB - 1) // KB
    start, end = start[None], end[None]

    tokens = lax.all_gather(dealt, "col", axis=1, tiled=True)
    cot = lax.all_to_all(dealt_g, "col", split_axis=0, concat_axis=1, tiled=True)
    qkv = jnp.dot(tokens, w_qkv, preferred_element_type=f32)
    q = (qkv[:, :192] + mine[0].astype(f32)).astype(bf16)
    k = qkv[:, 192:384].astype(bf16)
    v = (qkv[:, 384:] + mine[1].astype(f32)).astype(bf16)
    mixed, lse = attend_fwd(lo, hi, start, end, q, k, v)
    own_tok = lax.dynamic_slice_in_dim(tokens, col * own_rows, own_rows, axis=0)
    out, g1, gmix, dwo, dwin, dwout, dvec, dbin = middle(
        mixed.reshape(4, own_rows, FEAT), own_tok, cot, wo, win, wout, vec, b_in
    )
    dq, dk, dv = attend_bwd(lo, hi, start, end, q, k, v, gmix.reshape(tok_rows, FEAT), lse)
    dqkv = jnp.concatenate([dq, dk, dv], axis=1)
    dw_qkv = lax.dot_general(tokens, dqkv, TN, preferred_element_type=f32)
    db_q = jnp.sum(dq.astype(f32), axis=0)
    db_v = jnp.sum(dv.astype(f32), axis=0)
    back = lax.dot_general(dqkv, w_qkv, NT, preferred_element_type=f32).astype(bf16)
    grad_tok = lax.psum_scatter(back, "col", scatter_dimension=1, tiled=True).astype(f32)
    g1_cols = lax.dynamic_slice_in_dim(g1.reshape(tok_rows, D), col * FEAT, FEAT, axis=1)
    grad_tok = (grad_tok + g1_cols.astype(f32)).astype(bf16)

    dpack = jnp.concatenate([dw_qkv.astype(bf16), dwo.astype(bf16), dwin.astype(bf16), dwout.astype(bf16)], axis=1)
    dpack = sent_and_summed(dpack, 0)
    dmine = lax.psum_scatter(dvec[1:7], "col", scatter_dimension=1, tiled=True)
    dmine = jnp.concatenate([db_q[None], db_v[None], dmine], axis=0)
    dmine = dmine.reshape(8, rows, small).transpose(1, 0, 2).reshape(rows, 8 * small)
    dall = jnp.concatenate([dmine, dbin.reshape(rows, -1)], axis=1)
    dsum = jnp.sum(lax.all_to_all(dall, "row", 0, 0, tiled=True), axis=0)
    dv8 = dsum[: 8 * small].reshape(8, small)

    share = lax.all_to_all(out, "col", split_axis=1, concat_axis=0, tiled=True)

    def send_back(value):
        got_back = lax.all_to_all(value[arrive_order], "row", split_axis=0, concat_axis=0, tiled=True)
        placed = jnp.zeros_like(got_back).at[send_order].set(got_back)
        return lax.all_to_all(placed, "col", split_axis=0, concat_axis=1, tiled=True).astype(f32)

    output, input_grad = send_back(share), send_back(grad_tok)
    return (
        output, input_grad,
        dpack[:, :192], dpack[:, 192:384], dpack[:, 384:576], dpack[:, 576:768].T,
        dpack[:, 768:1536], dpack[:, 1536:].T,
        dv8[0], dv8[1], dv8[2], dsum[8 * small :], dv8[3], dv8[4], dv8[5], dv8[6], dv8[7],
    )


def solution(mesh):
    tok = P(("row", "col"), None)
    rc, cr, vec = P("row", "col"), P("col", "row"), P(("col", "row"))
    in_specs = (tok, tok, P("row"), P("row"), P("row", None), rc, rc, rc, cr, rc, cr) + (vec,) * 9
    out_specs = (tok, tok, rc, rc, rc, cr, rc, cr) + (vec,) * 9
    return jax.shard_map(per_device, mesh=mesh, in_specs=in_specs, out_specs=out_specs, check_vma=False)
```

```python
import functools

import jax
import jax.numpy as jnp
from jax import lax
from jax.experimental import pallas as pl
from jax.experimental.pallas import tpu as pltpu
from jax.sharding import PartitionSpec as P

D = 768
HD = 64
FEAT = 192
HEADS = 3
QB = 256
KB = 256

norm_eps = 1e-12
root_half = 0.7071067811865476
inv_root_two_pi = 0.3989422804014327
NN = (((1,), (0,)), ((), ()))
NT = (((1,), (1,)), ((), ()))
TN = (((0,), (0,)), ((), ()))
MESH = pl.DeviceIdType.MESH
f32 = jnp.float32
bf16 = jnp.bfloat16
VM = pl.BlockSpec(memory_space=pltpu.VMEM)
SM = pl.BlockSpec(memory_space=pltpu.SMEM)


def mm(a, b, dims):
    return lax.dot_general(a, b, dims, preferred_element_type=f32)


def lane_head(rows):
    return lax.broadcasted_iota(jnp.int32, (rows, FEAT), 1) // HD


def attend_fwd_body(
    lo_ref, hi_ref, start_ref, end_ref, tok_ref, w_ref, b_ref, q_ref, k_ref, v_ref, mix_ref, lse_ref, s_buf,
):
    scale = HD ** (-0.5)
    blocks = q_ref.shape[0] // QB
    heads = lane_head(QB)
    b_q, b_v = b_ref[0:1, :], b_ref[1:2, :]

    @pl.loop(0, blocks)
    def _(qb):
        rows = pl.ds(qb * QB, QB)
        out = mm(tok_ref[rows, :], w_ref[...], NN)
        q_ref[rows, :] = (out[:, :FEAT] + b_q).astype(bf16)
        k_ref[rows, :] = out[:, FEAT : 2 * FEAT].astype(bf16)
        v_ref[rows, :] = (out[:, 2 * FEAT :] + b_v).astype(bf16)

    @pl.loop(0, blocks)
    def _(qb):
        rows = pl.ds(qb * QB, QB)
        qv = q_ref[rows, :]
        qs = [jnp.where(heads == h, qv, jnp.zeros_like(qv)) for h in range(HEADS)]
        q_start = start_ref[:, rows]
        q_end = end_ref[:, rows]
        lo, hi = lo_ref[qb], hi_ref[qb]

        def scores(kb, tops):
            keys = pl.ds(pl.multiple_of(kb * KB, KB), KB)
            kv = k_ref[keys, :]
            pos = lax.broadcasted_iota(jnp.int32, (KB, QB), 0) + kb * KB
            allowed = (pos >= q_start) & (pos < q_end)
            out = []
            for h in range(HEADS):
                s = jnp.where(allowed, mm(kv, qs[h], NT) * scale, -1e30)
                s_buf[h, keys, :] = s
                out.append(jnp.maximum(tops[h], jnp.max(s, axis=0, keepdims=True)))
            return tuple(out)

        tops = lax.fori_loop(lo, hi, scores, tuple(jnp.full((1, QB), -1e30, f32) for _ in range(HEADS)))

        def weigh(kb, sums):
            keys = pl.ds(pl.multiple_of(kb * KB, KB), KB)
            out = []
            for h in range(HEADS):
                e = jnp.exp(s_buf[h, keys, :] - tops[h])
                s_buf[h, keys, :] = e
                out.append(sums[h] + jnp.sum(e, axis=0, keepdims=True))
            return tuple(out)

        sums = lax.fori_loop(lo, hi, weigh, tuple(jnp.zeros((1, QB), f32) for _ in range(HEADS)))
        inv = [1.0 / s for s in sums]

        def mix(kb, acc):
            keys = pl.ds(pl.multiple_of(kb * KB, KB), KB)
            vv = v_ref[keys, :]
            for h in range(HEADS):
                p = (s_buf[h, keys, :] * inv[h]).astype(bf16)
                acc = acc + jnp.where(heads == h, mm(p, vv, TN), 0.0)
            return acc

        acc = lax.fori_loop(lo, hi, mix, jnp.zeros((QB, FEAT), f32))
        mix_ref[rows, :] = acc.astype(bf16)
        for h in range(HEADS):
            lse_ref[pl.ds(h, 1), rows] = tops[h] + jnp.log(sums[h])


def attend_fwd(lo, hi, start, end, tokens, w_qkv, bias):
    rows = tokens.shape[0]
    part = jax.ShapeDtypeStruct((rows, FEAT), bf16)
    return pl.pallas_call(
        attend_fwd_body,
        out_shape=(part, part, part, part, jax.ShapeDtypeStruct((8, rows), f32)),
        in_specs=[SM, SM] + [VM] * 5,
        out_specs=(VM,) * 5,
        scratch_shapes=[pltpu.VMEM((HEADS, rows, QB), f32)],
        name="attend_fwd",
        compiler_params=pltpu.CompilerParams(vmem_limit_bytes=40 << 20),
        cost_estimate=pl.CostEstimate(flops=8_000_000_000, bytes_accessed=8_000_000, transcendentals=4_000_000),
    )(lo, hi, start, end, tokens, w_qkv, bias)


def attend_bwd_body(
    lo_ref, hi_ref, start_ref, end_ref, q_ref, k_ref, v_ref, do_ref, lse_ref,
    dqkv_ref, p_buf, dp_buf, dq_acc, dk_acc, dv_acc,
):
    scale = HD ** (-0.5)
    blocks = q_ref.shape[0] // QB
    heads = lane_head(QB)
    key_heads = lane_head(KB)
    dk_acc[...] = jnp.zeros_like(dk_acc)
    dv_acc[...] = jnp.zeros_like(dv_acc)

    @pl.loop(0, blocks)
    def _(qb):
        rows = pl.ds(qb * QB, QB)
        qv = q_ref[rows, :]
        dv_in = do_ref[rows, :]
        qs = [jnp.where(heads == h, qv, jnp.zeros_like(qv)) for h in range(HEADS)]
        dos = [jnp.where(heads == h, dv_in, jnp.zeros_like(dv_in)) for h in range(HEADS)]
        q_start = start_ref[:, rows]
        q_end = end_ref[:, rows]
        lse = [lse_ref[pl.ds(h, 1), rows] for h in range(HEADS)]
        lo, hi = lo_ref[qb], hi_ref[qb]

        def first(kb, sums):
            keys = pl.ds(pl.multiple_of(kb * KB, KB), KB)
            kv, vv = k_ref[keys, :], v_ref[keys, :]
            pos = lax.broadcasted_iota(jnp.int32, (KB, QB), 0) + kb * KB
            allowed = (pos >= q_start) & (pos < q_end)
            out = []
            grad_v = dv_acc[keys, :]
            for h in range(HEADS):
                p = jnp.where(allowed, jnp.exp(mm(kv, qs[h], NT) * scale - lse[h]), 0.0)
                dp = mm(vv, dos[h], NT)
                p_buf[h, keys, :] = p
                dp_buf[h, keys, :] = dp
                out.append(sums[h] + jnp.sum(p * dp, axis=0, keepdims=True))
                grad_v = grad_v + mm(p.astype(bf16), dos[h], NN)
            dv_acc[keys, :] = grad_v
            return tuple(out)

        sums = lax.fori_loop(lo, hi, first, tuple(jnp.zeros((1, QB), f32) for _ in range(HEADS)))

        def second(kb, acc):
            keys = pl.ds(pl.multiple_of(kb * KB, KB), KB)
            kv = k_ref[keys, :]
            grad_k = dk_acc[keys, :]
            for h in range(HEADS):
                ds = (p_buf[h, keys, :] * (dp_buf[h, keys, :] - sums[h])).astype(bf16)
                grad_k = grad_k + mm(ds, qs[h], NN)
                acc = acc + jnp.where(heads == h, mm(ds, kv, TN), 0.0)
            dk_acc[keys, :] = grad_k
            return acc

        acc = lax.fori_loop(lo, hi, second, jnp.zeros((QB, FEAT), f32))
        dq_acc[rows, :] = acc

    @pl.loop(0, blocks)
    def _(qb):
        rows = pl.ds(qb * QB, QB)
        parts = [dq_acc[rows, :] * scale, dk_acc[rows, :] * scale, dv_acc[rows, :]]
        dqkv_ref[rows, :] = jnp.concatenate([p.astype(bf16) for p in parts], axis=1)


def attend_bwd(lo, hi, start, end, q, k, v, do, lse):
    rows = q.shape[0]
    return pl.pallas_call(
        attend_bwd_body,
        out_shape=jax.ShapeDtypeStruct((rows, 3 * FEAT), bf16),
        in_specs=[SM, SM] + [VM] * 7,
        out_specs=VM,
        scratch_shapes=[
            pltpu.VMEM((HEADS, rows, QB), f32),
            pltpu.VMEM((HEADS, rows, QB), f32),
            pltpu.VMEM((rows, FEAT), f32),
            pltpu.VMEM((rows, FEAT), f32),
            pltpu.VMEM((rows, FEAT), f32),
        ],
        name="attend_bwd",
        compiler_params=pltpu.CompilerParams(vmem_limit_bytes=48 << 20),
        cost_estimate=pl.CostEstimate(flops=20_000_000_000, bytes_accessed=6_000_000, transcendentals=4_000_000),
    )(lo, hi, start, end, q, k, v, do, lse)


def remote(src, dst, send_sem, recv_sem, device):
    return pltpu.make_async_remote_copy(
        src_ref=src, dst_ref=dst, send_sem=send_sem, recv_sem=recv_sem,
        device_id=device, device_id_type=MESH,
    )


def col_peers():
    r, c = lax.axis_index("row"), lax.axis_index("col")
    sib, nbr, diag = c + 1 - 2 * (c % 2), (c + 2) % 4, 3 - c
    return r, c, sib, nbr, diag


def norm_rows(x):
    mean = jnp.mean(x, axis=1, keepdims=True)
    center = x - mean
    var = jnp.mean(center * center, axis=1, keepdims=True)
    inv = lax.rsqrt(var + norm_eps)
    return center * inv, inv


def norm_back(grad, gain, hat, inv):
    e = grad * gain
    mean_e = jnp.mean(e, axis=1, keepdims=True)
    mean_c = jnp.mean(e * hat, axis=1, keepdims=True)
    return inv * (e - mean_e - hat * mean_c)


CH = 128


def middle_body(
    mixed_ref, tok_ref, cot_ref, wo_ref, win_ref, wout_ref, vec_ref, bin_ref,
    out_ref, g1_ref, gmix_ref, dwo_ref, dwin_ref, dwout_ref, dvec_ref, dbin_ref,
    nfull, hidden, slope, g2full, own, d2ds, d2dr, xs, xr, normed, hat1, inv1, grad2,
    ds_s, ds_r, x_s, x_r, asib_s, asib_r, anbr_s, anbr_r, afwd_s, afwd_r,
):
    r, c, sib, nbr, diag = col_peers()
    chunks = tok_ref.shape[0] // CH

    barrier = pltpu.get_barrier_semaphore()
    for peer in (sib, nbr):
        pl.semaphore_signal(barrier, inc=1, device_id=(r, peer), device_id_type=MESH)
    pl.semaphore_wait(barrier, 2)

    bo, g1, s1, b2, g2, s2 = [vec_ref[pl.ds(i, 1), :] for i in range(6)]

    def d2d(st, k):
        return remote(d2ds.at[st, k], d2dr.at[st, k], ds_s.at[st, k], ds_r.at[st, k], (r, sib))

    def xcopy(st, k):
        return remote(xs.at[st, k], xr.at[st, k], x_s.at[st, k], x_r.at[st, k], (r, nbr))

    def rs_start(st, k, part):
        d2ds[st, k, 0] = part(sib).astype(bf16)
        d2ds[st, k, 1] = part(diag).astype(bf16)
        d2d(st, k).start()
        mine = part(c)
        other = part(nbr)
        d2d(st, k).wait_recv()
        xs[st, k] = (other + d2dr[st, k, 1].astype(f32)).astype(bf16)
        xcopy(st, k).start()
        own[st, k] = mine + d2dr[st, k, 0].astype(f32)

    def rs_end(st, k):
        xcopy(st, k).wait_recv()
        return own[st, k] + xr[st, k].astype(f32)

    gathered = (nfull, g2full, g1_ref)

    def piece(st, q, k):
        return gathered[st].at[q, pl.ds(pl.multiple_of(k * CH, CH), CH), :]

    def ag_copy(st, k, q, sems, target):
        return remote(piece(st, q, k), piece(st, q, k), sems[0].at[st, k], sems[1].at[st, k], (r, target))

    to_sib = functools.partial(ag_copy, sems=(asib_s, asib_r), target=sib)
    to_nbr = functools.partial(ag_copy, sems=(anbr_s, anbr_r), target=nbr)
    fwd = functools.partial(ag_copy, sems=(afwd_s, afwd_r), target=sib)

    def ag_start(st, k, value):
        gathered[st][c, pl.ds(pl.multiple_of(k * CH, CH), CH), :] = value
        to_nbr(st, k, c).start()
        to_sib(st, k, c).start()

    def ag_end(st, k):
        to_nbr(st, k, c).wait_recv()
        fwd(st, k, nbr).start()
        to_sib(st, k, c).wait_recv()
        fwd(st, k, nbr).wait_recv()

    def rows_of(k):
        return pl.ds(pl.multiple_of(k * CH, CH), CH)

    def all_rows(ref, k):
        return ref[:, rows_of(k), :].reshape(4 * CH, ref.shape[2])

    @pl.loop(0, chunks)
    def _(k):
        rs_start(0, k, lambda q: mm(mixed_ref[q, rows_of(k), :], wo_ref[...], NT))

    @pl.loop(0, chunks)
    def _(k):
        resid = rs_end(0, k) + tok_ref[rows_of(k), :].astype(f32) + bo
        hat, inv = norm_rows(resid)
        hat1[k] = hat
        inv1[k] = inv
        val = hat * g1 + s1
        normed[k] = val
        ag_start(0, k, val.astype(bf16))

    @pl.loop(0, chunks)
    def _(k):
        ag_end(0, k)
        pre = mm(all_rows(nfull, k), win_ref[...], NN) + bin_ref[...]
        cum = 0.5 * (1.0 + lax.erf(pre * root_half))
        dens = jnp.exp(-0.5 * pre * pre) * inv_root_two_pi
        hidden[:, rows_of(k), :] = (pre * cum).astype(bf16).reshape(4, CH, D)
        slope[:, rows_of(k), :] = (cum + pre * dens).reshape(4, CH, D)
        rs_start(1, k, lambda q: mm(hidden[q, rows_of(k), :], wout_ref[...], NT))

    dvec_ref[...] = jnp.zeros_like(dvec_ref)

    @pl.loop(0, chunks)
    def _(k):
        resid = rs_end(1, k) + normed[k] + b2
        hat, inv = norm_rows(resid)
        out_ref[rows_of(k), :] = (hat * g2 + s2).astype(out_ref.dtype)
        cot = cot_ref[rows_of(k), :].astype(f32)
        grad = norm_back(cot, g2, hat, inv)
        grad2[k] = grad
        ag_start(1, k, grad.astype(bf16))
        dvec_ref[pl.ds(2, 1), :] += jnp.sum(grad, axis=0, keepdims=True)
        dvec_ref[pl.ds(5, 1), :] += jnp.sum(cot * hat, axis=0, keepdims=True)
        dvec_ref[pl.ds(6, 1), :] += jnp.sum(cot, axis=0, keepdims=True)

    dwin_ref[...] = jnp.zeros_like(dwin_ref)
    dwout_ref[...] = jnp.zeros_like(dwout_ref)
    dwo_ref[...] = jnp.zeros_like(dwo_ref)
    dbin_ref[...] = jnp.zeros_like(dbin_ref)

    @pl.loop(0, chunks)
    def _(k):
        ag_end(1, k)
        g2c = all_rows(g2full, k)
        grad_pre = mm(g2c, wout_ref[...], NN) * all_rows(slope, k)
        dbin_ref[...] += jnp.sum(grad_pre, axis=0, keepdims=True)
        low = grad_pre.astype(bf16)
        hid = all_rows(hidden, k)
        hidden[:, rows_of(k), :] = low.reshape(4, CH, D)
        rs_start(2, k, lambda q: mm(hidden[q, rows_of(k), :], win_ref[...], NT))
        dwout_ref[...] += mm(g2c, hid, TN)
        dwin_ref[...] += mm(all_rows(nfull, k), low, TN)

    @pl.loop(0, chunks)
    def _(k):
        grad_normed = rs_end(2, k) + grad2[k]
        hat = hat1[k]
        grad = norm_back(grad_normed, g1, hat, inv1[k])
        ag_start(2, k, grad.astype(bf16))
        dvec_ref[pl.ds(1, 1), :] += jnp.sum(grad, axis=0, keepdims=True)
        dvec_ref[pl.ds(3, 1), :] += jnp.sum(grad_normed * hat, axis=0, keepdims=True)
        dvec_ref[pl.ds(4, 1), :] += jnp.sum(grad_normed, axis=0, keepdims=True)

    @pl.loop(0, chunks)
    def _(k):
        ag_end(2, k)
        g1c = all_rows(g1_ref, k)
        gmix_ref[:, rows_of(k), :] = mm(g1c, wo_ref[...], NN).astype(bf16).reshape(4, CH, FEAT)
        dwo_ref[...] += mm(g1c, all_rows(mixed_ref, k), TN)

    @pl.loop(0, chunks)
    def _(k):
        for st in range(3):
            d2d(st, k).wait_send()
            xcopy(st, k).wait_send()
            to_sib(st, k, c).wait_send()
            to_nbr(st, k, c).wait_send()
            fwd(st, k, nbr).wait_send()


def middle(mixed, tok, cot, wo, win, wout, vec, b_in):
    own_rows = tok.shape[0]
    chunks = own_rows // CH
    sem = pltpu.SemaphoreType.DMA((3, chunks))
    S = jax.ShapeDtypeStruct
    return pl.pallas_call(
        middle_body,
        out_shape=(
            S((own_rows, D), bf16),
            S((4, own_rows, D), bf16),
            S((4, own_rows, FEAT), bf16),
            S((D, FEAT), f32),
            S((D, D), f32),
            S((D, D), f32),
            S((8, D), f32),
            S((1, D), f32),
        ),
        in_specs=[VM] * 8,
        out_specs=(VM,) * 8,
        scratch_shapes=[
            pltpu.VMEM((4, own_rows, D), bf16),
            pltpu.VMEM((4, own_rows, D), bf16),
            pltpu.VMEM((4, own_rows, D), f32),
            pltpu.VMEM((4, own_rows, D), bf16),
            pltpu.VMEM((3, chunks, CH, D), f32),
            pltpu.VMEM((3, chunks, 2, CH, D), bf16),
            pltpu.VMEM((3, chunks, 2, CH, D), bf16),
            pltpu.VMEM((3, chunks, CH, D), bf16),
            pltpu.VMEM((3, chunks, CH, D), bf16),
            pltpu.VMEM((chunks, CH, D), f32),
            pltpu.VMEM((chunks, CH, D), f32),
            pltpu.VMEM((chunks, CH, 1), f32),
            pltpu.VMEM((chunks, CH, D), f32),
        ]
        + [sem] * 10,
        name="middle",
        compiler_params=pltpu.CompilerParams(collective_id=2, has_side_effects=True, vmem_limit_bytes=60 << 20),
        cost_estimate=pl.CostEstimate(flops=80_000_000_000, bytes_accessed=20_000_000, transcendentals=4_000_000),
    )(mixed, tok, cot, wo, win, wout, vec, b_in)


HALF = 384


def half_lanes(h):
    return pl.ds(pl.multiple_of(h * HALF, HALF), HALF)


def greet(peers, rows, row, c):
    barrier = pltpu.get_barrier_semaphore()
    for peer in peers:
        pl.semaphore_signal(barrier, inc=1, device_id=(row, peer), device_id_type=MESH)

    @pl.loop(1, rows)
    def _(i):
        pl.semaphore_signal(barrier, inc=1, device_id=((row + i) % rows, c), device_id_type=MESH)

    pl.semaphore_wait(barrier, len(peers) + rows - 1)


def to_col(src, dst):
    eye = lax.broadcasted_iota(jnp.int32, (128, 128), 0) == lax.broadcasted_iota(jnp.int32, (128, 128), 1)

    @pl.loop(0, dst.shape[0] // 128)
    def _(t):
        at = pl.ds(pl.multiple_of(t * 128, 128), 128)
        dst[at, :] = jnp.sum(jnp.where(eye, src[:, at], 0.0), axis=1, keepdims=True)


def rank_row(row_ref, col_ref):
    keys = row_ref[...]
    size = keys.shape[1]

    def step(t, acc):
        col = col_ref[pl.ds(pl.multiple_of(t * 128, 128), 128), :]
        less = jnp.where(col < keys, 1.0, 0.0)
        return acc + jnp.sum(less.reshape(16, 8, size), axis=0)

    acc = lax.fori_loop(0, size // 128, step, jnp.zeros((8, size), f32))
    return jnp.sum(acc, axis=0, keepdims=True)


def picker_rows(rank, first, count):
    want = (lax.broadcasted_iota(jnp.int32, (count, rank.shape[1]), 0) + first).astype(f32)
    return jnp.where(rank == want, 1.0, 0.0).astype(bf16)


def picker_cols(rank, count):
    have = lax.broadcasted_iota(jnp.int32, (rank.shape[0], count), 1).astype(f32)
    return jnp.where(rank == have, 1.0, 0.0).astype(bf16)


class Deal:
    def __init__(self, a, rows, bufs, sems):
        self.a, self.rows = a, rows
        self.xin, self.xout, self.sbuf, self.rbuf = bufs
        self.sib_s, self.sib_r, self.nbr_s, self.nbr_r, self.fwd_s, self.fwd_r, self.row_s, self.row_r, self.sh_s, self.sh_r = sems
        self.r, self.c, self.sib, self.nbr, self.diag = col_peers()
        self.h, self.core = self.c // 2, self.c % 2
        self.tokens = self.xin.shape[2] * 4
        self.slots = self.tokens // rows
        self.own_slots = self.slots // 2

    def to_sib(self):
        v = self.xin.at[self.a, self.c]
        return remote(v, v, self.sib_s.at[self.a], self.sib_r.at[self.a], (self.r, self.sib))

    def to_nbr(self):
        return remote(self.xout.at[self.a], self.xin.at[self.a, self.c], self.nbr_s.at[self.a], self.nbr_r.at[self.a], (self.r, self.nbr))

    def fwd(self):
        v = self.xin.at[self.a, self.nbr]
        return remote(v, v, self.fwd_s.at[self.a], self.fwd_r.at[self.a], (self.r, self.sib))

    def split(self, ref):
        self.xout[self.a] = ref[:, half_lanes(1 - self.h)].astype(bf16)
        self.to_nbr().start()
        self.xin[self.a, self.c] = ref[:, half_lanes(self.h)].astype(bf16)
        self.to_sib().start()

    def joined(self):
        self.to_nbr().wait_recv()
        self.fwd().start()
        self.to_sib().wait_recv()
        self.fwd().wait_recv()

    def row_copy(self, i):
        to = (self.r + i) % self.rows
        return remote(
            self.sbuf.at[self.a, i], self.rbuf.at[self.a, self.r, self.core],
            self.row_s.at[self.a, i], self.row_r.at[self.a, i], (to, self.c),
        )

    def share(self, i):
        v = self.rbuf.at[self.a, (self.r + self.rows - i) % self.rows, self.core]
        return remote(v, v, self.sh_s.at[self.a, i], self.sh_r.at[self.a, i], (self.r, self.sib))

    def pick_and_send(self, rank):
        source = self.xin[self.a].reshape(self.tokens, HALF)

        def picked(to):
            return mm(picker_rows(rank, to * self.slots + self.core * self.own_slots, self.own_slots), source, NN).astype(bf16)

        @pl.loop(1, self.rows)
        def _(i):
            self.sbuf[self.a, i] = picked((self.r + i) % self.rows)
            self.row_copy(i).start()

        self.rbuf[self.a, self.r, self.core] = picked(self.r)
        self.share(0).start()

    def shared(self):
        @pl.loop(1, self.rows)
        def _(i):
            self.row_copy(i).wait_recv()
            self.share(i).start()

        @pl.loop(0, self.rows)
        def _(i):
            self.share(i).wait_recv()

    def placed(self, rank_col):
        return mm(picker_cols(rank_col, self.tokens), self.rbuf[self.a].reshape(self.tokens, HALF), NN)

    def finish(self, joins=True):
        if joins:
            self.to_sib().wait_send()
            self.to_nbr().wait_send()
        self.fwd().wait_send()

        @pl.loop(1, self.rows)
        def _(i):
            self.row_copy(i).wait_send()

        @pl.loop(0, self.rows)
        def _(i):
            self.share(i).wait_send()


def deal_scratch(rows, own_rows):
    slots = 4 * own_rows // rows
    return [
        pltpu.VMEM((2, 4, own_rows, HALF), bf16),
        pltpu.VMEM((2, own_rows, HALF), bf16),
        pltpu.VMEM((2, rows, slots // 2, HALF), bf16),
        pltpu.VMEM((2, rows, 2, slots // 2, HALF), bf16),
    ]


def deal_sems(rows):
    return [pltpu.SemaphoreType.DMA((2,))] * 6 + [pltpu.SemaphoreType.DMA((2, rows))] * 4


def arrive_body(
    rows, x_ref, g_ref, place_ref, order_ref, vin_ref,
    tok_ref, cot_ref, rank_ref, vec_ref, bqv_ref, bin_ref,
    *scratch,
):
    bufs, sems = scratch[:4], scratch[4:14]
    key_g, key_w, col_g, col_w, cot_send, vbuf = scratch[14:20]
    an_s, an_r, as_s, as_r, af_s, af_r, ct_s, ct_r, vr_s, vr_r, vc_s, vc_r = scratch[20:]
    r, c, sib, nbr, diag = col_peers()
    h = c // 2
    own_rows = x_ref.shape[0]
    tokens = 4 * own_rows
    chunks = own_rows // CH
    greet((sib, nbr, diag), rows, r, c)

    first, second = Deal(0, rows, bufs, sems), Deal(1, rows, bufs, sems)
    first.split(x_ref)
    second.split(g_ref)

    def vec_row(i):
        v = vbuf.at[c, r]
        return remote(v, v, vr_s.at[i], vr_r.at[i], ((r + i) % rows, c))

    def vec_col(i, peer):
        v = vbuf.at[c]
        return remote(v, v, vc_s.at[i], vc_r.at[i], (r, peer))

    vbuf[c, r] = vin_ref[...]

    @pl.loop(1, rows)
    def _(i):
        vec_row(i).start()

    key_g[...] = place_ref[...].astype(f32)
    source = order_ref[...] // tokens
    key_w[...] = (source * tokens + lax.broadcasted_iota(jnp.int32, (1, tokens), 1)).astype(f32)
    to_col(key_g, col_g)
    to_col(key_w, col_w)
    rank_ref[0:1, :] = rank_row(key_g, col_g)
    rank_ref[1:2, :] = rank_row(key_w, col_w)
    rank_g = rank_ref[0:1, :]
    key_w[...] = rank_ref[1:2, :]
    to_col(key_w, col_w)

    first.joined()
    first.pick_and_send(rank_g)

    @pl.loop(1, rows)
    def _(i):
        vec_row(i).wait_recv()

    for i, peer in enumerate((sib, nbr, diag)):
        vec_col(i, peer).start()

    second.joined()
    second.pick_and_send(rank_g)

    for i, peer in enumerate((sib, nbr, diag)):
        vec_col(i, peer).wait_recv()
    width, wide = D // (4 * rows), 4 * D // (4 * rows)
    lane = lax.broadcasted_iota(jnp.int32, (HALF, D), 0)
    feat = lax.broadcasted_iota(jnp.int32, (HALF, D), 1)
    everyone = vbuf[:, :, 0, :].reshape(4 * rows, HALF).astype(bf16)
    mine = vbuf[c][:, 0, :].astype(bf16)
    owner = lax.broadcasted_iota(jnp.int32, (4 * rows, D), 0) == lax.broadcasted_iota(jnp.int32, (4 * rows, D), 1) // width
    vec_ref[...] = jnp.zeros_like(vec_ref)
    for i in range(6):
        hot = jnp.where(lane - (i + 2) * width == feat % width, 1.0, 0.0).astype(bf16)
        vec_ref[i : i + 1, :] = jnp.sum(jnp.where(owner, mm(everyone, hot, NN), 0.0), axis=0, keepdims=True)
    row_owner = lax.broadcasted_iota(jnp.int32, (rows, D), 0)
    row_feat = lax.broadcasted_iota(jnp.int32, (rows, D), 1)
    hot = jnp.where(lane - 8 * width == feat % wide, 1.0, 0.0).astype(bf16)
    bin_ref[...] = jnp.sum(jnp.where(row_owner == row_feat // wide, mm(mine, hot, NN), 0.0), axis=0, keepdims=True)
    bqv_ref[...] = jnp.zeros_like(bqv_ref)
    for i in range(2):
        hot = jnp.where(lane - i * width == feat % width, 1.0, 0.0).astype(bf16)
        whole = jnp.sum(jnp.where(row_owner == row_feat // width, mm(mine, hot, NN), 0.0), axis=0, keepdims=True)
        bqv_ref[i : i + 1, :] = whole[:, :FEAT]

    def piece(q, k, half):
        return tok_ref.at[q, pl.ds(pl.multiple_of(k * CH, CH), CH), half_lanes(half)]

    def tok_copy(qi, q, k, half, s, rr, peer):
        v = piece(q, k, half)
        return remote(v, v, s.at[qi, k], rr.at[qi, k], (r, peer))

    ours = ((0, c), (1, nbr))
    first.shared()

    @pl.loop(0, chunks)
    def _(k):
        at = pl.ds(pl.multiple_of(k * CH, CH), CH)
        for qi, q in ours:
            rank = col_w[pl.ds(pl.multiple_of(q * own_rows + k * CH, CH), CH), :]
            tok_ref[q, at, half_lanes(h)] = first.placed(rank).astype(bf16)
            tok_copy(qi, q, k, h, an_s, an_r, nbr).start()
            tok_copy(qi, q, k, h, as_s, as_r, sib).start()

    second.shared()
    rank = col_w[pl.ds(pl.multiple_of(nbr * own_rows, CH), own_rows), :]
    cot_send[...] = second.placed(rank).astype(bf16)
    cot_copy = remote(cot_send, cot_ref.at[:, half_lanes(h)], ct_s.at[0], ct_r.at[0], (r, nbr))
    cot_copy.start()
    rank = col_w[pl.ds(pl.multiple_of(c * own_rows, CH), own_rows), :]
    cot_ref[:, half_lanes(h)] = second.placed(rank).astype(bf16)

    @pl.loop(0, chunks)
    def _(k):
        for qi, q in ours:
            tok_copy(1 - qi, q, k, 1 - h, an_s, an_r, nbr).wait_recv()
            tok_copy(qi, q, k, 1 - h, af_s, af_r, sib).start()

    @pl.loop(0, chunks)
    def _(k):
        for qi, q in ours:
            tok_copy(qi, q, k, h, as_s, as_r, sib).wait_recv()
            tok_copy(qi, q, k, 1 - h, af_s, af_r, sib).wait_recv()
            tok_copy(qi, q, k, h, an_s, an_r, nbr).wait_send()
            tok_copy(qi, q, k, h, as_s, as_r, sib).wait_send()
            tok_copy(qi, q, k, 1 - h, af_s, af_r, sib).wait_send()

    cot_copy.wait()
    first.finish()
    second.finish()

    @pl.loop(1, rows)
    def _(i):
        vec_row(i).wait_send()

    for i, peer in enumerate((sib, nbr, diag)):
        vec_col(i, peer).wait_send()


def arrive(rows, x, g, place, order, vin):
    own_rows = x.shape[0]
    tokens = 4 * own_rows
    chunks = own_rows // CH
    S, V, DS = jax.ShapeDtypeStruct, pltpu.VMEM, pltpu.SemaphoreType.DMA
    return pl.pallas_call(
        functools.partial(arrive_body, rows),
        out_shape=(
            S((4, own_rows, D), bf16), S((own_rows, D), bf16), S((8, tokens), f32),
            S((8, D), f32), S((8, FEAT), f32), S((1, D), f32),
        ),
        in_specs=[VM] * 5,
        out_specs=(VM,) * 6,
        scratch_shapes=deal_scratch(rows, own_rows)
        + deal_sems(rows)
        + [
            V((1, tokens), f32), V((1, tokens), f32), V((tokens, 1), f32), V((tokens, 1), f32),
            V((own_rows, HALF), bf16), V((4, rows, 8, HALF), f32),
        ]
        + [DS((2, chunks))] * 6
        + [DS((1,))] * 2
        + [DS((rows,))] * 2
        + [DS((3,))] * 2,
        name="arrive",
        compiler_params=pltpu.CompilerParams(collective_id=1, has_side_effects=True, vmem_limit_bytes=56 << 20),
        cost_estimate=pl.CostEstimate(flops=60_000_000_000, bytes_accessed=20_000_000, transcendentals=0),
    )(x, g, place, order, vin)


def ring_spot(row, rows):
    return jnp.where(row % 2 == 0, row // 2, rows - 1 - row // 2)


def ring_row(spot, rows):
    spot = (spot + rows) % rows
    return jnp.where(spot < rows // 2, 2 * spot, 2 * (rows - 1 - spot) + 1)


class Ring:
    def __init__(self, rows, own, sbuf, rbuf, sems):
        self.rows, self.hops = rows, rows // 2
        self.own = own
        self.sbuf, self.rbuf = sbuf, rbuf
        self.send, self.recv = sems
        self.r, self.c = lax.axis_index("row"), lax.axis_index("col")
        self.spot = ring_spot(self.r, rows)

    def copy(self, way, t):
        to = ring_row(self.spot + (1 if way == 0 else self.rows - 1), self.rows)
        return remote(
            self.sbuf.at[way, t], self.rbuf.at[way, t], self.send.at[way, t], self.recv.at[way, t], (to, self.c)
        )

    def block(self, way, t):
        if way == 0:
            return ring_row(self.spot + self.hops - t, self.rows)
        return ring_row(self.spot + self.rows - (self.hops - 1) + t, self.rows)

    def start(self):
        for way in range(2 if self.hops > 1 else 1):
            self.sbuf[way, 0] = self.own(self.block(way, 0)).astype(bf16)
            self.copy(way, 0).start()

    def hop(self, t):
        for way in range(2):
            if t < self.hops - way:
                self.copy(way, t - 1).wait_recv()
                total = self.own(self.block(way, t)) + self.rbuf[way, t - 1].astype(f32)
                self.sbuf[way, t] = total.astype(bf16)
                self.copy(way, t).start()

    def result(self):
        self.copy(0, self.hops - 1).wait_recv()
        total = self.own(self.r) + self.rbuf[0, self.hops - 1].astype(f32)
        if self.hops > 1:
            self.copy(1, self.hops - 2).wait_recv()
            total = total + self.rbuf[1, self.hops - 2].astype(f32)
        return total

    def finish(self):
        for way in range(2):
            for t in range(self.hops - way):
                self.copy(way, t).wait_send()


def depart_body(
    rows, out_in, g1_ref, dqkv_ref, w_ref, tok_ref, rank_ref, dwo_ref, dwin_ref, dwout_ref, dvec_ref, dbin_ref,
    out_ref, grad_ref, gw_ref, gff_ref, gvec_ref, gwide_ref,
    *scratch,
):
    bufs, sems = scratch[:4], scratch[4:14]
    key, col_g, sums, dw = scratch[14:18]
    d2ds, d2dr, keep, xs, xr, gsend, grecv, r1s, r1r, r2s, r2r, vmine, vall, vrow = scratch[18:32]
    ds_s, ds_r, x_s, x_r, fin_s, fin_r, q1_s, q1_r, q2_s, q2_r, vc_s, vc_r, vr_s, vr_r = scratch[32:]
    r, c, sib, nbr, diag = col_peers()
    h = c // 2
    own_rows = out_in.shape[0]
    tokens = 4 * own_rows
    chunks = own_rows // CH
    block = D // rows
    greet((sib, nbr, diag), rows, r, c)

    def rows_of(k):
        return pl.ds(pl.multiple_of(k * CH, CH), CH)

    outs, grads = Deal(0, rows, bufs, sems), Deal(1, rows, bufs, sems)
    outs.split(out_in)
    ring_ff = Ring(
        rows, lambda b: jnp.concatenate([dwin_ref[b], dwout_ref[b]], axis=1), r1s, r1r, (q1_s, q1_r)
    )
    ring_at = Ring(
        rows, lambda b: jnp.concatenate([dw[b], dwo_ref[b]], axis=1), r2s, r2r, (q2_s, q2_r)
    )
    ring_ff.start()

    vmine[...] = jnp.zeros_like(vmine)
    vmine[0:8, :] = dvec_ref[...]

    def vec_col(i, peer):
        return remote(vmine, vall.at[c], vc_s.at[i], vc_r.at[i], (r, peer))

    for i, peer in enumerate((sib, nbr, diag)):
        vec_col(i, peer).start()

    def d2d(k):
        return remote(d2ds.at[k], d2dr.at[k], ds_s.at[k], ds_r.at[k], (r, sib))

    def xcopy(k):
        return remote(xs.at[k], xr.at[k], x_s.at[k], x_r.at[k], (r, nbr))

    def part(q, k):
        return mm(dqkv_ref[pl.ds(pl.multiple_of(q * own_rows + k * CH, CH), CH), :], w_ref[...], NT)

    @pl.loop(0, chunks)
    def _(k):
        d2ds[k, 0] = part(sib, k).astype(bf16)
        d2ds[k, 1] = part(diag, k).astype(bf16)
        d2d(k).start()
        for i, q in ((0, c), (1, nbr)):
            keep[k, i] = part(q, k)

    @pl.loop(0, chunks)
    def _(k):
        d2d(k).wait_recv()
        for i in range(2):
            keep[k, i] = keep[k, i] + d2dr[k, i].astype(f32)
            xs[k, 1 - i] = keep[k, i, :, half_lanes(1 - h)].astype(bf16)
        xcopy(k).start()

    key[...] = rank_ref[0:1, :]
    to_col(key, col_g)
    rank_w = rank_ref[1:2, :]
    outs.joined()
    outs.pick_and_send(rank_w)

    whole = mm(tok_ref[...].reshape(tokens, D), dqkv_ref[...], TN)
    for b in range(rows):
        dw[b] = whole[b * block : (b + 1) * block]
    sums[...] = jnp.zeros_like(sums)

    @pl.loop(0, tokens // QB)
    def _(k):
        part_rows = dqkv_ref[pl.ds(pl.multiple_of(k * QB, QB), QB), :].astype(f32)
        sums[0:1, :] += jnp.sum(part_rows, axis=0, keepdims=True)

    ring_ff.hop(1)

    @pl.loop(0, chunks)
    def _(k):
        xcopy(k).wait_recv()
        for i, q in ((0, c), (1, nbr)):
            total = keep[k, i, :, half_lanes(h)] + xr[k, i].astype(f32) + g1_ref[q, rows_of(k), half_lanes(h)].astype(f32)
            grads.xin[1, q, rows_of(k), :] = total.astype(bf16)

    shares = [
        remote(grads.xin.at[1, q], grads.xin.at[1, q], s.at[1], rr.at[1], (r, sib))
        for q, s, rr in ((c, grads.sib_s, grads.sib_r), (nbr, grads.fwd_s, grads.fwd_r))
    ]
    for copy in shares:
        copy.start()
    for copy in shares:
        copy.wait_recv()
    grads.pick_and_send(rank_w)
    ring_at.start()

    for i, peer in enumerate((sib, nbr, diag)):
        vec_col(i, peer).wait_recv()
    total = vmine[...] + vall[sib] + vall[nbr] + vall[diag]
    vrow[r, 0:8, :] = total[0:8, :]
    vrow[r, 8:9, :] = dbin_ref[...]
    vrow[r, 9:10, :] = jnp.concatenate([sums[0:1, :], jnp.zeros((1, FEAT), f32)], axis=1)

    def vec_row(i):
        v = vrow.at[r]
        return remote(v, v, vr_s.at[i], vr_r.at[i], ((r + i) % rows, c))

    @pl.loop(1, rows)
    def _(i):
        vec_row(i).start()

    for t in range(2, rows // 2):
        ring_ff.hop(t)
    gff_ref[...] = ring_ff.result()
    for t in range(1, rows // 2):
        ring_at.hop(t)
    gw_ref[...] = ring_at.result()

    outs.shared()

    def final(deal, i):
        rank = col_g[pl.ds(pl.multiple_of(nbr * own_rows, CH), own_rows), :]
        gsend[i] = deal.placed(rank).astype(bf16)
        return remote(gsend.at[i], grecv.at[i], fin_s.at[i], fin_r.at[i], (r, nbr))

    def own_half(deal, ref):
        rank = col_g[pl.ds(pl.multiple_of(c * own_rows, CH), own_rows), :]
        ref[:, half_lanes(h)] = deal.placed(rank)

    out_copy = final(outs, 0)
    out_copy.start()
    own_half(outs, out_ref)
    grads.shared()
    grad_copy = final(grads, 1)
    grad_copy.start()
    own_half(grads, grad_ref)

    @pl.loop(1, rows)
    def _(i):
        vec_row(i).wait_recv()

    total = vrow[0]
    for i in range(1, rows):
        total = total + vrow[i]
    width, wide = D // (4 * rows), 4 * D // (4 * rows)
    spots = lax.broadcasted_iota(jnp.int32, (D, 128), 0)
    outs_at = lax.broadcasted_iota(jnp.int32, (D, 128), 1)

    def chosen(values, first, size):
        hot = jnp.where((spots - first == outs_at) & (outs_at < size), 1.0, 0.0)
        return lax.dot_general(values, hot, NN, precision=lax.Precision.HIGHEST, preferred_element_type=f32)

    gvec_ref[0:8, :] = chosen(total[0:8, :], (c * rows + r) * width, width)
    gwide_ref[0:1, :] = chosen(total[8:16, :], r * wide, wide)[0:1, :]
    gwide_ref[1:2, :] = chosen(total[8:16, :], r * width, width)[1:2, :]
    gwide_ref[2:3, :] = chosen(total[8:16, :], 2 * FEAT + r * width, width)[1:2, :]

    out_copy.wait_recv()
    out_ref[:, half_lanes(1 - h)] = grecv[0].astype(f32)
    grad_copy.wait_recv()
    grad_ref[:, half_lanes(1 - h)] = grecv[1].astype(f32)

    out_copy.wait_send()
    grad_copy.wait_send()
    outs.finish()
    for copy in shares:
        copy.wait_send()

    @pl.loop(1, rows)
    def _(i):
        grads.row_copy(i).wait_send()

    @pl.loop(0, rows)
    def _(i):
        grads.share(i).wait_send()

    @pl.loop(0, chunks)
    def _(k):
        d2d(k).wait_send()
        xcopy(k).wait_send()

    ring_ff.finish()
    ring_at.finish()
    for i, peer in enumerate((sib, nbr, diag)):
        vec_col(i, peer).wait_send()

    @pl.loop(1, rows)
    def _(i):
        vec_row(i).wait_send()


def depart(rows, out, g1, dqkv, w_qkv, tok, rank, dwo, dwin, dwout, dvec, dbin):
    own_rows = out.shape[0]
    tokens = 4 * own_rows
    chunks = own_rows // CH
    block, hops = D // rows, rows // 2
    S, V, DS = jax.ShapeDtypeStruct, pltpu.VMEM, pltpu.SemaphoreType.DMA
    return pl.pallas_call(
        functools.partial(depart_body, rows),
        out_shape=(
            S((own_rows, D), f32), S((own_rows, D), f32), S((block, D), f32), S((block, 2 * D), f32),
            S((8, 128), f32), S((8, 128), f32),
        ),
        in_specs=[VM] * 11,
        out_specs=(VM,) * 6,
        scratch_shapes=deal_scratch(rows, own_rows)
        + deal_sems(rows)
        + [V((1, tokens), f32), V((tokens, 1), f32), V((8, 3 * FEAT), f32), V((rows, block, 3 * FEAT), f32)]
        + [
            V((chunks, 2, CH, D), bf16), V((chunks, 2, CH, D), bf16), V((chunks, 2, CH, D), f32),
            V((chunks, 2, CH, HALF), bf16), V((chunks, 2, CH, HALF), bf16),
            V((2, own_rows, HALF), bf16), V((2, own_rows, HALF), bf16),
            V((2, hops, block, 2 * D), bf16), V((2, hops, block, 2 * D), bf16),
            V((2, hops, block, D), bf16), V((2, hops, block, D), bf16),
            V((16, D), f32), V((4, 16, D), f32), V((rows, 16, D), f32),
        ]
        + [DS((chunks,))] * 4
        + [DS((2,))] * 2
        + [DS((2, hops))] * 4
        + [DS((3,))] * 2
        + [DS((rows,))] * 2,
        name="depart",
        compiler_params=pltpu.CompilerParams(collective_id=3, has_side_effects=True, vmem_limit_bytes=60 << 20),
        cost_estimate=pl.CostEstimate(flops=60_000_000_000, bytes_accessed=20_000_000, transcendentals=0),
    )(out, g1, dqkv, w_qkv, tok, rank, dwo, dwin, dwout, dvec, dbin)


def per_device(
    inputs, cotangent, token_order, token_place, seq_lengths,
    query_weight, key_weight, value_weight, output_weight, inner_weight, outer_weight,
    query_bias, value_bias, output_bias, inner_bias, outer_bias,
    first_gain, first_shift, second_gain, second_shift,
):
    rows = lax.axis_size("row")
    col = lax.axis_index("col")
    own_rows = inputs.shape[0]
    tok_rows = 4 * own_rows

    pack = jnp.concatenate(
        [query_weight, key_weight, value_weight, output_weight.T, inner_weight, outer_weight.T], axis=1
    )
    pack = lax.all_gather(pack, "row", axis=0, tiled=True)
    w_qkv, wo, win, wout = pack[:, :576], pack[:, 576:768], pack[:, 768:1536], pack[:, 1536:]
    vin = jnp.concatenate(
        [query_bias, value_bias, output_bias, first_gain, first_shift, outer_bias, second_gain, second_shift, inner_bias]
    ).astype(f32)
    vin = jnp.broadcast_to(jnp.pad(vin, (0, HALF - vin.shape[0]))[None], (8, HALF))

    seq_ends = jnp.cumsum(seq_lengths[0])
    seq_starts = seq_ends - seq_lengths[0]
    positions = jnp.arange(tok_rows, dtype=jnp.int32)
    seg = jnp.sum((positions[:, None] >= seq_ends[None, :]).astype(jnp.int32), axis=1)
    hot = (seg[:, None] == jnp.arange(seq_ends.shape[0])[None, :]).astype(jnp.int32)
    start = jnp.sum(hot * seq_starts[None], axis=1)
    end = jnp.sum(hot * seq_ends[None], axis=1)
    lo = start[::QB] // KB
    hi = (end[QB - 1 :: QB] + KB - 1) // KB
    start, end = start[None], end[None]

    tok, cot, rank, vec, bqv, b_in = arrive(rows, inputs, cotangent, token_place[None], token_order[None], vin)
    q, k, v, mixed, lse = attend_fwd(lo, hi, start, end, tok.reshape(tok_rows, D), w_qkv, bqv)
    own_tok = lax.dynamic_index_in_dim(tok, col, axis=0, keepdims=False)
    out, g1, gmix, dwo, dwin, dwout, dvec, dbin = middle(
        mixed.reshape(4, own_rows, FEAT), own_tok, cot, wo, win, wout, vec, b_in
    )
    dqkv = attend_bwd(lo, hi, start, end, q, k, v, gmix.reshape(tok_rows, FEAT), lse)
    output, input_grad, gw, gff, gvec, gwide = depart(
        rows, out, g1, dqkv, w_qkv, tok, rank,
        dwo.reshape(rows, -1, FEAT), dwin.reshape(rows, -1, D), dwout.reshape(rows, -1, D), dvec, dbin,
    )
    small, wide = query_bias.shape[0], inner_bias.shape[0]
    return (
        output, input_grad,
        gw[:, :192], gw[:, 192:384], gw[:, 384:576], gw[:, 576:].T,
        gff[:, :D], gff[:, D:].T,
        gwide[1, :small], gwide[2, :small], gvec[1, :small], gwide[0, :wide],
        gvec[2, :small], gvec[3, :small], gvec[4, :small], gvec[5, :small], gvec[6, :small],
    )


def solution(mesh):
    tok = P(("row", "col"), None)
    rc, cr, vec = P("row", "col"), P("col", "row"), P(("col", "row"))
    in_specs = (tok, tok, P("row"), P("row"), P("row", None), rc, rc, rc, cr, rc, cr) + (vec,) * 9
    out_specs = (tok, tok, rc, rc, rc, cr, rc, cr) + (vec,) * 9
    return jax.shard_map(per_device, mesh=mesh, in_specs=in_specs, out_specs=out_specs, check_vma=False)
```

```python
import functools

import jax
import jax.numpy as jnp
from jax import lax
from jax.experimental import pallas as pl
from jax.experimental.pallas import tpu as pltpu
from jax.sharding import PartitionSpec as P

D = 768
HD = 64
FEAT = 192
HEADS = 3
QB = 256
KB = 256

norm_eps = 1e-12
root_half = 0.7071067811865476
inv_root_two_pi = 0.3989422804014327
NN = (((1,), (0,)), ((), ()))
NT = (((1,), (1,)), ((), ()))
TN = (((0,), (0,)), ((), ()))
MESH = pl.DeviceIdType.MESH
f32 = jnp.float32
bf16 = jnp.bfloat16
VM = pl.BlockSpec(memory_space=pltpu.VMEM)
SM = pl.BlockSpec(memory_space=pltpu.SMEM)


def mm(a, b, dims):
    return lax.dot_general(a, b, dims, preferred_element_type=f32)


def lane_head(rows):
    return lax.broadcasted_iota(jnp.int32, (rows, FEAT), 1) // HD


def attend_fwd_body(
    lo_ref, hi_ref, start_ref, end_ref, tok_ref, w_ref, b_ref, q_ref, k_ref, v_ref, mix_ref, lse_ref, s_buf,
):
    scale = HD ** (-0.5)
    blocks = q_ref.shape[0] // QB
    heads = lane_head(QB)
    b_q, b_v = b_ref[0:1, :], b_ref[1:2, :]

    @pl.loop(0, blocks)
    def _(qb):
        rows = pl.ds(qb * QB, QB)
        out = mm(tok_ref[rows, :], w_ref[...], NN)
        q_ref[rows, :] = (out[:, :FEAT] + b_q).astype(bf16)
        k_ref[rows, :] = out[:, FEAT : 2 * FEAT].astype(bf16)
        v_ref[rows, :] = (out[:, 2 * FEAT :] + b_v).astype(bf16)

    @pl.loop(0, blocks)
    def _(qb):
        rows = pl.ds(qb * QB, QB)
        qv = q_ref[rows, :]
        qs = [jnp.where(heads == h, qv, jnp.zeros_like(qv)) for h in range(HEADS)]
        q_start = start_ref[:, rows]
        q_end = end_ref[:, rows]
        lo, hi = lo_ref[qb], hi_ref[qb]

        def scores(kb, tops):
            keys = pl.ds(pl.multiple_of(kb * KB, KB), KB)
            kv = k_ref[keys, :]
            pos = lax.broadcasted_iota(jnp.int32, (KB, QB), 0) + kb * KB
            allowed = (pos >= q_start) & (pos < q_end)
            out = []
            for h in range(HEADS):
                s = jnp.where(allowed, mm(kv, qs[h], NT) * scale, -1e30)
                s_buf[h, keys, :] = s
                out.append(jnp.maximum(tops[h], jnp.max(s, axis=0, keepdims=True)))
            return tuple(out)

        tops = lax.fori_loop(lo, hi, scores, tuple(jnp.full((1, QB), -1e30, f32) for _ in range(HEADS)))

        def weigh(kb, sums):
            keys = pl.ds(pl.multiple_of(kb * KB, KB), KB)
            out = []
            for h in range(HEADS):
                e = jnp.exp(s_buf[h, keys, :] - tops[h])
                s_buf[h, keys, :] = e
                out.append(sums[h] + jnp.sum(e, axis=0, keepdims=True))
            return tuple(out)

        sums = lax.fori_loop(lo, hi, weigh, tuple(jnp.zeros((1, QB), f32) for _ in range(HEADS)))
        inv = [1.0 / s for s in sums]

        def mix(kb, acc):
            keys = pl.ds(pl.multiple_of(kb * KB, KB), KB)
            vv = v_ref[keys, :]
            for h in range(HEADS):
                p = (s_buf[h, keys, :] * inv[h]).astype(bf16)
                acc = acc + jnp.where(heads == h, mm(p, vv, TN), 0.0)
            return acc

        acc = lax.fori_loop(lo, hi, mix, jnp.zeros((QB, FEAT), f32))
        mix_ref[rows, :] = acc.astype(bf16)
        for h in range(HEADS):
            lse_ref[pl.ds(h, 1), rows] = tops[h] + jnp.log(sums[h])


def attend_fwd(lo, hi, start, end, tokens, w_qkv, bias):
    rows = tokens.shape[0]
    part = jax.ShapeDtypeStruct((rows, FEAT), bf16)
    return pl.pallas_call(
        attend_fwd_body,
        out_shape=(part, part, part, part, jax.ShapeDtypeStruct((8, rows), f32)),
        in_specs=[SM, SM] + [VM] * 5,
        out_specs=(VM,) * 5,
        scratch_shapes=[pltpu.VMEM((HEADS, rows, QB), f32)],
        name="attend_fwd",
        compiler_params=pltpu.CompilerParams(vmem_limit_bytes=40 << 20),
        cost_estimate=pl.CostEstimate(flops=8_000_000_000, bytes_accessed=8_000_000, transcendentals=4_000_000),
    )(lo, hi, start, end, tokens, w_qkv, bias)


def attend_bwd_body(
    lo_ref, hi_ref, start_ref, end_ref, q_ref, k_ref, v_ref, do_ref, lse_ref,
    dqkv_ref, p_buf, dp_buf, dq_acc, dk_acc, dv_acc,
):
    scale = HD ** (-0.5)
    blocks = q_ref.shape[0] // QB
    heads = lane_head(QB)
    key_heads = lane_head(KB)
    dk_acc[...] = jnp.zeros_like(dk_acc)
    dv_acc[...] = jnp.zeros_like(dv_acc)

    @pl.loop(0, blocks)
    def _(qb):
        rows = pl.ds(qb * QB, QB)
        qv = q_ref[rows, :]
        dv_in = do_ref[rows, :]
        qs = [jnp.where(heads == h, qv, jnp.zeros_like(qv)) for h in range(HEADS)]
        dos = [jnp.where(heads == h, dv_in, jnp.zeros_like(dv_in)) for h in range(HEADS)]
        q_start = start_ref[:, rows]
        q_end = end_ref[:, rows]
        lse = [lse_ref[pl.ds(h, 1), rows] for h in range(HEADS)]
        lo, hi = lo_ref[qb], hi_ref[qb]

        def first(kb, sums):
            keys = pl.ds(pl.multiple_of(kb * KB, KB), KB)
            kv, vv = k_ref[keys, :], v_ref[keys, :]
            pos = lax.broadcasted_iota(jnp.int32, (KB, QB), 0) + kb * KB
            allowed = (pos >= q_start) & (pos < q_end)
            out = []
            grad_v = dv_acc[keys, :]
            for h in range(HEADS):
                p = jnp.where(allowed, jnp.exp(mm(kv, qs[h], NT) * scale - lse[h]), 0.0)
                dp = mm(vv, dos[h], NT)
                p_buf[h, keys, :] = p
                dp_buf[h, keys, :] = dp
                out.append(sums[h] + jnp.sum(p * dp, axis=0, keepdims=True))
                grad_v = grad_v + mm(p.astype(bf16), dos[h], NN)
            dv_acc[keys, :] = grad_v
            return tuple(out)

        sums = lax.fori_loop(lo, hi, first, tuple(jnp.zeros((1, QB), f32) for _ in range(HEADS)))

        def second(kb, acc):
            keys = pl.ds(pl.multiple_of(kb * KB, KB), KB)
            kv = k_ref[keys, :]
            grad_k = dk_acc[keys, :]
            for h in range(HEADS):
                ds = (p_buf[h, keys, :] * (dp_buf[h, keys, :] - sums[h])).astype(bf16)
                grad_k = grad_k + mm(ds, qs[h], NN)
                acc = acc + jnp.where(heads == h, mm(ds, kv, TN), 0.0)
            dk_acc[keys, :] = grad_k
            return acc

        acc = lax.fori_loop(lo, hi, second, jnp.zeros((QB, FEAT), f32))
        dq_acc[rows, :] = acc

    @pl.loop(0, blocks)
    def _(qb):
        rows = pl.ds(qb * QB, QB)
        parts = [dq_acc[rows, :] * scale, dk_acc[rows, :] * scale, dv_acc[rows, :]]
        dqkv_ref[rows, :] = jnp.concatenate([p.astype(bf16) for p in parts], axis=1)


def attend_bwd(lo, hi, start, end, q, k, v, do, lse):
    rows = q.shape[0]
    return pl.pallas_call(
        attend_bwd_body,
        out_shape=jax.ShapeDtypeStruct((rows, 3 * FEAT), bf16),
        in_specs=[SM, SM] + [VM] * 7,
        out_specs=VM,
        scratch_shapes=[
            pltpu.VMEM((HEADS, rows, QB), f32),
            pltpu.VMEM((HEADS, rows, QB), f32),
            pltpu.VMEM((rows, FEAT), f32),
            pltpu.VMEM((rows, FEAT), f32),
            pltpu.VMEM((rows, FEAT), f32),
        ],
        name="attend_bwd",
        compiler_params=pltpu.CompilerParams(vmem_limit_bytes=48 << 20),
        cost_estimate=pl.CostEstimate(flops=20_000_000_000, bytes_accessed=6_000_000, transcendentals=4_000_000),
    )(lo, hi, start, end, q, k, v, do, lse)


def remote(src, dst, send_sem, recv_sem, device):
    return pltpu.make_async_remote_copy(
        src_ref=src, dst_ref=dst, send_sem=send_sem, recv_sem=recv_sem,
        device_id=device, device_id_type=MESH,
    )


def col_peers():
    r, c = lax.axis_index("row"), lax.axis_index("col")
    sib, nbr, diag = c + 1 - 2 * (c % 2), (c + 2) % 4, 3 - c
    return r, c, sib, nbr, diag


def norm_rows(x):
    mean = jnp.mean(x, axis=1, keepdims=True)
    center = x - mean
    var = jnp.mean(center * center, axis=1, keepdims=True)
    inv = lax.rsqrt(var + norm_eps)
    return center * inv, inv


def norm_back(grad, gain, hat, inv):
    e = grad * gain
    mean_e = jnp.mean(e, axis=1, keepdims=True)
    mean_c = jnp.mean(e * hat, axis=1, keepdims=True)
    return inv * (e - mean_e - hat * mean_c)


CH = 128


HALF = 384


def half_lanes(h):
    return pl.ds(pl.multiple_of(h * HALF, HALF), HALF)


def greet(peers, rows, row, c):
    barrier = pltpu.get_barrier_semaphore()
    for peer in peers:
        pl.semaphore_signal(barrier, inc=1, device_id=(row, peer), device_id_type=MESH)

    @pl.loop(1, rows)
    def _(i):
        pl.semaphore_signal(barrier, inc=1, device_id=((row + i) % rows, c), device_id_type=MESH)

    pl.semaphore_wait(barrier, len(peers) + rows - 1)


def to_col(src, dst):
    eye = lax.broadcasted_iota(jnp.int32, (128, 128), 0) == lax.broadcasted_iota(jnp.int32, (128, 128), 1)

    @pl.loop(0, dst.shape[0] // 128)
    def _(t):
        at = pl.ds(pl.multiple_of(t * 128, 128), 128)
        dst[at, :] = jnp.sum(jnp.where(eye, src[:, at], 0.0), axis=1, keepdims=True)


def rank_row(row_ref, col_ref):
    keys = row_ref[...]
    size = keys.shape[1]

    def step(t, acc):
        col = col_ref[pl.ds(pl.multiple_of(t * 128, 128), 128), :]
        less = jnp.where(col < keys, 1.0, 0.0)
        return acc + jnp.sum(less.reshape(16, 8, size), axis=0)

    acc = lax.fori_loop(0, size // 128, step, jnp.zeros((8, size), f32))
    return jnp.sum(acc, axis=0, keepdims=True)


def picker_rows(rank, first, count):
    want = (lax.broadcasted_iota(jnp.int32, (count, rank.shape[1]), 0) + first).astype(f32)
    return jnp.where(rank == want, 1.0, 0.0).astype(bf16)


def picker_cols(rank, count):
    have = lax.broadcasted_iota(jnp.int32, (rank.shape[0], count), 1).astype(f32)
    return jnp.where(rank == have, 1.0, 0.0).astype(bf16)


def placed(rank_col, got):
    tokens = got.shape[0] * got.shape[1] * got.shape[2]
    return mm(picker_cols(rank_col, tokens), got.reshape(tokens, HALF), NN)


class Deal:
    def __init__(self, a, rows, bufs, sems):
        self.a, self.rows = a, rows
        self.xin, self.xout, self.sbuf, self.rbuf = bufs
        self.sib_s, self.sib_r, self.nbr_s, self.nbr_r, self.fwd_s, self.fwd_r, self.row_s, self.row_r, self.sh_s, self.sh_r = sems
        self.r, self.c, self.sib, self.nbr, self.diag = col_peers()
        self.h, self.core = self.c // 2, self.c % 2
        self.tokens = self.xin.shape[2] * 4
        self.slots = self.tokens // rows
        self.own_slots = self.slots // 2

    def to_sib(self):
        v = self.xin.at[self.a, self.c]
        return remote(v, v, self.sib_s.at[self.a], self.sib_r.at[self.a], (self.r, self.sib))

    def to_nbr(self):
        return remote(self.xout.at[self.a], self.xin.at[self.a, self.c], self.nbr_s.at[self.a], self.nbr_r.at[self.a], (self.r, self.nbr))

    def fwd(self):
        v = self.xin.at[self.a, self.nbr]
        return remote(v, v, self.fwd_s.at[self.a], self.fwd_r.at[self.a], (self.r, self.sib))

    def split(self, ref):
        self.xout[self.a] = ref[:, half_lanes(1 - self.h)].astype(bf16)
        self.to_nbr().start()
        self.xin[self.a, self.c] = ref[:, half_lanes(self.h)].astype(bf16)
        self.to_sib().start()

    def joined(self):
        self.to_nbr().wait_recv()
        self.fwd().start()
        self.to_sib().wait_recv()
        self.fwd().wait_recv()

    def row_copy(self, i):
        to = (self.r + i) % self.rows
        return remote(
            self.sbuf.at[self.a, i], self.rbuf.at[self.a, self.r, self.core],
            self.row_s.at[self.a, i], self.row_r.at[self.a, i], (to, self.c),
        )

    def share(self, i):
        v = self.rbuf.at[self.a, (self.r + self.rows - i) % self.rows, self.core]
        return remote(v, v, self.sh_s.at[self.a, i], self.sh_r.at[self.a, i], (self.r, self.sib))

    def pick_and_send(self, rank):
        source = self.xin[self.a].reshape(self.tokens, HALF)

        def picked(to):
            return mm(picker_rows(rank, to * self.slots + self.core * self.own_slots, self.own_slots), source, NN).astype(bf16)

        @pl.loop(1, self.rows)
        def _(i):
            self.sbuf[self.a, i] = picked((self.r + i) % self.rows)
            self.row_copy(i).start()

        self.rbuf[self.a, self.r, self.core] = picked(self.r)
        self.share(0).start()

    def shared(self):
        @pl.loop(1, self.rows)
        def _(i):
            self.row_copy(i).wait_recv()
            self.share(i).start()

        @pl.loop(0, self.rows)
        def _(i):
            self.share(i).wait_recv()

    def placed(self, rank_col):
        return placed(rank_col, self.rbuf[self.a])

    def joined_sent(self):
        self.to_sib().wait_send()
        self.to_nbr().wait_send()
        self.fwd().wait_send()

    def rows_sent(self):
        @pl.loop(1, self.rows)
        def _(i):
            self.row_copy(i).wait_send()

        @pl.loop(0, self.rows)
        def _(i):
            self.share(i).wait_send()


def deal_scratch(rows, own_rows, count):
    slots = 4 * own_rows // rows
    return [
        pltpu.VMEM((count, 4, own_rows, HALF), bf16),
        pltpu.VMEM((count, own_rows, HALF), bf16),
        pltpu.VMEM((count, rows, slots // 2, HALF), bf16),
        pltpu.VMEM((count, rows, 2, slots // 2, HALF), bf16),
    ]


def deal_sems(rows, count):
    return [pltpu.SemaphoreType.DMA((count,))] * 6 + [pltpu.SemaphoreType.DMA((count, rows))] * 4


def arrive_body(
    rows, x_ref, g_ref, place_ref, order_ref, vin_ref,
    tok_ref, own_ref, cot_ref, cot_send, rank_ref, vec_ref, bqv_ref, bin_ref,
    *scratch,
):
    bufs, sems = scratch[:4], scratch[4:14]
    key_g, key_w, col_g, col_w, vbuf = scratch[14:19]
    an_s, an_r, as_s, as_r, af_s, af_r, vr_s, vr_r, vc_s, vc_r = scratch[19:]
    r, c, sib, nbr, diag = col_peers()
    h = c // 2
    own_rows = x_ref.shape[0]
    tokens = 4 * own_rows
    chunks = own_rows // CH
    greet((sib, nbr, diag), rows, r, c)

    first, second = Deal(0, rows, bufs, sems), Deal(1, rows, bufs, sems)
    first.split(x_ref)
    second.split(g_ref)

    def vec_row(i):
        v = vbuf.at[c, r]
        return remote(v, v, vr_s.at[i], vr_r.at[i], ((r + i) % rows, c))

    def vec_col(i, peer):
        v = vbuf.at[c]
        return remote(v, v, vc_s.at[i], vc_r.at[i], (r, peer))

    vbuf[c, r] = vin_ref[...]

    @pl.loop(1, rows)
    def _(i):
        vec_row(i).start()

    key_g[...] = place_ref[...].astype(f32)
    source = order_ref[...] // tokens
    key_w[...] = (source * tokens + lax.broadcasted_iota(jnp.int32, (1, tokens), 1)).astype(f32)
    to_col(key_g, col_g)
    to_col(key_w, col_w)
    rank_ref[0:1, :] = rank_row(key_g, col_g)
    rank_ref[1:2, :] = rank_row(key_w, col_w)
    rank_g = rank_ref[0:1, :]
    key_w[...] = rank_ref[1:2, :]
    to_col(key_w, col_w)

    first.joined()
    first.pick_and_send(rank_g)

    @pl.loop(1, rows)
    def _(i):
        vec_row(i).wait_recv()

    for i, peer in enumerate((sib, nbr, diag)):
        vec_col(i, peer).start()

    second.joined()
    second.pick_and_send(rank_g)

    for i, peer in enumerate((sib, nbr, diag)):
        vec_col(i, peer).wait_recv()
    width, wide = D // (4 * rows), 4 * D // (4 * rows)
    lane = lax.broadcasted_iota(jnp.int32, (HALF, D), 0)
    feat = lax.broadcasted_iota(jnp.int32, (HALF, D), 1)
    everyone = vbuf[:, :, 0, :].reshape(4 * rows, HALF).astype(bf16)
    mine = vbuf[c][:, 0, :].astype(bf16)
    owner = lax.broadcasted_iota(jnp.int32, (4 * rows, D), 0) == lax.broadcasted_iota(jnp.int32, (4 * rows, D), 1) // width
    vec_ref[...] = jnp.zeros_like(vec_ref)
    for i in range(6):
        hot = jnp.where(lane - (i + 2) * width == feat % width, 1.0, 0.0).astype(bf16)
        vec_ref[i : i + 1, :] = jnp.sum(jnp.where(owner, mm(everyone, hot, NN), 0.0), axis=0, keepdims=True)
    row_owner = lax.broadcasted_iota(jnp.int32, (rows, D), 0)
    row_feat = lax.broadcasted_iota(jnp.int32, (rows, D), 1)
    hot = jnp.where(lane - 8 * width == feat % wide, 1.0, 0.0).astype(bf16)
    bin_ref[...] = jnp.sum(jnp.where(row_owner == row_feat // wide, mm(mine, hot, NN), 0.0), axis=0, keepdims=True)
    bqv_ref[...] = jnp.zeros_like(bqv_ref)
    for i in range(2):
        hot = jnp.where(lane - i * width == feat % width, 1.0, 0.0).astype(bf16)
        whole = jnp.sum(jnp.where(row_owner == row_feat // width, mm(mine, hot, NN), 0.0), axis=0, keepdims=True)
        bqv_ref[i : i + 1, :] = whole[:, :FEAT]

    def piece(q, k, half):
        return tok_ref.at[q, pl.ds(pl.multiple_of(k * CH, CH), CH), half_lanes(half)]

    def tok_copy(qi, q, k, half, s, rr, peer):
        v = piece(q, k, half)
        return remote(v, v, s.at[qi, k], rr.at[qi, k], (r, peer))

    ours = ((0, c), (1, nbr))
    first.shared()

    @pl.loop(0, chunks)
    def _(k):
        at = pl.ds(pl.multiple_of(k * CH, CH), CH)
        for qi, q in ours:
            rank = col_w[pl.ds(pl.multiple_of(q * own_rows + k * CH, CH), CH), :]
            tok_ref[q, at, half_lanes(h)] = first.placed(rank).astype(bf16)
            tok_copy(qi, q, k, h, an_s, an_r, nbr).start()
            tok_copy(qi, q, k, h, as_s, as_r, sib).start()

    def pass_on(k):
        for qi, q in ours:
            tok_copy(1 - qi, q, k, 1 - h, an_s, an_r, nbr).wait_recv()
            tok_copy(qi, q, k, 1 - h, af_s, af_r, sib).start()

    pl.loop(0, chunks // 2)(pass_on)
    second.shared()
    pl.loop(chunks // 2, chunks)(pass_on)
    for q, ref in ((nbr, cot_send), (c, cot_ref)):

        @pl.loop(0, chunks)
        def _(k):
            rank = col_w[pl.ds(pl.multiple_of(q * own_rows + k * CH, CH), CH), :]
            ref[pl.ds(pl.multiple_of(k * CH, CH), CH), :] = second.placed(rank).astype(bf16)

    @pl.loop(0, chunks)
    def _(k):
        for qi, q in ours:
            tok_copy(qi, q, k, h, as_s, as_r, sib).wait_recv()
            tok_copy(qi, q, k, 1 - h, af_s, af_r, sib).wait_recv()
            tok_copy(qi, q, k, h, an_s, an_r, nbr).wait_send()
            tok_copy(qi, q, k, h, as_s, as_r, sib).wait_send()
            tok_copy(qi, q, k, 1 - h, af_s, af_r, sib).wait_send()

    own_ref[...] = tok_ref[c]

    for deal in (first, second):
        deal.joined_sent()
        deal.rows_sent()

    @pl.loop(1, rows)
    def _(i):
        vec_row(i).wait_send()

    for i, peer in enumerate((sib, nbr, diag)):
        vec_col(i, peer).wait_send()


def arrive(rows, x, g, place, order, vin):
    own_rows = x.shape[0]
    tokens = 4 * own_rows
    chunks = own_rows // CH
    S, V, DS = jax.ShapeDtypeStruct, pltpu.VMEM, pltpu.SemaphoreType.DMA
    return pl.pallas_call(
        functools.partial(arrive_body, rows),
        out_shape=(
            S((4, own_rows, D), bf16), S((own_rows, D), bf16),
            S((own_rows, HALF), bf16), S((own_rows, HALF), bf16), S((8, tokens), f32),
            S((8, D), f32), S((8, FEAT), f32), S((1, D), f32),
        ),
        in_specs=[VM] * 5,
        out_specs=(VM,) * 8,
        scratch_shapes=deal_scratch(rows, own_rows, 2)
        + deal_sems(rows, 2)
        + [
            V((1, tokens), f32), V((1, tokens), f32), V((tokens, 1), f32), V((tokens, 1), f32),
            V((4, rows, 8, HALF), f32),
        ]
        + [DS((2, chunks))] * 6
        + [DS((rows,))] * 2
        + [DS((3,))] * 2,
        name="arrive",
        compiler_params=pltpu.CompilerParams(collective_id=1, has_side_effects=True, vmem_limit_bytes=56 << 20),
        cost_estimate=pl.CostEstimate(flops=60_000_000_000, bytes_accessed=20_000_000, transcendentals=0),
    )(x, g, place, order, vin)


def ring_spot(row, rows):
    return jnp.where(row % 2 == 0, row // 2, rows - 1 - row // 2)


def ring_row(spot, rows):
    spot = (spot + rows) % rows
    return jnp.where(spot < rows // 2, 2 * spot, 2 * (rows - 1 - spot) + 1)


class Ring:
    def __init__(self, rows, own, sbuf, rbuf, sems):
        self.rows, self.hops = rows, rows // 2
        self.own = own
        self.sbuf, self.rbuf = sbuf, rbuf
        self.send, self.recv = sems
        self.r, self.c = lax.axis_index("row"), lax.axis_index("col")
        self.spot = ring_spot(self.r, rows)

    def copy(self, way, t):
        to = ring_row(self.spot + (1 if way == 0 else self.rows - 1), self.rows)
        return remote(
            self.sbuf.at[way, t], self.rbuf.at[way, t], self.send.at[way, t], self.recv.at[way, t], (to, self.c)
        )

    def block(self, way, t):
        if way == 0:
            return ring_row(self.spot + self.hops - t, self.rows)
        return ring_row(self.spot + self.rows - (self.hops - 1) + t, self.rows)

    def start(self):
        for way in range(2 if self.hops > 1 else 1):
            self.sbuf[way, 0] = self.own(self.block(way, 0)).astype(bf16)
            self.copy(way, 0).start()

    def hop(self, t):
        for way in range(2):
            if t < self.hops - way:
                self.copy(way, t - 1).wait_recv()
                total = self.own(self.block(way, t)) + self.rbuf[way, t - 1].astype(f32)
                self.sbuf[way, t] = total.astype(bf16)
                self.copy(way, t).start()

    def result(self):
        self.copy(0, self.hops - 1).wait_recv()
        total = self.own(self.r) + self.rbuf[0, self.hops - 1].astype(f32)
        if self.hops > 1:
            self.copy(1, self.hops - 2).wait_recv()
            total = total + self.rbuf[1, self.hops - 2].astype(f32)
        return total

    def finish(self):
        for way in range(2):
            for t in range(self.hops - way):
                self.copy(way, t).wait_send()


def middle_body(
    rows, mixed_ref, tok_ref, cot_own, cot_got, wo_ref, win_ref, wout_ref, vec_ref, bin_ref, rank_ref,
    back_ref, g1_ref, gmix_ref, dwo_ref, gin_ref, gout_ref, dvec_ref, dbin_ref,
    *scratch,
):
    nfull, hidden, slope, g2full, own, d2ds, d2dr, xs, xr, hat1, inv1, grad2, dwin, dwout = scratch[:14]
    out_buf, xin, xout, sbuf, ring_out, ring_in = scratch[14:20]
    ds_s, ds_r, x_s, x_r, asib_s, asib_r, anbr_s, anbr_r, afwd_s, afwd_r, q_s, q_r = scratch[20:32]
    r, c, sib, nbr, diag = col_peers()
    h = c // 2
    chunks = out_buf.shape[0] // CH
    block = D // rows
    greet((sib, nbr), rows, r, c)
    outs = Deal(0, rows, (xin, xout, sbuf, back_ref), scratch[32:])
    ring = Ring(rows, lambda b: jnp.concatenate([dwin[b], dwout[b]], axis=1), ring_out, ring_in, (q_s, q_r))

    bo, g1, s1, b2, g2, s2 = [vec_ref[pl.ds(i, 1), :] for i in range(6)]

    def d2d(st, k):
        return remote(d2ds.at[k], d2dr.at[k], ds_s.at[st, k], ds_r.at[st, k], (r, sib))

    def xcopy(st, k):
        return remote(xs.at[k], xr.at[k], x_s.at[st, k], x_r.at[st, k], (r, nbr))

    def rs_start(st, k, part):
        if st > 0:
            d2d(st - 1, k).wait_send()
            xcopy(st - 1, k).wait_send()
        d2ds[k, 0] = part(sib).astype(bf16)
        d2ds[k, 1] = part(diag).astype(bf16)
        d2d(st, k).start()
        mine = part(c)
        other = part(nbr)
        d2d(st, k).wait_recv()
        xs[k] = (other + d2dr[k, 1].astype(f32)).astype(bf16)
        xcopy(st, k).start()
        own[k] = mine + d2dr[k, 0].astype(f32)

    def rs_end(st, k):
        xcopy(st, k).wait_recv()
        return own[k] + xr[k].astype(f32)

    gathered = (nfull, g2full, g1_ref)

    def piece(st, q, k):
        return gathered[st].at[q, pl.ds(pl.multiple_of(k * CH, CH), CH), :]

    def ag_copy(st, k, q, sems, target):
        return remote(piece(st, q, k), piece(st, q, k), sems[0].at[st, k], sems[1].at[st, k], (r, target))

    to_sib = functools.partial(ag_copy, sems=(asib_s, asib_r), target=sib)
    to_nbr = functools.partial(ag_copy, sems=(anbr_s, anbr_r), target=nbr)
    fwd = functools.partial(ag_copy, sems=(afwd_s, afwd_r), target=sib)

    def ag_start(st, k, value):
        gathered[st][c, pl.ds(pl.multiple_of(k * CH, CH), CH), :] = value
        to_nbr(st, k, c).start()
        to_sib(st, k, c).start()

    def ag_end(st, k):
        to_nbr(st, k, c).wait_recv()
        fwd(st, k, nbr).start()
        to_sib(st, k, c).wait_recv()
        fwd(st, k, nbr).wait_recv()

    def rows_of(k):
        return pl.ds(pl.multiple_of(k * CH, CH), CH)

    def all_rows(ref, k):
        return ref[:, rows_of(k), :].reshape(4 * CH, ref.shape[2])

    @pl.loop(0, chunks)
    def _(k):
        rs_start(0, k, lambda q: mm(mixed_ref[q, rows_of(k), :], wo_ref[...], NT))

    @pl.loop(0, chunks)
    def _(k):
        resid = rs_end(0, k) + tok_ref[rows_of(k), :].astype(f32) + bo
        hat, inv = norm_rows(resid)
        hat1[k] = hat
        inv1[k] = inv
        val = hat * g1 + s1
        ag_start(0, k, val.astype(bf16))

    @pl.loop(0, chunks)
    def _(k):
        ag_end(0, k)
        pre = mm(all_rows(nfull, k), win_ref[...], NN) + bin_ref[...]
        cum = 0.5 * (1.0 + lax.erf(pre * root_half))
        dens = jnp.exp(-0.5 * pre * pre) * inv_root_two_pi
        hidden[:, rows_of(k), :] = (pre * cum).astype(bf16).reshape(4, CH, D)
        slope[:, rows_of(k), :] = (cum + pre * dens).reshape(4, CH, D)
        rs_start(1, k, lambda q: mm(hidden[q, rows_of(k), :], wout_ref[...], NT))

    dvec_ref[...] = jnp.zeros_like(dvec_ref)

    @pl.loop(0, chunks)
    def _(k):
        resid = rs_end(1, k) + (hat1[k] * g1 + s1) + b2
        hat, inv = norm_rows(resid)
        out_buf[rows_of(k), :] = (hat * g2 + s2).astype(bf16)
        halves = (cot_own[rows_of(k), :], cot_got[rows_of(k), :])
        low, high = jnp.where(h == 0, halves[0], halves[1]), jnp.where(h == 0, halves[1], halves[0])
        cot = jnp.concatenate([low, high], axis=1).astype(f32)
        grad = norm_back(cot, g2, hat, inv)
        grad2[k] = grad
        ag_start(1, k, grad.astype(bf16))
        dvec_ref[pl.ds(2, 1), :] += jnp.sum(grad, axis=0, keepdims=True)
        dvec_ref[pl.ds(5, 1), :] += jnp.sum(cot * hat, axis=0, keepdims=True)
        dvec_ref[pl.ds(6, 1), :] += jnp.sum(cot, axis=0, keepdims=True)

    outs.split(out_buf)
    dwin[...] = jnp.zeros_like(dwin)
    dwout[...] = jnp.zeros_like(dwout)
    dwo_ref[...] = jnp.zeros_like(dwo_ref)
    dbin_ref[...] = jnp.zeros_like(dbin_ref)

    def add_blocks(ref, value):
        if block % 8 == 0:
            ref[...] += value.reshape(rows, block, D)
        else:
            for b in range(rows):
                ref[b] += value[b * block : (b + 1) * block]

    def back_hidden(k):
        ag_end(1, k)
        g2c = all_rows(g2full, k)
        grad_pre = mm(g2c, wout_ref[...], NN) * all_rows(slope, k)
        dbin_ref[...] += jnp.sum(grad_pre, axis=0, keepdims=True)
        low = grad_pre.astype(bf16)
        hid = all_rows(hidden, k)
        hidden[:, rows_of(k), :] = low.reshape(4, CH, D)
        rs_start(2, k, lambda q: mm(hidden[q, rows_of(k), :], win_ref[...], NT))
        add_blocks(dwout, mm(g2c, hid, TN))
        add_blocks(dwin, mm(all_rows(nfull, k), low, TN))

    pl.loop(0, chunks // 2)(back_hidden)
    outs.joined()
    outs.pick_and_send(rank_ref[1:2, :])
    pl.loop(chunks // 2, chunks)(back_hidden)
    ring.start()

    def hops(part):
        for t in range(1 + part * (ring.hops - 1) // 3, 1 + (part + 1) * (ring.hops - 1) // 3):
            ring.hop(t)

    def back_first(k):
        grad_normed = rs_end(2, k) + grad2[k]
        hat = hat1[k]
        grad = norm_back(grad_normed, g1, hat, inv1[k])
        ag_start(2, k, grad.astype(bf16))
        dvec_ref[pl.ds(1, 1), :] += jnp.sum(grad, axis=0, keepdims=True)
        dvec_ref[pl.ds(3, 1), :] += jnp.sum(grad_normed * hat, axis=0, keepdims=True)
        dvec_ref[pl.ds(4, 1), :] += jnp.sum(grad_normed, axis=0, keepdims=True)

    pl.loop(0, chunks // 2)(back_first)
    hops(0)
    pl.loop(chunks // 2, chunks)(back_first)
    hops(1)

    def back_mixed(k):
        ag_end(2, k)
        g1c = all_rows(g1_ref, k)
        gmix_ref[:, rows_of(k), :] = mm(g1c, wo_ref[...], NN).astype(bf16).reshape(4, CH, FEAT)
        dwo_ref[...] += mm(g1c, all_rows(mixed_ref, k), TN)

    pl.loop(0, chunks // 2)(back_mixed)
    hops(2)
    pl.loop(chunks // 2, chunks)(back_mixed)
    outs.shared()
    total = ring.result()
    gin_ref[...] = total[:, :D]
    gout_ref[...] = total[:, D:].T

    @pl.loop(0, chunks)
    def _(k):
        d2d(2, k).wait_send()
        xcopy(2, k).wait_send()
        for st in range(3):
            to_sib(st, k, c).wait_send()
            to_nbr(st, k, c).wait_send()
            fwd(st, k, nbr).wait_send()

    outs.joined_sent()
    outs.rows_sent()
    ring.finish()


def middle(rows, mixed, tok, cot_own, cot_got, wo, win, wout, vec, b_in, rank):
    own_rows = tok.shape[0]
    chunks = own_rows // CH
    block, hops, slots = D // rows, rows // 2, 4 * own_rows // rows
    sem = pltpu.SemaphoreType.DMA((3, chunks))
    S, V = jax.ShapeDtypeStruct, pltpu.VMEM
    return pl.pallas_call(
        functools.partial(middle_body, rows),
        out_shape=(
            S((1, rows, 2, slots // 2, HALF), bf16),
            S((4, own_rows, D), bf16),
            S((4, own_rows, FEAT), bf16),
            S((D, FEAT), f32),
            S((block, D), f32),
            S((D, block), f32),
            S((8, D), f32),
            S((1, D), f32),
        ),
        in_specs=[VM] * 10,
        out_specs=(VM,) * 8,
        scratch_shapes=[
            pltpu.VMEM((4, own_rows, D), bf16),
            pltpu.VMEM((4, own_rows, D), bf16),
            pltpu.VMEM((4, own_rows, D), f32),
            pltpu.VMEM((4, own_rows, D), bf16),
            pltpu.VMEM((chunks, CH, D), f32),
            pltpu.VMEM((chunks, 2, CH, D), bf16),
            pltpu.VMEM((chunks, 2, CH, D), bf16),
            pltpu.VMEM((chunks, CH, D), bf16),
            pltpu.VMEM((chunks, CH, D), bf16),
            pltpu.VMEM((chunks, CH, D), f32),
            pltpu.VMEM((chunks, CH, 1), f32),
            pltpu.VMEM((chunks, CH, D), f32),
            V((rows, block, D), f32),
            V((rows, block, D), f32),
            V((own_rows, D), bf16),
        ]
        + deal_scratch(rows, own_rows, 1)[:3]
        + [V((2, hops, block, 2 * D), bf16)] * 2
        + [sem] * 10
        + [pltpu.SemaphoreType.DMA((2, hops))] * 2
        + deal_sems(rows, 1),
        name="middle",
        compiler_params=pltpu.CompilerParams(collective_id=2, has_side_effects=True, vmem_limit_bytes=62 << 20),
        cost_estimate=pl.CostEstimate(flops=80_000_000_000, bytes_accessed=20_000_000, transcendentals=4_000_000),
    )(mixed, tok, cot_own, cot_got, wo, win, wout, vec, b_in, rank)


def depart_body(
    rows, back_ref, g1_ref, dqkv_ref, w_ref, tok_ref, rank_ref, dwo_ref, dvec_ref, dbin_ref,
    out_ref, grad_ref, gq_ref, gk_ref, gv_ref, go_ref, gvec_ref, gwide_ref,
    *scratch,
):
    bufs, sems = scratch[:4], scratch[4:14]
    key, col_g, sums, dw = scratch[14:18]
    d2ds, d2dr, keep, xs, xr, gsend, grecv, r2s, r2r, vmine, vall, vrow = scratch[18:30]
    ds_s, ds_r, x_s, x_r, fin_s, fin_r, q2_s, q2_r, sh_s, sh_r, vc_s, vc_r, vr_s, vr_r = scratch[30:]
    r, c, sib, nbr, diag = col_peers()
    h = c // 2
    own_rows = out_ref.shape[0]
    tokens = 4 * own_rows
    chunks = own_rows // CH
    block = D // rows
    greet((sib, nbr, diag), rows, r, c)

    def rows_of(k):
        return pl.ds(pl.multiple_of(k * CH, CH), CH)

    def token_rows(q, k):
        return pl.ds(pl.multiple_of(q * own_rows + k * CH, CH), CH)

    grads = Deal(0, rows, bufs, sems)
    ring = Ring(rows, lambda b: jnp.concatenate([dw[b], dwo_ref[b]], axis=1), r2s, r2r, (q2_s, q2_r))
    ours = ((0, c), (1, nbr))

    vmine[...] = jnp.zeros_like(vmine)
    vmine[0:8, :] = dvec_ref[...]

    def vec_col(i, peer):
        return remote(vmine, vall.at[c], vc_s.at[i], vc_r.at[i], (r, peer))

    for i, peer in enumerate((sib, nbr, diag)):
        vec_col(i, peer).start()

    def d2d(k):
        return remote(d2ds.at[k], d2dr.at[k], ds_s.at[k], ds_r.at[k], (r, sib))

    def xcopy(k):
        return remote(xs.at[k], xr.at[k], x_s.at[k], x_r.at[k], (r, nbr))

    def part(q, k):
        return mm(dqkv_ref[token_rows(q, k), :], w_ref[...], NT)

    @pl.loop(0, chunks)
    def _(k):
        d2ds[k, 0] = part(sib, k).astype(bf16)
        d2ds[k, 1] = part(diag, k).astype(bf16)
        d2d(k).start()
        for i, q in ours:
            keep[k, i] = part(q, k)
        d2d(k).wait_recv()
        for i in range(2):
            keep[k, i] = keep[k, i] + d2dr[k, i].astype(f32)
            xs[k, 1 - i] = keep[k, i, :, half_lanes(1 - h)].astype(bf16)
        xcopy(k).start()

    whole = mm(tok_ref[...].reshape(tokens, D), dqkv_ref[...], TN)
    for b in range(rows):
        dw[b] = whole[b * block : (b + 1) * block]
    ring.start()

    sums[...] = jnp.zeros_like(sums)

    @pl.loop(0, tokens // QB)
    def _(k):
        part_rows = dqkv_ref[pl.ds(pl.multiple_of(k * QB, QB), QB), :].astype(f32)
        sums[0:1, :] += jnp.sum(part_rows, axis=0, keepdims=True)

    for i, peer in enumerate((sib, nbr, diag)):
        vec_col(i, peer).wait_recv()
    total = vmine[...] + vall[sib] + vall[nbr] + vall[diag]
    vrow[r, 0:8, :] = total[0:8, :]
    vrow[r, 8:9, :] = dbin_ref[...]
    vrow[r, 9:10, :] = jnp.concatenate([sums[0:1, :], jnp.zeros((1, FEAT), f32)], axis=1)

    def vec_row(i):
        v = vrow.at[r]
        return remote(v, v, vr_s.at[i], vr_r.at[i], ((r + i) % rows, c))

    @pl.loop(1, rows)
    def _(i):
        vec_row(i).start()

    key[...] = rank_ref[0:1, :]
    to_col(key, col_g)

    def final(i, k):
        return remote(gsend.at[i, k], grecv.at[i, k], fin_s.at[i, k], fin_r.at[i, k], (r, nbr))

    def send_final(i, got):
        @pl.loop(0, chunks)
        def _(k):
            gsend[i, k] = placed(col_g[token_rows(nbr, k), :], got[0]).astype(bf16)
            final(i, k).start()

    def own_final(got, ref):
        @pl.loop(0, chunks)
        def _(k):
            ref[rows_of(k), half_lanes(h)] = placed(col_g[token_rows(c, k), :], got[0])

    def take_final(i, ref):
        @pl.loop(0, chunks)
        def _(k):
            final(i, k).wait_recv()
            ref[rows_of(k), half_lanes(1 - h)] = grecv[i, k].astype(f32)

    send_final(0, back_ref)
    if ring.hops > 1:
        ring.hop(1)
    own_final(back_ref, out_ref)

    def shared(k, i, q):
        v = grads.xin.at[0, q, rows_of(k)]
        return remote(v, v, sh_s.at[i, k], sh_r.at[i, k], (r, sib))

    def grad_rows(k):
        xcopy(k).wait_recv()
        for i, q in ours:
            total = keep[k, i, :, half_lanes(h)] + xr[k, i].astype(f32) + g1_ref[q, rows_of(k), half_lanes(h)].astype(f32)
            grads.xin[0, q, rows_of(k), :] = total.astype(bf16)
            shared(k, i, q).start()

    pl.loop(0, chunks)(grad_rows)

    @pl.loop(0, chunks)
    def _(k):
        for i, q in ours:
            shared(k, i, q).wait_recv()

    grads.pick_and_send(rank_ref[1:2, :])
    for t in range(2, ring.hops):
        ring.hop(t)
    total = ring.result()
    for i, ref in enumerate((gq_ref, gk_ref, gv_ref)):
        ref[...] = total[:, i * FEAT : (i + 1) * FEAT]
    go_ref[...] = total[:, 3 * FEAT :].T

    @pl.loop(1, rows)
    def _(i):
        vec_row(i).wait_recv()

    total = vrow[0]
    for i in range(1, rows):
        total = total + vrow[i]
    width, wide = D // (4 * rows), 4 * D // (4 * rows)
    spots = lax.broadcasted_iota(jnp.int32, (D, 128), 0)
    outs_at = lax.broadcasted_iota(jnp.int32, (D, 128), 1)

    def chosen(values, first, size):
        hot = jnp.where((spots - first == outs_at) & (outs_at < size), 1.0, 0.0)
        return lax.dot_general(values, hot, NN, precision=lax.Precision.HIGHEST, preferred_element_type=f32)

    gvec_ref[0:8, :] = chosen(total[0:8, :], (c * rows + r) * width, width)
    gwide_ref[0:1, :] = chosen(total[8:16, :], r * wide, wide)[0:1, :]
    gwide_ref[1:2, :] = chosen(total[8:16, :], r * width, width)[1:2, :]
    gwide_ref[2:3, :] = chosen(total[8:16, :], 2 * FEAT + r * width, width)[1:2, :]
    take_final(0, out_ref)

    grads.shared()
    send_final(1, grads.rbuf)
    own_final(grads.rbuf, grad_ref)
    take_final(1, grad_ref)

    grads.rows_sent()

    @pl.loop(0, chunks)
    def _(k):
        for i, q in ours:
            shared(k, i, q).wait_send()
            final(i, k).wait_send()
        d2d(k).wait_send()
        xcopy(k).wait_send()

    ring.finish()
    for i, peer in enumerate((sib, nbr, diag)):
        vec_col(i, peer).wait_send()

    @pl.loop(1, rows)
    def _(i):
        vec_row(i).wait_send()


def depart(rows, back, g1, dqkv, w_qkv, tok, rank, dwo, dvec, dbin):
    own_rows = tok.shape[1]
    tokens = 4 * own_rows
    chunks = own_rows // CH
    block, hops = D // rows, rows // 2
    S, V, DS = jax.ShapeDtypeStruct, pltpu.VMEM, pltpu.SemaphoreType.DMA
    third = S((block, FEAT), f32)
    return pl.pallas_call(
        functools.partial(depart_body, rows),
        out_shape=(
            S((own_rows, D), f32), S((own_rows, D), f32), third, third, third, S((FEAT, block), f32),
            S((8, 128), f32), S((8, 128), f32),
        ),
        in_specs=[VM] * 9,
        out_specs=(VM,) * 8,
        scratch_shapes=deal_scratch(rows, own_rows, 1)
        + deal_sems(rows, 1)
        + [V((1, tokens), f32), V((tokens, 1), f32), V((8, 3 * FEAT), f32), V((rows, block, 3 * FEAT), f32)]
        + [
            V((chunks, 2, CH, D), bf16), V((chunks, 2, CH, D), bf16), V((chunks, 2, CH, D), f32),
            V((chunks, 2, CH, HALF), bf16), V((chunks, 2, CH, HALF), bf16),
            V((2, chunks, CH, HALF), bf16), V((2, chunks, CH, HALF), bf16),
            V((2, hops, block, D), bf16), V((2, hops, block, D), bf16),
            V((16, D), f32), V((4, 16, D), f32), V((rows, 16, D), f32),
        ]
        + [DS((chunks,))] * 4
        + [DS((2, chunks))] * 2
        + [DS((2, hops))] * 2
        + [DS((2, chunks))] * 2
        + [DS((3,))] * 2
        + [DS((rows,))] * 2,
        name="depart",
        compiler_params=pltpu.CompilerParams(collective_id=3, has_side_effects=True, vmem_limit_bytes=60 << 20),
        cost_estimate=pl.CostEstimate(flops=60_000_000_000, bytes_accessed=20_000_000, transcendentals=0),
    )(back, g1, dqkv, w_qkv, tok, rank, dwo, dvec, dbin)


def per_device(
    inputs, cotangent, token_order, token_place, seq_lengths,
    query_weight, key_weight, value_weight, output_weight, inner_weight, outer_weight,
    query_bias, value_bias, output_bias, inner_bias, outer_bias,
    first_gain, first_shift, second_gain, second_shift,
):
    rows = lax.axis_size("row")
    own_rows = inputs.shape[0]
    tok_rows = 4 * own_rows

    pack = jnp.concatenate(
        [query_weight, key_weight, value_weight, output_weight.T, inner_weight, outer_weight.T], axis=1
    )
    pack = lax.all_gather(pack, "row", axis=0, tiled=True)
    w_qkv, wo, win, wout = pack[:, :576], pack[:, 576:768], pack[:, 768:1536], pack[:, 1536:]
    vin = jnp.concatenate(
        [query_bias, value_bias, output_bias, first_gain, first_shift, outer_bias, second_gain, second_shift, inner_bias]
    ).astype(f32)
    vin = jnp.broadcast_to(jnp.pad(vin, (0, HALF - vin.shape[0]))[None], (8, HALF))

    seq_ends = jnp.cumsum(seq_lengths[0])
    seq_starts = seq_ends - seq_lengths[0]
    positions = jnp.arange(tok_rows, dtype=jnp.int32)
    seg = jnp.sum((positions[:, None] >= seq_ends[None, :]).astype(jnp.int32), axis=1)
    hot = (seg[:, None] == jnp.arange(seq_ends.shape[0])[None, :]).astype(jnp.int32)
    start = jnp.sum(hot * seq_starts[None], axis=1)
    end = jnp.sum(hot * seq_ends[None], axis=1)
    lo = start[::QB] // KB
    hi = (end[QB - 1 :: QB] + KB - 1) // KB
    start, end = start[None], end[None]

    tok, own_tok, cot_own, cot_send, rank, vec, bqv, b_in = arrive(
        rows, inputs, cotangent, token_place[None], token_order[None], vin
    )
    cot_got = lax.ppermute(cot_send, "col", [(i, (i + 2) % 4) for i in range(4)])
    q, k, v, mixed, lse = attend_fwd(lo, hi, start, end, tok.reshape(tok_rows, D), w_qkv, bqv)
    back, g1, gmix, dwo, g_in, g_out, dvec, dbin = middle(
        rows, mixed.reshape(4, own_rows, FEAT), own_tok, cot_own, cot_got, wo, win, wout, vec, b_in, rank
    )
    dqkv = attend_bwd(lo, hi, start, end, q, k, v, gmix.reshape(tok_rows, FEAT), lse)
    output, input_grad, gq, gk, gv, go, gvec, gwide = depart(
        rows, back, g1, dqkv, w_qkv, tok, rank, dwo.reshape(rows, -1, FEAT), dvec, dbin
    )
    small, wide = query_bias.shape[0], inner_bias.shape[0]
    return (
        output, input_grad, gq, gk, gv, go, g_in, g_out,
        gwide[1, :small], gwide[2, :small], gvec[1, :small], gwide[0, :wide],
        gvec[2, :small], gvec[3, :small], gvec[4, :small], gvec[5, :small], gvec[6, :small],
    )


def solution(mesh):
    tok = P(("row", "col"), None)
    rc, cr, vec = P("row", "col"), P("col", "row"), P(("col", "row"))
    in_specs = (tok, tok, P("row"), P("row"), P("row", None), rc, rc, rc, cr, rc, cr) + (vec,) * 9
    out_specs = (tok, tok, rc, rc, rc, cr, rc, cr) + (vec,) * 9
    return jax.shard_map(per_device, mesh=mesh, in_specs=in_specs, out_specs=out_specs, check_vma=False)
```

```python
import functools

import jax
import jax.numpy as jnp
from jax import lax
from jax.experimental import pallas as pl
from jax.experimental.pallas import tpu as pltpu
from jax.sharding import PartitionSpec as P

D = 768
HD = 64
FEAT = 192
HEADS = 3
QB = 256
WINS = (384, 512, 640, 768, 1024, 1408)

norm_eps = 1e-12
root_half = 0.7071067811865476
inv_root_two_pi = 0.3989422804014327
NN = (((1,), (0,)), ((), ()))
NT = (((1,), (1,)), ((), ()))
TN = (((0,), (0,)), ((), ()))
MESH = pl.DeviceIdType.MESH
f32 = jnp.float32
bf16 = jnp.bfloat16
VM = pl.BlockSpec(memory_space=pltpu.VMEM)
SM = pl.BlockSpec(memory_space=pltpu.SMEM)
ANY = pl.BlockSpec(memory_space=pl.ANY)


def mm(a, b, dims):
    return lax.dot_general(a, b, dims, preferred_element_type=f32)


def lane_head(rows):
    return lax.broadcasted_iota(jnp.int32, (rows, FEAT), 1) // HD


def sequence_of(lens_ref, pos):
    start, end, run = jnp.zeros_like(pos), jnp.zeros_like(pos), 0
    for i in range(lens_ref.shape[1]):
        length = lens_ref[0, i]
        end = end + jnp.where(pos >= run, length, 0)
        run = run + length
        start = start + jnp.where(pos >= run, length, 0)
    return start, end


def for_window(lens_ref, qb, rows, body):
    first = sequence_of(lens_ref, qb * QB)[0] // 128 * 128
    span = sequence_of(lens_ref, qb * QB + QB - 1)[1] - first
    for less, win in zip((0,) + WINS, WINS):

        @pl.when((span > less) & (span <= win))
        def _():
            body(pl.multiple_of(jnp.minimum(first, rows - win), 128), win)


def attend_fwd_body(lens_ref, tok_ref, pack_ref, b_ref, q_ref, k_ref, v_ref, mix_ref, lse_ref, w_ref, sem):
    fetch = pltpu.make_async_copy(pack_ref, w_ref, sem.at[0])
    fetch.start()
    scale = HD ** (-0.5)
    total_rows = q_ref.shape[0]
    heads = lane_head(QB)
    lanes = lax.broadcasted_iota(jnp.int32, (QB, 128), 1)
    b_q, b_v = b_ref[0:1, :], b_ref[1:2, :]
    step = 2 * QB
    fetch.wait()

    @pl.loop(0, total_rows // step)
    def _(i):
        rows = pl.ds(pl.multiple_of(i * step, step), step)
        out = mm(tok_ref[rows, :], w_ref[:, : 3 * FEAT], NN)
        q_ref[rows, :] = (out[:, :FEAT] + b_q).astype(bf16)
        k_ref[rows, :] = out[:, FEAT : 2 * FEAT].astype(bf16)
        v_ref[rows, :] = (out[:, 2 * FEAT :] + b_v).astype(bf16)

    def by_head(parts):
        return jnp.where(heads == 0, parts[0], jnp.where(heads == 1, parts[1], parts[2]))

    @pl.loop(0, total_rows // QB)
    def _(qb):
        rows = pl.ds(pl.multiple_of(qb * QB, QB), QB)
        start, end = sequence_of(lens_ref, lax.broadcasted_iota(jnp.int32, (QB, 1), 0) + qb * QB)

        def window(at, win):
            qv = q_ref[rows, :] * scale
            kv, vv = k_ref[pl.ds(at, win), :], v_ref[pl.ds(at, win), :]
            pos = lax.broadcasted_iota(jnp.int32, (QB, win), 1) + at
            allowed = (pos >= start) & (pos < end)
            scores = [
                jnp.where(allowed, mm(jnp.where(heads == h, qv, jnp.zeros_like(qv)), kv, NT), -1e30)
                for h in range(HEADS)
            ]
            tops = [jnp.max(s, axis=1, keepdims=True) for s in scores]
            weights = [jnp.exp(scores[h] - tops[h]) for h in range(HEADS)]
            totals = [jnp.sum(e, axis=1, keepdims=True) for e in weights]
            mixed = by_head([mm(weights[h].astype(bf16), vv, NN) for h in range(HEADS)])
            mix_ref[rows, :] = (mixed / by_head(totals)).astype(bf16)
            lse = jnp.zeros((QB, 128), f32)
            for h in range(HEADS):
                lse = jnp.where(lanes == h, tops[h] + jnp.log(totals[h]), lse)
            lse_ref[:, rows] = lse.T[:8]

        for_window(lens_ref, qb, total_rows, window)


def attend_fwd(lens, tokens, pack, bias):
    rows = tokens.shape[0]
    part = jax.ShapeDtypeStruct((rows, FEAT), bf16)
    return pl.pallas_call(
        attend_fwd_body,
        out_shape=(part, part, part, part, jax.ShapeDtypeStruct((8, rows), f32)),
        in_specs=[SM, VM, ANY, VM],
        out_specs=(VM,) * 5,
        scratch_shapes=[pltpu.VMEM((D, D), bf16), pltpu.SemaphoreType.DMA((1,))],
        name="attend_fwd",
        compiler_params=pltpu.CompilerParams(vmem_limit_bytes=62 << 20),
        cost_estimate=pl.CostEstimate(flops=8_000_000_000, bytes_accessed=8_000_000, transcendentals=4_000_000),
    )(lens, tokens, pack, bias)


def attend_bwd_body(
    lens_ref, q_in, k_in, v_in, mix_in, lse_in, do_ref, dqkv_ref,
    k_ref, q_ref, v_ref, mix_ref, lse_ref, k_turned, dq_acc, dk_acc, dv_acc, fetch_sem,
):
    fetches = [
        pltpu.make_async_copy(src, dst, fetch_sem.at[i])
        for i, (src, dst) in enumerate(
            ((k_in, k_ref), (q_in, q_ref), (v_in, v_ref), (mix_in, mix_ref), (lse_in, lse_ref))
        )
    ]
    for fetch in fetches:
        fetch.start()
    scale = HD ** (-0.5)
    total_rows = q_ref.shape[0]
    blocks = total_rows // QB
    heads = lane_head(QB)
    dk_acc[...] = jnp.zeros_like(dk_acc)
    dv_acc[...] = jnp.zeros_like(dv_acc)
    fetches[0].wait()

    @pl.loop(0, blocks)
    def _(qb):
        rows = pl.ds(pl.multiple_of(qb * QB, QB), QB)
        k_turned[:, rows] = k_ref[rows, :].T

    for fetch in fetches[1:]:
        fetch.wait()

    @pl.loop(0, blocks)
    def _(qb):
        rows = pl.ds(pl.multiple_of(qb * QB, QB), QB)
        start, end = sequence_of(lens_ref, lax.broadcasted_iota(jnp.int32, (1, QB), 1) + qb * QB)

        def window(at, win):
            qv = q_ref[rows, :] * scale
            do = do_ref[rows, :]
            along = (do.astype(f32) * mix_ref[rows, :].astype(f32)).T
            keys = pl.ds(at, win)
            kv, vv = k_ref[keys, :], v_ref[keys, :]
            pos = lax.broadcasted_iota(jnp.int32, (win, QB), 0) + at
            allowed = (pos >= start) & (pos < end)
            each = range(HEADS)
            qs = [jnp.where(heads == h, qv, jnp.zeros_like(qv)) for h in each]
            dos = [jnp.where(heads == h, do, jnp.zeros_like(do)) for h in each]
            inner = [jnp.sum(along[h * HD : (h + 1) * HD], axis=0, keepdims=True) for h in each]
            scores = [mm(kv, qs[h], NT) for h in each]
            probs = [jnp.where(allowed, jnp.exp(scores[h] - lse_ref[h : h + 1, rows]), 0.0) for h in each]
            dps = [mm(vv, dos[h], NT) for h in each]
            lows = [p.astype(bf16) for p in probs]
            dss = [(probs[h] * (dps[h] - inner[h])).astype(bf16) for h in each]
            grad_v = sum([mm(lows[h], dos[h], NN) for h in each])
            grad_k = sum([mm(dss[h], qs[h], NN) for h in each])
            grad_q = [mm(k_turned[h * HD : (h + 1) * HD, keys], dss[h], NN) for h in each]
            dk_acc[keys, :] += grad_k
            dv_acc[keys, :] += grad_v
            dq_acc[rows, :] = jnp.concatenate(grad_q, axis=0).T

        for_window(lens_ref, qb, total_rows, window)

    @pl.loop(0, blocks)
    def _(qb):
        rows = pl.ds(pl.multiple_of(qb * QB, QB), QB)
        parts = [dq_acc[rows, :] * scale, dk_acc[rows, :], dv_acc[rows, :]]
        dqkv_ref[rows, :] = jnp.concatenate([p.astype(bf16) for p in parts], axis=1)


def attend_bwd(lens, q, k, v, mixed, do, lse):
    rows = q.shape[0]
    return pl.pallas_call(
        attend_bwd_body,
        out_shape=jax.ShapeDtypeStruct((rows, 3 * FEAT), bf16),
        in_specs=[SM] + [ANY] * 5 + [VM],
        out_specs=VM,
        scratch_shapes=[pltpu.VMEM((rows, FEAT), bf16)] * 4
        + [
            pltpu.VMEM((8, rows), f32),
            pltpu.VMEM((FEAT, rows), bf16),
            pltpu.VMEM((rows, FEAT), f32),
            pltpu.VMEM((rows, FEAT), f32),
            pltpu.VMEM((rows, FEAT), f32),
            pltpu.SemaphoreType.DMA((5,)),
        ],
        name="attend_bwd",
        compiler_params=pltpu.CompilerParams(vmem_limit_bytes=62 << 20),
        cost_estimate=pl.CostEstimate(flops=20_000_000_000, bytes_accessed=6_000_000, transcendentals=4_000_000),
    )(lens, q, k, v, mixed, lse, do)


def remote(src, dst, send_sem, recv_sem, device):
    return pltpu.make_async_remote_copy(
        src_ref=src, dst_ref=dst, send_sem=send_sem, recv_sem=recv_sem,
        device_id=device, device_id_type=MESH,
    )


def col_peers():
    r, c = lax.axis_index("row"), lax.axis_index("col")
    sib, nbr, diag = c + 1 - 2 * (c % 2), (c + 2) % 4, 3 - c
    return r, c, sib, nbr, diag


def norm_rows(x):
    mean = jnp.mean(x, axis=1, keepdims=True)
    center = x - mean
    var = jnp.mean(center * center, axis=1, keepdims=True)
    inv = lax.rsqrt(var + norm_eps)
    return center * inv, inv


def norm_back(grad, gain, hat, inv):
    e = grad * gain
    mean_e = jnp.mean(e, axis=1, keepdims=True)
    mean_c = jnp.mean(e * hat, axis=1, keepdims=True)
    return inv * (e - mean_e - hat * mean_c)


CH = 128


HALF = 384


def half_lanes(h):
    return pl.ds(pl.multiple_of(h * HALF, HALF), HALF)


def greet(peers, rows, row, c):
    barrier = pltpu.get_barrier_semaphore()
    for peer in peers:
        pl.semaphore_signal(barrier, inc=1, device_id=(row, peer), device_id_type=MESH)

    @pl.loop(1, rows)
    def _(i):
        pl.semaphore_signal(barrier, inc=1, device_id=((row + i) % rows, c), device_id_type=MESH)

    pl.semaphore_wait(barrier, len(peers) + rows - 1)


def to_col(src, dst):
    eye = lax.broadcasted_iota(jnp.int32, (128, 128), 0) == lax.broadcasted_iota(jnp.int32, (128, 128), 1)

    @pl.loop(0, dst.shape[0] // 128)
    def _(t):
        at = pl.ds(pl.multiple_of(t * 128, 128), 128)
        dst[at, :] = jnp.sum(jnp.where(eye, src[:, at], 0.0), axis=1, keepdims=True)


def rank_row(row_ref, col_ref):
    keys = row_ref[...]
    size = keys.shape[1]

    def step(t, acc):
        col = col_ref[pl.ds(pl.multiple_of(t * 128, 128), 128), :]
        less = jnp.where(col < keys, 1.0, 0.0)
        return acc + jnp.sum(less.reshape(16, 8, size), axis=0)

    acc = lax.fori_loop(0, size // 128, step, jnp.zeros((8, size), f32))
    return jnp.sum(acc, axis=0, keepdims=True)


def picker_rows(rank, first, count):
    want = (lax.broadcasted_iota(jnp.int32, (count, rank.shape[1]), 0) + first).astype(f32)
    return jnp.where(rank == want, 1.0, 0.0).astype(bf16)


def picker_cols(rank, count):
    have = lax.broadcasted_iota(jnp.int32, (rank.shape[0], count), 1).astype(f32)
    return jnp.where(rank == have, 1.0, 0.0).astype(bf16)


def ring_spot(row, rows):
    return jnp.where(row % 2 == 0, row // 2, rows - 1 - row // 2)


def ring_row(spot, rows):
    spot = (spot + rows) % rows
    return jnp.where(spot < rows // 2, 2 * spot, 2 * (rows - 1 - spot) + 1)


class RingGather:
    def __init__(self, rows, place, sems):
        self.rows, self.hops, self.place = rows, rows // 2, place
        self.send, self.recv = sems
        self.r, self.c = lax.axis_index("row"), lax.axis_index("col")
        self.spot = ring_spot(self.r, rows)

    def copy(self, way, t):
        step, to = (self.rows - t, 1) if way == 0 else (t, self.rows - 1)
        v = self.place(ring_row(self.spot + step, self.rows))
        return remote(v, v, self.send.at[way, t], self.recv.at[way, t], (ring_row(self.spot + to, self.rows), self.c))

    def start(self):
        for way in range(2):
            if self.hops > way:
                self.copy(way, 0).start()

    def hop(self, t):
        for way in range(2):
            if t < self.hops - way:
                self.copy(way, t - 1).wait_recv()
                self.copy(way, t).start()

    def done(self):
        for way in range(2):
            if self.hops > way:
                self.copy(way, self.hops - way - 1).wait_recv()

    def finish(self):
        for way in range(2):
            for t in range(self.hops - way):
                self.copy(way, t).wait_send()


def placed(rank_col, got):
    tokens = got.shape[0] * got.shape[1] * got.shape[2]
    return mm(picker_cols(rank_col, tokens), got.reshape(tokens, HALF), NN)


class Deal:
    def __init__(self, a, rows, bufs, sems):
        self.a, self.rows = a, rows
        self.xin, self.xout, self.sbuf, self.rbuf = bufs
        self.sib_s, self.sib_r, self.nbr_s, self.nbr_r, self.fwd_s, self.fwd_r, self.row_s, self.row_r, self.sh_s, self.sh_r = sems
        self.r, self.c, self.sib, self.nbr, self.diag = col_peers()
        self.h, self.core = self.c // 2, self.c % 2
        self.tokens = self.xin.shape[2] * 4
        self.slots = self.tokens // rows
        self.own_slots = self.slots // 2

    def to_sib(self):
        v = self.xin.at[self.a, self.c]
        return remote(v, v, self.sib_s.at[self.a], self.sib_r.at[self.a], (self.r, self.sib))

    def to_nbr(self):
        return remote(self.xout.at[self.a], self.xin.at[self.a, self.c], self.nbr_s.at[self.a], self.nbr_r.at[self.a], (self.r, self.nbr))

    def fwd(self):
        v = self.xin.at[self.a, self.nbr]
        return remote(v, v, self.fwd_s.at[self.a], self.fwd_r.at[self.a], (self.r, self.sib))

    def start_split(self):
        self.to_nbr().start()
        self.to_sib().start()

    def split(self, ref):
        self.xout[self.a] = ref[:, half_lanes(1 - self.h)].astype(bf16)
        self.to_nbr().start()
        self.xin[self.a, self.c] = ref[:, half_lanes(self.h)].astype(bf16)
        self.to_sib().start()

    def joined(self):
        self.to_nbr().wait_recv()
        self.fwd().start()
        self.to_sib().wait_recv()
        self.fwd().wait_recv()

    def row_copy(self, i):
        to = (self.r + i) % self.rows
        return remote(
            self.sbuf.at[self.a, i], self.rbuf.at[self.a, self.r, self.core],
            self.row_s.at[self.a, i], self.row_r.at[self.a, i], (to, self.c),
        )

    def share(self, i):
        v = self.rbuf.at[self.a, (self.r + self.rows - i) % self.rows, self.core]
        return remote(v, v, self.sh_s.at[self.a, i], self.sh_r.at[self.a, i], (self.r, self.sib))

    def pick_and_send(self, rank):
        source = self.xin[self.a].reshape(self.tokens, HALF)

        def picked(to):
            return mm(picker_rows(rank, to * self.slots + self.core * self.own_slots, self.own_slots), source, NN).astype(bf16)

        @pl.loop(1, self.rows)
        def _(i):
            self.sbuf[self.a, i] = picked((self.r + i) % self.rows)
            self.row_copy(i).start()

        self.rbuf[self.a, self.r, self.core] = picked(self.r)
        self.share(0).start()

    def shared(self):
        @pl.loop(1, self.rows)
        def _(i):
            self.row_copy(i).wait_recv()
            self.share(i).start()

        @pl.loop(0, self.rows)
        def _(i):
            self.share(i).wait_recv()

    def placed(self, rank_col):
        return placed(rank_col, self.rbuf[self.a])

    def joined_sent(self):
        self.to_sib().wait_send()
        self.to_nbr().wait_send()
        self.fwd().wait_send()

    def rows_sent(self):
        @pl.loop(1, self.rows)
        def _(i):
            self.row_copy(i).wait_send()

        @pl.loop(0, self.rows)
        def _(i):
            self.share(i).wait_send()


def deal_scratch(rows, own_rows, count):
    slots = 4 * own_rows // rows
    return [
        pltpu.VMEM((count, 4, own_rows, HALF), bf16),
        pltpu.VMEM((count, own_rows, HALF), bf16),
        pltpu.VMEM((count, rows, slots // 2, HALF), bf16),
        pltpu.VMEM((count, rows, 2, slots // 2, HALF), bf16),
    ]


def deal_sems(rows, count):
    return [pltpu.SemaphoreType.DMA((count,))] * 6 + [pltpu.SemaphoreType.DMA((count, rows))] * 4


def arrive_body(
    rows, x_ref, g_ref, place_ref, order_ref, vin_ref, part_ref,
    pack_ref, tok_ref, own_ref, cot_ref, cot_send, rank_ref, vec_ref, bqv_ref, bin_ref,
    *scratch,
):
    bufs, sems = scratch[:4], scratch[4:14]
    key_g, key_w, col_g, col_w, vbuf = scratch[14:19]
    an_s, an_r, as_s, as_r, af_s, af_r, vr_s, vr_r, vc_s, vc_r, w_s, w_r = scratch[19:]
    r, c, sib, nbr, diag = col_peers()
    h = c // 2
    own_rows = x_ref.shape[0]
    tokens = 4 * own_rows
    chunks = own_rows // CH
    greet((sib, nbr, diag), rows, r, c)

    first, second = Deal(0, rows, bufs, sems), Deal(1, rows, bufs, sems)
    first.split(x_ref)
    ring = RingGather(rows, lambda b: pack_ref.at[b], (w_s, w_r))
    pack_ref[r] = part_ref[...]
    ring.start()
    second.split(g_ref)

    def vec_row(i):
        v = vbuf.at[c, r]
        return remote(v, v, vr_s.at[i], vr_r.at[i], ((r + i) % rows, c))

    def vec_col(i, peer):
        v = vbuf.at[c]
        return remote(v, v, vc_s.at[i], vc_r.at[i], (r, peer))

    vbuf[c, r] = vin_ref[...]

    @pl.loop(1, rows)
    def _(i):
        vec_row(i).start()

    key_g[...] = place_ref[...].astype(f32)
    source = order_ref[...] // tokens
    key_w[...] = (source * tokens + lax.broadcasted_iota(jnp.int32, (1, tokens), 1)).astype(f32)
    to_col(key_g, col_g)
    to_col(key_w, col_w)
    rank_ref[0:1, :] = rank_row(key_g, col_g)
    if ring.hops > 1:
        ring.hop(1)
    rank_ref[1:2, :] = rank_row(key_w, col_w)
    rank_g = rank_ref[0:1, :]
    key_w[...] = rank_ref[1:2, :]
    to_col(key_w, col_w)
    for t in range(2, ring.hops):
        ring.hop(t)

    first.joined()
    first.pick_and_send(rank_g)

    @pl.loop(1, rows)
    def _(i):
        vec_row(i).wait_recv()

    for i, peer in enumerate((sib, nbr, diag)):
        vec_col(i, peer).start()

    second.joined()
    second.pick_and_send(rank_g)

    for i, peer in enumerate((sib, nbr, diag)):
        vec_col(i, peer).wait_recv()
    width, wide = D // (4 * rows), 4 * D // (4 * rows)
    lane = lax.broadcasted_iota(jnp.int32, (HALF, D), 0)
    feat = lax.broadcasted_iota(jnp.int32, (HALF, D), 1)
    everyone = vbuf[:, :, 0, :].reshape(4 * rows, HALF).astype(bf16)
    mine = vbuf[c][:, 0, :].astype(bf16)
    owner = lax.broadcasted_iota(jnp.int32, (4 * rows, D), 0) == lax.broadcasted_iota(jnp.int32, (4 * rows, D), 1) // width
    vec_ref[...] = jnp.zeros_like(vec_ref)
    for i in range(6):
        hot = jnp.where(lane - (i + 2) * width == feat % width, 1.0, 0.0).astype(bf16)
        vec_ref[i : i + 1, :] = jnp.sum(jnp.where(owner, mm(everyone, hot, NN), 0.0), axis=0, keepdims=True)
    row_owner = lax.broadcasted_iota(jnp.int32, (rows, D), 0)
    row_feat = lax.broadcasted_iota(jnp.int32, (rows, D), 1)
    hot = jnp.where(lane - 8 * width == feat % wide, 1.0, 0.0).astype(bf16)
    bin_ref[...] = jnp.sum(jnp.where(row_owner == row_feat // wide, mm(mine, hot, NN), 0.0), axis=0, keepdims=True)
    bqv_ref[...] = jnp.zeros_like(bqv_ref)
    for i in range(2):
        hot = jnp.where(lane - i * width == feat % width, 1.0, 0.0).astype(bf16)
        whole = jnp.sum(jnp.where(row_owner == row_feat // width, mm(mine, hot, NN), 0.0), axis=0, keepdims=True)
        bqv_ref[i : i + 1, :] = whole[:, :FEAT]

    def piece(q, k, half):
        return tok_ref.at[q, pl.ds(pl.multiple_of(k * CH, CH), CH), half_lanes(half)]

    def tok_copy(qi, q, k, half, s, rr, peer):
        v = piece(q, k, half)
        return remote(v, v, s.at[qi, k], rr.at[qi, k], (r, peer))

    ours = ((0, c), (1, nbr))
    first.shared()

    @pl.loop(0, chunks)
    def _(k):
        at = pl.ds(pl.multiple_of(k * CH, CH), CH)
        for qi, q in ours:
            rank = col_w[pl.ds(pl.multiple_of(q * own_rows + k * CH, CH), CH), :]
            tok_ref[q, at, half_lanes(h)] = first.placed(rank).astype(bf16)
            tok_copy(qi, q, k, h, an_s, an_r, nbr).start()
            tok_copy(qi, q, k, h, as_s, as_r, sib).start()

    def pass_on(k):
        for qi, q in ours:
            tok_copy(1 - qi, q, k, 1 - h, an_s, an_r, nbr).wait_recv()
            tok_copy(qi, q, k, 1 - h, af_s, af_r, sib).start()

    pl.loop(0, chunks // 2)(pass_on)
    second.shared()
    pl.loop(chunks // 2, chunks)(pass_on)
    for q, ref in ((nbr, cot_send), (c, cot_ref)):

        @pl.loop(0, chunks)
        def _(k):
            rank = col_w[pl.ds(pl.multiple_of(q * own_rows + k * CH, CH), CH), :]
            ref[pl.ds(pl.multiple_of(k * CH, CH), CH), :] = second.placed(rank).astype(bf16)

    @pl.loop(0, chunks)
    def _(k):
        for qi, q in ours:
            tok_copy(qi, q, k, h, as_s, as_r, sib).wait_recv()
            tok_copy(qi, q, k, 1 - h, af_s, af_r, sib).wait_recv()
            tok_copy(qi, q, k, h, an_s, an_r, nbr).wait_send()
            tok_copy(qi, q, k, h, as_s, as_r, sib).wait_send()
            tok_copy(qi, q, k, 1 - h, af_s, af_r, sib).wait_send()

    own_ref[...] = tok_ref[c]
    ring.done()
    ring.finish()

    for deal in (first, second):
        deal.joined_sent()
        deal.rows_sent()

    @pl.loop(1, rows)
    def _(i):
        vec_row(i).wait_send()

    for i, peer in enumerate((sib, nbr, diag)):
        vec_col(i, peer).wait_send()


def arrive(rows, x, g, place, order, vin, part):
    own_rows = x.shape[0]
    tokens = 4 * own_rows
    chunks = own_rows // CH
    S, V, DS = jax.ShapeDtypeStruct, pltpu.VMEM, pltpu.SemaphoreType.DMA
    return pl.pallas_call(
        functools.partial(arrive_body, rows),
        out_shape=(
            S((rows, D // rows, D), bf16), S((4, own_rows, D), bf16), S((own_rows, D), bf16),
            S((own_rows, HALF), bf16), S((own_rows, HALF), bf16), S((8, tokens), f32),
            S((8, D), f32), S((8, FEAT), f32), S((1, D), f32),
        ),
        in_specs=[VM] * 6,
        out_specs=(VM,) * 9,
        scratch_shapes=deal_scratch(rows, own_rows, 2)
        + deal_sems(rows, 2)
        + [
            V((1, tokens), f32), V((1, tokens), f32), V((tokens, 1), f32), V((tokens, 1), f32),
            V((4, rows, 8, HALF), f32),
        ]
        + [DS((2, chunks))] * 6
        + [DS((rows,))] * 2
        + [DS((3,))] * 2
        + [DS((2, rows // 2))] * 2,
        name="arrive",
        compiler_params=pltpu.CompilerParams(collective_id=1, has_side_effects=True, vmem_limit_bytes=62 << 20),
        cost_estimate=pl.CostEstimate(flops=60_000_000_000, bytes_accessed=20_000_000, transcendentals=0),
    )(x, g, place, order, vin, part)


class Ring:
    def __init__(self, rows, own, sbuf, rbuf, sems):
        self.rows, self.hops = rows, rows // 2
        self.own = own
        self.sbuf, self.rbuf = sbuf, rbuf
        self.send, self.recv = sems
        self.r, self.c = lax.axis_index("row"), lax.axis_index("col")
        self.spot = ring_spot(self.r, rows)

    def copy(self, way, t):
        to = ring_row(self.spot + (1 if way == 0 else self.rows - 1), self.rows)
        return remote(
            self.sbuf.at[way, t], self.rbuf.at[way, t], self.send.at[way, t], self.recv.at[way, t], (to, self.c)
        )

    def block(self, way, t):
        if way == 0:
            return ring_row(self.spot + self.hops - t, self.rows)
        return ring_row(self.spot + self.rows - (self.hops - 1) + t, self.rows)

    def start(self):
        for way in range(2 if self.hops > 1 else 1):
            self.sbuf[way, 0] = self.own(self.block(way, 0)).astype(bf16)
            self.copy(way, 0).start()

    def hop(self, t):
        for way in range(2):
            if t < self.hops - way:
                self.copy(way, t - 1).wait_recv()
                total = self.own(self.block(way, t)) + self.rbuf[way, t - 1].astype(f32)
                self.sbuf[way, t] = total.astype(bf16)
                self.copy(way, t).start()

    def result(self):
        self.copy(0, self.hops - 1).wait_recv()
        total = self.own(self.r) + self.rbuf[0, self.hops - 1].astype(f32)
        if self.hops > 1:
            self.copy(1, self.hops - 2).wait_recv()
            total = total + self.rbuf[1, self.hops - 2].astype(f32)
        return total

    def finish(self):
        for way in range(2):
            for t in range(self.hops - way):
                self.copy(way, t).wait_send()


def middle_body(
    rows, mixed_ref, tok_ref, cot_own, cot_got, pack_ref, ff_ref, vec_ref, bin_ref, rank_ref,
    back_ref, g1_ref, gmix_ref, dwo_ref, gin_ref, gout_ref, dvec_ref, dbin_ref,
    *scratch,
):
    nfull, hidden, slope, g2full, own, d2ds, d2dr, xs, xr, hat1, inv1, grad2, dwin, dwout = scratch[:14]
    wo_ref, attn_w, ff_all, wide, w_sem, wr_s, wr_r, xin, xout, sbuf, ring_out, ring_in = scratch[14:26]
    ds_s, ds_r, x_s, x_r, asib_s, asib_r, anbr_s, anbr_r, afwd_s, afwd_r, q_s, q_r = scratch[26:38]
    r, c, sib, nbr, diag = col_peers()
    h = c // 2
    chunks = tok_ref.shape[0] // CH
    block = D // rows
    fetch = pltpu.make_async_copy(pack_ref, attn_w, w_sem.at[0])
    fetch.start()
    greet((sib, nbr), rows, r, c)
    ff_ring = RingGather(rows, lambda b: ff_all.at[b], (wr_s, wr_r))
    ff_all[r] = ff_ref[...]
    ff_ring.start()
    fetch.wait()
    wo_ref[...] = attn_w[:, 3 * FEAT :]
    outs = Deal(0, rows, (xin, xout, sbuf, back_ref), scratch[38:])
    ring = Ring(rows, lambda b: jnp.concatenate([dwin[b], dwout[b]], axis=1), ring_out, ring_in, (q_s, q_r))

    bo, g1, s1, b2, g2, s2 = [vec_ref[pl.ds(i, 1), :] for i in range(6)]

    def win():
        return ff_all[:, :, :D].reshape(D, D) if block % 16 == 0 else attn_w[...]

    def wout():
        return ff_all[:, :, D:].reshape(D, D) if block % 16 == 0 else wide[...]

    def d2d(st, k):
        return remote(d2ds.at[k], d2dr.at[k], ds_s.at[st, k], ds_r.at[st, k], (r, sib))

    def xcopy(st, k):
        return remote(xs.at[k], xr.at[k], x_s.at[st, k], x_r.at[st, k], (r, nbr))

    def rs_start(st, k, part):
        if st > 0:
            d2d(st - 1, k).wait_send()
            xcopy(st - 1, k).wait_send()
        d2ds[k, 0] = part(sib).astype(bf16)
        d2ds[k, 1] = part(diag).astype(bf16)
        d2d(st, k).start()
        mine = part(c)
        other = part(nbr)
        d2d(st, k).wait_recv()
        xs[k] = (other + d2dr[k, 1].astype(f32)).astype(bf16)
        xcopy(st, k).start()
        own[k] = mine + d2dr[k, 0].astype(f32)

    def rs_end(st, k):
        xcopy(st, k).wait_recv()
        return own[k] + xr[k].astype(f32)

    gathered = (nfull, g2full, g1_ref)

    def piece(st, q, k):
        return gathered[st].at[q, pl.ds(pl.multiple_of(k * CH, CH), CH), :]

    def ag_copy(st, k, q, sems, target):
        return remote(piece(st, q, k), piece(st, q, k), sems[0].at[st, k], sems[1].at[st, k], (r, target))

    to_sib = functools.partial(ag_copy, sems=(asib_s, asib_r), target=sib)
    to_nbr = functools.partial(ag_copy, sems=(anbr_s, anbr_r), target=nbr)
    fwd = functools.partial(ag_copy, sems=(afwd_s, afwd_r), target=sib)

    def ag_start(st, k, value):
        gathered[st][c, pl.ds(pl.multiple_of(k * CH, CH), CH), :] = value
        to_nbr(st, k, c).start()
        to_sib(st, k, c).start()

    def ag_end(st, k):
        to_nbr(st, k, c).wait_recv()
        fwd(st, k, nbr).start()
        to_sib(st, k, c).wait_recv()
        fwd(st, k, nbr).wait_recv()

    def rows_of(k):
        return pl.ds(pl.multiple_of(k * CH, CH), CH)

    def all_rows(ref, k):
        return ref[:, rows_of(k), :].reshape(4 * CH, ref.shape[2])

    def ff_hops(part):
        for t in range(1 + part * (ff_ring.hops - 1) // 3, 1 + (part + 1) * (ff_ring.hops - 1) // 3):
            ff_ring.hop(t)

    def mix_heads(k):
        rs_start(0, k, lambda q: mm(mixed_ref[q, rows_of(k), :], wo_ref[...], NT))

    def first_norm(k):
        resid = rs_end(0, k) + tok_ref[rows_of(k), :].astype(f32) + bo
        hat, inv = norm_rows(resid)
        hat1[k] = hat
        inv1[k] = inv
        val = hat * g1 + s1
        ag_start(0, k, val.astype(bf16))

    pl.loop(0, chunks // 2)(mix_heads)
    ff_hops(0)
    pl.loop(chunks // 2, chunks)(mix_heads)
    ff_hops(1)
    pl.loop(0, chunks // 2)(first_norm)
    ff_hops(2)
    pl.loop(chunks // 2, chunks)(first_norm)
    ff_ring.done()
    if block % 16 != 0:
        for b in range(rows):
            attn_w[b * block : (b + 1) * block, :] = ff_all[b, :, :D]
            wide[b * block : (b + 1) * block, :] = ff_all[b, :, D:]

    @pl.loop(0, chunks)
    def _(k):
        ag_end(0, k)
        pre = mm(all_rows(nfull, k), win(), NN) + bin_ref[...]
        cum = 0.5 * (1.0 + lax.erf(pre * root_half))
        dens = jnp.exp(-0.5 * pre * pre) * inv_root_two_pi
        hidden[:, rows_of(k), :] = (pre * cum).astype(bf16).reshape(4, CH, D)
        slope[:, rows_of(k), :] = (cum + pre * dens).reshape(4, CH, D)
        rs_start(1, k, lambda q: mm(hidden[q, rows_of(k), :], wout(), NT))

    dvec_ref[...] = jnp.zeros_like(dvec_ref)

    @pl.loop(0, chunks)
    def _(k):
        resid = rs_end(1, k) + (hat1[k] * g1 + s1) + b2
        hat, inv = norm_rows(resid)
        low, high = [half.astype(bf16) for half in jnp.split(hat * g2 + s2, 2, axis=1)]
        xin[0, c, rows_of(k), :] = jnp.where(h == 0, low, high)
        xout[0, rows_of(k), :] = jnp.where(h == 0, high, low)
        halves = (cot_own[rows_of(k), :], cot_got[rows_of(k), :])
        low, high = jnp.where(h == 0, halves[0], halves[1]), jnp.where(h == 0, halves[1], halves[0])
        cot = jnp.concatenate([low, high], axis=1).astype(f32)
        grad = norm_back(cot, g2, hat, inv)
        grad2[k] = grad
        ag_start(1, k, grad.astype(bf16))
        dvec_ref[pl.ds(2, 1), :] += jnp.sum(grad, axis=0, keepdims=True)
        dvec_ref[pl.ds(5, 1), :] += jnp.sum(cot * hat, axis=0, keepdims=True)
        dvec_ref[pl.ds(6, 1), :] += jnp.sum(cot, axis=0, keepdims=True)

    outs.start_split()
    dwin[...] = jnp.zeros_like(dwin)
    dwout[...] = jnp.zeros_like(dwout)
    dwo_ref[...] = jnp.zeros_like(dwo_ref)
    dbin_ref[...] = jnp.zeros_like(dbin_ref)

    def add_blocks(ref, value):
        if block % 8 == 0:
            ref[...] += value.reshape(rows, block, D)
        else:
            for b in range(rows):
                ref[b] += value[b * block : (b + 1) * block]

    def back_hidden(k):
        ag_end(1, k)
        g2c = all_rows(g2full, k)
        grad_pre = mm(g2c, wout(), NN) * all_rows(slope, k)
        dbin_ref[...] += jnp.sum(grad_pre, axis=0, keepdims=True)
        low = grad_pre.astype(bf16)
        hid = all_rows(hidden, k)
        hidden[:, rows_of(k), :] = low.reshape(4, CH, D)
        rs_start(2, k, lambda q: mm(hidden[q, rows_of(k), :], win(), NT))
        add_blocks(dwout, mm(g2c, hid, TN))
        add_blocks(dwin, mm(all_rows(nfull, k), low, TN))

    pl.loop(0, chunks // 2)(back_hidden)
    outs.joined()
    outs.pick_and_send(rank_ref[1:2, :])
    pl.loop(chunks // 2, chunks)(back_hidden)
    ring.start()

    def hops(part):
        for t in range(1 + part * (ring.hops - 1) // 3, 1 + (part + 1) * (ring.hops - 1) // 3):
            ring.hop(t)

    def back_first(k):
        grad_normed = rs_end(2, k) + grad2[k]
        hat = hat1[k]
        grad = norm_back(grad_normed, g1, hat, inv1[k])
        ag_start(2, k, grad.astype(bf16))
        dvec_ref[pl.ds(1, 1), :] += jnp.sum(grad, axis=0, keepdims=True)
        dvec_ref[pl.ds(3, 1), :] += jnp.sum(grad_normed * hat, axis=0, keepdims=True)
        dvec_ref[pl.ds(4, 1), :] += jnp.sum(grad_normed, axis=0, keepdims=True)

    pl.loop(0, chunks // 2)(back_first)
    hops(0)
    pl.loop(chunks // 2, chunks)(back_first)
    hops(1)

    def back_mixed(k):
        ag_end(2, k)
        g1c = all_rows(g1_ref, k)
        gmix_ref[:, rows_of(k), :] = mm(g1c, wo_ref[...], NN).astype(bf16).reshape(4, CH, FEAT)
        dwo_ref[...] += mm(g1c, all_rows(mixed_ref, k), TN)

    pl.loop(0, chunks // 2)(back_mixed)
    hops(2)
    pl.loop(chunks // 2, chunks)(back_mixed)
    outs.shared()
    total = ring.result()
    gin_ref[...] = total[:, :D]
    gout_ref[...] = total[:, D:].T

    @pl.loop(0, chunks)
    def _(k):
        d2d(2, k).wait_send()
        xcopy(2, k).wait_send()
        for st in range(3):
            to_sib(st, k, c).wait_send()
            to_nbr(st, k, c).wait_send()
            fwd(st, k, nbr).wait_send()

    outs.joined_sent()
    outs.rows_sent()
    ring.finish()
    ff_ring.finish()


def middle(rows, mixed, tok, cot_own, cot_got, pack, ff_part, vec, b_in, rank):
    own_rows = tok.shape[0]
    chunks = own_rows // CH
    block, hops, slots = D // rows, rows // 2, 4 * own_rows // rows
    sem = pltpu.SemaphoreType.DMA((3, chunks))
    S, V = jax.ShapeDtypeStruct, pltpu.VMEM
    return pl.pallas_call(
        functools.partial(middle_body, rows),
        out_shape=(
            S((1, rows, 2, slots // 2, HALF), bf16),
            S((4, own_rows, D), bf16),
            S((4, own_rows, FEAT), bf16),
            S((D, FEAT), f32),
            S((block, D), f32),
            S((D, block), f32),
            S((8, D), f32),
            S((1, D), f32),
        ),
        in_specs=[VM] * 4 + [ANY] + [VM] * 4,
        out_specs=(VM,) * 8,
        scratch_shapes=[
            pltpu.VMEM((4, own_rows, D), bf16),
            pltpu.VMEM((4, own_rows, D), bf16),
            pltpu.VMEM((4, own_rows, D), f32),
            pltpu.VMEM((4, own_rows, D), bf16),
            pltpu.VMEM((chunks, CH, D), f32),
            pltpu.VMEM((chunks, 2, CH, D), bf16),
            pltpu.VMEM((chunks, 2, CH, D), bf16),
            pltpu.VMEM((chunks, CH, D), bf16),
            pltpu.VMEM((chunks, CH, D), bf16),
            pltpu.VMEM((chunks, CH, D), f32),
            pltpu.VMEM((chunks, CH, 1), f32),
            pltpu.VMEM((chunks, CH, D), f32),
            V((rows, block, D), f32),
            V((rows, block, D), f32),
            V((D, FEAT), bf16),
            V((D, D), bf16),
            V((rows, block, 2 * D), bf16),
            V((8, 128) if block % 16 == 0 else (D, D), bf16),
            pltpu.SemaphoreType.DMA((1,)),
            pltpu.SemaphoreType.DMA((2, hops)),
            pltpu.SemaphoreType.DMA((2, hops)),
        ]
        + deal_scratch(rows, own_rows, 1)[:3]
        + [V((2, hops, block, 2 * D), bf16)] * 2
        + [sem] * 10
        + [pltpu.SemaphoreType.DMA((2, hops))] * 2
        + deal_sems(rows, 1),
        name="middle",
        compiler_params=pltpu.CompilerParams(collective_id=2, has_side_effects=True, vmem_limit_bytes=62 << 20),
        cost_estimate=pl.CostEstimate(flops=80_000_000_000, bytes_accessed=20_000_000, transcendentals=4_000_000),
    )(mixed, tok, cot_own, cot_got, pack, ff_part, vec, b_in, rank)


def depart_body(
    rows, back_ref, g1_ref, dqkv_ref, pack_ref, tok_ref, rank_ref, dwo_ref, dvec_ref, dbin_ref,
    out_ref, grad_ref, gq_ref, gk_ref, gv_ref, go_ref, gvec_ref, gwide_ref,
    *scratch,
):
    bufs, sems = scratch[:4], scratch[4:14]
    key, col_g, sums, dw = scratch[14:18]
    d2ds, d2dr, keep, xs, xr, gsend, grecv, r2s, r2r, vmine, vall, vrow, w_ref, w_sem = scratch[18:32]
    ds_s, ds_r, x_s, x_r, fin_s, fin_r, q2_s, q2_r, sh_s, sh_r, vc_s, vc_r, vr_s, vr_r = scratch[32:]
    r, c, sib, nbr, diag = col_peers()
    h = c // 2
    own_rows = out_ref.shape[0]
    tokens = 4 * own_rows
    chunks = own_rows // CH
    block = D // rows
    fetch = pltpu.make_async_copy(pack_ref, w_ref, w_sem.at[0])
    fetch.start()
    greet((sib, nbr, diag), rows, r, c)
    fetch.wait()

    def rows_of(k):
        return pl.ds(pl.multiple_of(k * CH, CH), CH)

    def token_rows(q, k):
        return pl.ds(pl.multiple_of(q * own_rows + k * CH, CH), CH)

    grads = Deal(0, rows, bufs, sems)
    ring = Ring(rows, lambda b: jnp.concatenate([dw[b], dwo_ref[b]], axis=1), r2s, r2r, (q2_s, q2_r))
    ours = ((0, c), (1, nbr))

    vmine[...] = jnp.zeros_like(vmine)
    vmine[0:8, :] = dvec_ref[...]

    def vec_col(i, peer):
        return remote(vmine, vall.at[c], vc_s.at[i], vc_r.at[i], (r, peer))

    for i, peer in enumerate((sib, nbr, diag)):
        vec_col(i, peer).start()

    def d2d(k):
        return remote(d2ds.at[k], d2dr.at[k], ds_s.at[k], ds_r.at[k], (r, sib))

    def xcopy(k):
        return remote(xs.at[k], xr.at[k], x_s.at[k], x_r.at[k], (r, nbr))

    def part(q, k):
        return mm(dqkv_ref[token_rows(q, k), :], w_ref[:, : 3 * FEAT], NT)

    @pl.loop(0, chunks)
    def _(k):
        d2ds[k, 0] = part(sib, k).astype(bf16)
        d2ds[k, 1] = part(diag, k).astype(bf16)
        d2d(k).start()
        for i, q in ours:
            keep[k, i] = part(q, k)
        d2d(k).wait_recv()
        for i in range(2):
            keep[k, i] = keep[k, i] + d2dr[k, i].astype(f32)
            xs[k, 1 - i] = keep[k, i, :, half_lanes(1 - h)].astype(bf16)
        xcopy(k).start()

    whole = mm(tok_ref[...].reshape(tokens, D), dqkv_ref[...], TN)
    for b in range(rows):
        dw[b] = whole[b * block : (b + 1) * block]
    ring.start()

    sums[...] = jnp.zeros_like(sums)

    @pl.loop(0, tokens // QB)
    def _(k):
        part_rows = dqkv_ref[pl.ds(pl.multiple_of(k * QB, QB), QB), :].astype(f32)
        sums[0:1, :] += jnp.sum(part_rows, axis=0, keepdims=True)

    for i, peer in enumerate((sib, nbr, diag)):
        vec_col(i, peer).wait_recv()
    total = vmine[...] + vall[sib] + vall[nbr] + vall[diag]
    vrow[r, 0:8, :] = total[0:8, :]
    vrow[r, 8:9, :] = dbin_ref[...]
    vrow[r, 9:10, :] = jnp.concatenate([sums[0:1, :], jnp.zeros((1, FEAT), f32)], axis=1)

    def vec_row(i):
        v = vrow.at[r]
        return remote(v, v, vr_s.at[i], vr_r.at[i], ((r + i) % rows, c))

    @pl.loop(1, rows)
    def _(i):
        vec_row(i).start()

    key[...] = rank_ref[0:1, :]
    to_col(key, col_g)

    def final(i, k):
        return remote(gsend.at[i, k], grecv.at[i, k], fin_s.at[i, k], fin_r.at[i, k], (r, nbr))

    def send_final(i, got):
        @pl.loop(0, chunks)
        def _(k):
            gsend[i, k] = placed(col_g[token_rows(nbr, k), :], got[0]).astype(bf16)
            final(i, k).start()

    def own_final(got, ref):
        @pl.loop(0, chunks)
        def _(k):
            ref[rows_of(k), half_lanes(h)] = placed(col_g[token_rows(c, k), :], got[0]).astype(bf16)

    def take_final(i, ref):
        @pl.loop(0, chunks)
        def _(k):
            final(i, k).wait_recv()
            ref[rows_of(k), half_lanes(1 - h)] = grecv[i, k]

    send_final(0, back_ref)
    if ring.hops > 1:
        ring.hop(1)
    own_final(back_ref, out_ref)

    def shared(k, i, q):
        v = grads.xin.at[0, q, rows_of(k)]
        return remote(v, v, sh_s.at[i, k], sh_r.at[i, k], (r, sib))

    def grad_rows(k):
        xcopy(k).wait_recv()
        for i, q in ours:
            total = keep[k, i, :, half_lanes(h)] + xr[k, i].astype(f32) + g1_ref[q, rows_of(k), half_lanes(h)].astype(f32)
            grads.xin[0, q, rows_of(k), :] = total.astype(bf16)
            shared(k, i, q).start()

    pl.loop(0, chunks)(grad_rows)

    @pl.loop(0, chunks)
    def _(k):
        for i, q in ours:
            shared(k, i, q).wait_recv()

    grads.pick_and_send(rank_ref[1:2, :])
    for t in range(2, ring.hops):
        ring.hop(t)
    total = ring.result()
    for i, ref in enumerate((gq_ref, gk_ref, gv_ref)):
        ref[...] = total[:, i * FEAT : (i + 1) * FEAT]
    go_ref[...] = total[:, 3 * FEAT :].T

    @pl.loop(1, rows)
    def _(i):
        vec_row(i).wait_recv()

    total = vrow[0]
    for i in range(1, rows):
        total = total + vrow[i]
    width, wide = D // (4 * rows), 4 * D // (4 * rows)
    spots = lax.broadcasted_iota(jnp.int32, (D, 128), 0)
    outs_at = lax.broadcasted_iota(jnp.int32, (D, 128), 1)

    def chosen(values, first, size):
        hot = jnp.where((spots - first == outs_at) & (outs_at < size), 1.0, 0.0)
        return lax.dot_general(values, hot, NN, precision=lax.Precision.HIGHEST, preferred_element_type=f32)

    gvec_ref[0:8, :] = chosen(total[0:8, :], (c * rows + r) * width, width)
    gwide_ref[0:1, :] = chosen(total[8:16, :], r * wide, wide)[0:1, :]
    gwide_ref[1:2, :] = chosen(total[8:16, :], r * width, width)[1:2, :]
    gwide_ref[2:3, :] = chosen(total[8:16, :], 2 * FEAT + r * width, width)[1:2, :]
    take_final(0, out_ref)

    grads.shared()
    send_final(1, grads.rbuf)
    own_final(grads.rbuf, grad_ref)
    take_final(1, grad_ref)

    grads.rows_sent()

    @pl.loop(0, chunks)
    def _(k):
        for i, q in ours:
            shared(k, i, q).wait_send()
            final(i, k).wait_send()
        d2d(k).wait_send()
        xcopy(k).wait_send()

    ring.finish()
    for i, peer in enumerate((sib, nbr, diag)):
        vec_col(i, peer).wait_send()

    @pl.loop(1, rows)
    def _(i):
        vec_row(i).wait_send()


def depart(rows, back, g1, dqkv, pack, tok, rank, dwo, dvec, dbin):
    own_rows = tok.shape[1]
    tokens = 4 * own_rows
    chunks = own_rows // CH
    block, hops = D // rows, rows // 2
    S, V, DS = jax.ShapeDtypeStruct, pltpu.VMEM, pltpu.SemaphoreType.DMA
    third = S((block, FEAT), f32)
    return pl.pallas_call(
        functools.partial(depart_body, rows),
        out_shape=(
            S((own_rows, D), bf16), S((own_rows, D), bf16), third, third, third, S((FEAT, block), f32),
            S((8, 128), f32), S((8, 128), f32),
        ),
        in_specs=[VM] * 3 + [ANY] + [VM] * 5,
        out_specs=(VM,) * 8,
        scratch_shapes=deal_scratch(rows, own_rows, 1)
        + deal_sems(rows, 1)
        + [V((1, tokens), f32), V((tokens, 1), f32), V((8, 3 * FEAT), f32), V((rows, block, 3 * FEAT), f32)]
        + [
            V((chunks, 2, CH, D), bf16), V((chunks, 2, CH, D), bf16), V((chunks, 2, CH, D), f32),
            V((chunks, 2, CH, HALF), bf16), V((chunks, 2, CH, HALF), bf16),
            V((2, chunks, CH, HALF), bf16), V((2, chunks, CH, HALF), bf16),
            V((2, hops, block, D), bf16), V((2, hops, block, D), bf16),
            V((16, D), f32), V((4, 16, D), f32), V((rows, 16, D), f32), V((D, D), bf16), DS((1,)),
        ]
        + [DS((chunks,))] * 4
        + [DS((2, chunks))] * 2
        + [DS((2, hops))] * 2
        + [DS((2, chunks))] * 2
        + [DS((3,))] * 2
        + [DS((rows,))] * 2,
        name="depart",
        compiler_params=pltpu.CompilerParams(collective_id=3, has_side_effects=True, vmem_limit_bytes=62 << 20),
        cost_estimate=pl.CostEstimate(flops=60_000_000_000, bytes_accessed=20_000_000, transcendentals=0),
    )(back, g1, dqkv, pack, tok, rank, dwo, dvec, dbin)


def gather_up_body(*refs):
    weights, vectors, (attn_ref, ff_ref, vin_ref) = refs[:6], refs[6:-3], refs[-3:]
    q, k, v, o, inner, outer = weights
    attn_ref[...] = jnp.concatenate([q[...], k[...], v[...], o[...].T], axis=1)
    ff_ref[:, :D] = inner[...]
    ff_ref[:, D:] = outer[...].T
    parts = [ref[...].astype(f32) for ref in vectors]
    left = HALF - sum(part.shape[1] for part in parts)
    row = jnp.concatenate(parts + [jnp.zeros((1, left), f32)], axis=1)
    vin_ref[...] = jnp.broadcast_to(row, vin_ref.shape)


def gather_up(weights, vectors):
    S, block = jax.ShapeDtypeStruct, weights[0].shape[0]
    return pl.pallas_call(
        gather_up_body,
        out_shape=(S((block, D), bf16), S((block, 2 * D), bf16), S((8, HALF), f32)),
        in_specs=[VM] * (len(weights) + len(vectors)),
        out_specs=(VM, VM, VM),
        name="gather_up",
        compiler_params=pltpu.CompilerParams(vmem_limit_bytes=62 << 20),
    )(*weights, *(v[None] for v in vectors))


def hand_out_body(small, wide, *refs):
    arrays, (gvec_ref, gwide_ref) = refs[:8], refs[8:10]
    outs = refs[10:]
    for src, dst in zip(arrays, outs[:8]):
        dst[...] = src[...].astype(f32)
    q, v, o, inner, outer, gain1, shift1, gain2, shift2 = outs[8:]
    q[...] = gwide_ref[1:2, :small]
    v[...] = gwide_ref[2:3, :small]
    inner[...] = gwide_ref[0:1, :wide]
    for i, ref in enumerate((o, outer, gain1, shift1, gain2, shift2)):
        ref[...] = gvec_ref[i + 1 : i + 2, :small]


def hand_out(small, wide, arrays, gvec, gwide):
    S = jax.ShapeDtypeStruct
    one, four = S((1, small), f32), S((1, wide), f32)
    outs = pl.pallas_call(
        functools.partial(hand_out_body, small, wide),
        out_shape=tuple(S(a.shape, f32) for a in arrays) + (one, one, one, four) + (one,) * 5,
        in_specs=[VM] * 10,
        out_specs=(VM,) * 17,
        name="hand_out",
        compiler_params=pltpu.CompilerParams(vmem_limit_bytes=62 << 20),
    )(*arrays, gvec, gwide)
    return outs[:8] + tuple(v.reshape(-1) for v in outs[8:])


def per_device(
    inputs, cotangent, token_order, token_place, seq_lengths,
    query_weight, key_weight, value_weight, output_weight, inner_weight, outer_weight,
    query_bias, value_bias, output_bias, inner_bias, outer_bias,
    first_gain, first_shift, second_gain, second_shift,
):
    rows = lax.axis_size("row")
    own_rows = inputs.shape[0]
    tok_rows = 4 * own_rows

    attn_part, ff_part, vin = gather_up(
        (query_weight, key_weight, value_weight, output_weight, inner_weight, outer_weight),
        (
            query_bias, value_bias, output_bias, first_gain, first_shift, outer_bias, second_gain, second_shift,
            inner_bias,
        ),
    )
    pack, tok, own_tok, cot_own, cot_send, rank, vec, bqv, b_in = arrive(
        rows, inputs, cotangent, token_place[None], token_order[None], vin, attn_part
    )
    pack = pack.reshape(D, D)
    cot_got = lax.ppermute(cot_send, "col", [(i, (i + 2) % 4) for i in range(4)])
    q, k, v, mixed, lse = attend_fwd(seq_lengths, tok.reshape(tok_rows, D), pack, bqv)
    back, g1, gmix, dwo, g_in, g_out, dvec, dbin = middle(
        rows, mixed.reshape(4, own_rows, FEAT), own_tok, cot_own, cot_got, pack, ff_part, vec, b_in, rank
    )
    dqkv = attend_bwd(seq_lengths, q, k, v, mixed, gmix.reshape(tok_rows, FEAT), lse)
    output, input_grad, gq, gk, gv, go, gvec, gwide = depart(
        rows, back, g1, dqkv, pack, tok, rank, dwo.reshape(rows, -1, FEAT), dvec, dbin
    )
    return hand_out(
        query_bias.shape[0], inner_bias.shape[0], (output, input_grad, gq, gk, gv, go, g_in, g_out), gvec, gwide
    )


def solution(mesh):
    tok = P(("row", "col"), None)
    rc, cr, vec = P("row", "col"), P("col", "row"), P(("col", "row"))
    in_specs = (tok, tok, P("row"), P("row"), P("row", None), rc, rc, rc, cr, rc, cr) + (vec,) * 9
    out_specs = (tok, tok, rc, rc, rc, cr, rc, cr) + (vec,) * 9
    return jax.shard_map(per_device, mesh=mesh, in_specs=in_specs, out_specs=out_specs, check_vma=False)
```

```python
import functools

import jax
import jax.numpy as jnp
from jax import lax
from jax.experimental import pallas as pl
from jax.experimental.pallas import tpu as pltpu
from jax.sharding import PartitionSpec as P

D = 768
HD = 64
FEAT = 192
HEADS = 3
QB = 256
WINS = (384, 512, 640, 768, 1024, 1408)

norm_eps = 1e-12
root_half = 0.7071067811865476
inv_root_two_pi = 0.3989422804014327
NN = (((1,), (0,)), ((), ()))
NT = (((1,), (1,)), ((), ()))
TN = (((0,), (0,)), ((), ()))
MESH = pl.DeviceIdType.MESH
f32 = jnp.float32
bf16 = jnp.bfloat16
VM = pl.BlockSpec(memory_space=pltpu.VMEM)
SM = pl.BlockSpec(memory_space=pltpu.SMEM)
ANY = pl.BlockSpec(memory_space=pl.ANY)


def mm(a, b, dims):
    return lax.dot_general(a, b, dims, preferred_element_type=f32)


def lane_head(rows):
    return lax.broadcasted_iota(jnp.int32, (rows, FEAT), 1) // HD


def sequence_of(lens_ref, pos):
    start, end, run = jnp.zeros_like(pos), jnp.zeros_like(pos), 0
    for i in range(lens_ref.shape[1]):
        length = lens_ref[0, i]
        end = end + jnp.where(pos >= run, length, 0)
        run = run + length
        start = start + jnp.where(pos >= run, length, 0)
    return start, end


def for_window(lens_ref, qb, rows, body):
    first = sequence_of(lens_ref, qb * QB)[0] // 128 * 128
    span = sequence_of(lens_ref, qb * QB + QB - 1)[1] - first
    for less, win in zip((0,) + WINS, WINS):

        @pl.when((span > less) & (span <= win))
        def _():
            body(pl.multiple_of(jnp.minimum(first, rows - win), 128), win)


def attend_fwd_body(
    lens_ref, tok_in, pack_ref, b_ref, q_out, k_out, v_out, mix_ref, lse_ref, q_ref, k_ref, v_ref, tok_ref, w_ref, sem,
):
    step = 2 * QB
    steps = tok_ref.shape[0] // step
    fetch = pltpu.make_async_copy(pack_ref, w_ref, sem.at[0])
    fetch.start()

    def tokens(i):
        at = pl.ds(pl.multiple_of(i * step, step), step)
        return pltpu.make_async_copy(tok_in.at[at], tok_ref.at[at], sem.at[4 + i])

    pl.loop(0, steps)(lambda i: tokens(i).start())
    scale = HD ** (-0.5)
    total_rows = q_ref.shape[0]
    heads = lane_head(QB)
    lanes = lax.broadcasted_iota(jnp.int32, (QB, 128), 1)
    b_q, b_v = b_ref[0:1, :], b_ref[1:2, :]
    fetch.wait()

    @pl.loop(0, steps)
    def _(i):
        tokens(i).wait()
        rows = pl.ds(pl.multiple_of(i * step, step), step)
        out = mm(tok_ref[rows, :], w_ref[:, : 3 * FEAT], NN)
        q_ref[rows, :] = (out[:, :FEAT] + b_q).astype(bf16)
        k_ref[rows, :] = out[:, FEAT : 2 * FEAT].astype(bf16)
        v_ref[rows, :] = (out[:, 2 * FEAT :] + b_v).astype(bf16)

    leaving = [
        pltpu.make_async_copy(src, dst, sem.at[n + 1])
        for n, (src, dst) in enumerate(((q_ref, q_out), (k_ref, k_out), (v_ref, v_out)))
    ]
    for copy in leaving:
        copy.start()

    def by_head(parts):
        return jnp.where(heads == 0, parts[0], jnp.where(heads == 1, parts[1], parts[2]))

    @pl.loop(0, total_rows // QB)
    def _(qb):
        rows = pl.ds(pl.multiple_of(qb * QB, QB), QB)
        start, end = sequence_of(lens_ref, lax.broadcasted_iota(jnp.int32, (QB, 1), 0) + qb * QB)

        def window(at, win):
            qv = q_ref[rows, :] * scale
            kv, vv = k_ref[pl.ds(at, win), :], v_ref[pl.ds(at, win), :]
            pos = lax.broadcasted_iota(jnp.int32, (QB, win), 1) + at
            allowed = (pos >= start) & (pos < end)
            scores = [
                jnp.where(allowed, mm(jnp.where(heads == h, qv, jnp.zeros_like(qv)), kv, NT), -1e30)
                for h in range(HEADS)
            ]
            tops = [jnp.max(s, axis=1, keepdims=True) for s in scores]
            weights = [jnp.exp(scores[h] - tops[h]) for h in range(HEADS)]
            totals = [jnp.sum(e, axis=1, keepdims=True) for e in weights]
            mixed = by_head([mm(weights[h].astype(bf16), vv, NN) for h in range(HEADS)])
            mix_ref[rows, :] = (mixed / by_head(totals)).astype(bf16)
            lse = jnp.zeros((QB, 128), f32)
            for h in range(HEADS):
                lse = jnp.where(lanes == h, tops[h] + jnp.log(totals[h]), lse)
            lse_ref[:, rows] = lse.T[:8]

        for_window(lens_ref, qb, total_rows, window)

    for copy in leaving:
        copy.wait()


def attend_fwd(lens, tokens, pack, bias):
    rows = tokens.shape[0]
    part = jax.ShapeDtypeStruct((rows, FEAT), bf16)
    return pl.pallas_call(
        attend_fwd_body,
        out_shape=(part, part, part, part, jax.ShapeDtypeStruct((8, rows), f32)),
        in_specs=[SM, ANY, ANY, VM],
        out_specs=(ANY, ANY, ANY, VM, VM),
        scratch_shapes=[pltpu.VMEM((rows, FEAT), bf16)] * 3
        + [
            pltpu.VMEM((rows, D), bf16),
            pltpu.VMEM((D, D), bf16),
            pltpu.SemaphoreType.DMA((4 + rows // (2 * QB),)),
        ],
        name="attend_fwd",
        compiler_params=pltpu.CompilerParams(vmem_limit_bytes=62 << 20),
        cost_estimate=pl.CostEstimate(flops=8_000_000_000, bytes_accessed=8_000_000, transcendentals=4_000_000),
    )(lens, tokens, pack, bias)


def attend_bwd_body(
    lens_ref, q_in, k_in, v_in, mix_in, lse_in, do_ref, dqkv_ref,
    k_ref, q_ref, v_ref, mix_ref, lse_ref, k_turned, dq_acc, dk_acc, dv_acc, fetch_sem,
):
    fetches = [
        pltpu.make_async_copy(src, dst, fetch_sem.at[i])
        for i, (src, dst) in enumerate(
            ((k_in, k_ref), (q_in, q_ref), (v_in, v_ref), (mix_in, mix_ref), (lse_in, lse_ref))
        )
    ]
    for fetch in fetches:
        fetch.start()
    scale = HD ** (-0.5)
    total_rows = q_ref.shape[0]
    blocks = total_rows // QB
    heads = lane_head(QB)
    dk_acc[...] = jnp.zeros_like(dk_acc)
    dv_acc[...] = jnp.zeros_like(dv_acc)
    fetches[0].wait()

    @pl.loop(0, blocks)
    def _(qb):
        rows = pl.ds(pl.multiple_of(qb * QB, QB), QB)
        k_turned[:, rows] = k_ref[rows, :].T

    for fetch in fetches[1:]:
        fetch.wait()

    @pl.loop(0, blocks)
    def _(qb):
        rows = pl.ds(pl.multiple_of(qb * QB, QB), QB)
        start, end = sequence_of(lens_ref, lax.broadcasted_iota(jnp.int32, (1, QB), 1) + qb * QB)

        def window(at, win):
            qv = q_ref[rows, :] * scale
            do = do_ref[rows, :]
            along = (do.astype(f32) * mix_ref[rows, :].astype(f32)).T
            keys = pl.ds(at, win)
            kv, vv = k_ref[keys, :], v_ref[keys, :]
            pos = lax.broadcasted_iota(jnp.int32, (win, QB), 0) + at
            allowed = (pos >= start) & (pos < end)
            each = range(HEADS)
            qs = [jnp.where(heads == h, qv, jnp.zeros_like(qv)) for h in each]
            dos = [jnp.where(heads == h, do, jnp.zeros_like(do)) for h in each]
            inner = [jnp.sum(along[h * HD : (h + 1) * HD], axis=0, keepdims=True) for h in each]
            scores = [mm(kv, qs[h], NT) for h in each]
            probs = [jnp.where(allowed, jnp.exp(scores[h] - lse_ref[h : h + 1, rows]), 0.0) for h in each]
            dps = [mm(vv, dos[h], NT) for h in each]
            lows = [p.astype(bf16) for p in probs]
            dss = [(probs[h] * (dps[h] - inner[h])).astype(bf16) for h in each]
            grad_v = sum([mm(lows[h], dos[h], NN) for h in each])
            grad_k = sum([mm(dss[h], qs[h], NN) for h in each])
            grad_q = [mm(k_turned[h * HD : (h + 1) * HD, keys], dss[h], NN) for h in each]
            dk_acc[keys, :] += grad_k
            dv_acc[keys, :] += grad_v
            dq_acc[rows, :] = jnp.concatenate(grad_q, axis=0).T

        for_window(lens_ref, qb, total_rows, window)

    @pl.loop(0, blocks)
    def _(qb):
        rows = pl.ds(pl.multiple_of(qb * QB, QB), QB)
        parts = [dq_acc[rows, :] * scale, dk_acc[rows, :], dv_acc[rows, :]]
        dqkv_ref[rows, :] = jnp.concatenate([p.astype(bf16) for p in parts], axis=1)


def attend_bwd(lens, q, k, v, mixed, do, lse):
    rows = q.shape[0]
    return pl.pallas_call(
        attend_bwd_body,
        out_shape=jax.ShapeDtypeStruct((rows, 3 * FEAT), bf16),
        in_specs=[SM] + [ANY] * 5 + [VM],
        out_specs=VM,
        scratch_shapes=[pltpu.VMEM((rows, FEAT), bf16)] * 4
        + [
            pltpu.VMEM((8, rows), f32),
            pltpu.VMEM((FEAT, rows), bf16),
            pltpu.VMEM((rows, FEAT), f32),
            pltpu.VMEM((rows, FEAT), f32),
            pltpu.VMEM((rows, FEAT), f32),
            pltpu.SemaphoreType.DMA((5,)),
        ],
        name="attend_bwd",
        compiler_params=pltpu.CompilerParams(vmem_limit_bytes=62 << 20),
        cost_estimate=pl.CostEstimate(flops=20_000_000_000, bytes_accessed=6_000_000, transcendentals=4_000_000),
    )(lens, q, k, v, mixed, lse, do)


def remote(src, dst, send_sem, recv_sem, device):
    return pltpu.make_async_remote_copy(
        src_ref=src, dst_ref=dst, send_sem=send_sem, recv_sem=recv_sem,
        device_id=device, device_id_type=MESH,
    )


def col_peers():
    r, c = lax.axis_index("row"), lax.axis_index("col")
    sib, nbr, diag = c + 1 - 2 * (c % 2), (c + 2) % 4, 3 - c
    return r, c, sib, nbr, diag


def norm_rows(x):
    mean = jnp.mean(x, axis=1, keepdims=True)
    center = x - mean
    var = jnp.mean(center * center, axis=1, keepdims=True)
    inv = lax.rsqrt(var + norm_eps)
    return center * inv, inv


def norm_back(grad, gain, hat, inv):
    e = grad * gain
    mean_e = jnp.mean(e, axis=1, keepdims=True)
    mean_c = jnp.mean(e * hat, axis=1, keepdims=True)
    return inv * (e - mean_e - hat * mean_c)


CH = 128


HALF = 384


def half_lanes(h):
    return pl.ds(pl.multiple_of(h * HALF, HALF), HALF)


def greet(peers, rows, row, c):
    barrier = pltpu.get_barrier_semaphore()
    for peer in peers:
        pl.semaphore_signal(barrier, inc=1, device_id=(row, peer), device_id_type=MESH)

    @pl.loop(1, rows)
    def _(i):
        pl.semaphore_signal(barrier, inc=1, device_id=((row + i) % rows, c), device_id_type=MESH)

    pl.semaphore_wait(barrier, len(peers) + rows - 1)


def to_col(src, dst):
    eye = lax.broadcasted_iota(jnp.int32, (128, 128), 0) == lax.broadcasted_iota(jnp.int32, (128, 128), 1)

    @pl.loop(0, dst.shape[0] // 128)
    def _(t):
        at = pl.ds(pl.multiple_of(t * 128, 128), 128)
        dst[at, :] = jnp.sum(jnp.where(eye, src[:, at], 0.0), axis=1, keepdims=True)


def rank_row(row_ref, col_ref):
    keys = row_ref[...]
    size = keys.shape[1]

    def step(t, acc):
        col = col_ref[pl.ds(pl.multiple_of(t * 128, 128), 128), :]
        less = jnp.where(col < keys, 1.0, 0.0)
        return acc + jnp.sum(less.reshape(16, 8, size), axis=0)

    acc = lax.fori_loop(0, size // 128, step, jnp.zeros((8, size), f32))
    return jnp.sum(acc, axis=0, keepdims=True)


def picker_rows(rank, first, count):
    want = (lax.broadcasted_iota(jnp.int32, (count, rank.shape[1]), 0) + first).astype(f32)
    return jnp.where(rank == want, 1.0, 0.0).astype(bf16)


def picker_cols(rank, count):
    have = lax.broadcasted_iota(jnp.int32, (rank.shape[0], count), 1).astype(f32)
    return jnp.where(rank == have, 1.0, 0.0).astype(bf16)


def ring_spot(row, rows):
    return jnp.where(row % 2 == 0, row // 2, rows - 1 - row // 2)


def ring_row(spot, rows):
    spot = (spot + rows) % rows
    return jnp.where(spot < rows // 2, 2 * spot, 2 * (rows - 1 - spot) + 1)


class RingGather:
    def __init__(self, rows, place, sems):
        self.rows, self.hops, self.place = rows, rows // 2, place
        self.send, self.recv = sems
        self.r, self.c = lax.axis_index("row"), lax.axis_index("col")
        self.spot = ring_spot(self.r, rows)

    def copy(self, way, t):
        step, to = (self.rows - t, 1) if way == 0 else (t, self.rows - 1)
        v = self.place(ring_row(self.spot + step, self.rows))
        return remote(v, v, self.send.at[way, t], self.recv.at[way, t], (ring_row(self.spot + to, self.rows), self.c))

    def start(self):
        for way in range(2):
            if self.hops > way:
                self.copy(way, 0).start()

    def hop(self, t):
        for way in range(2):
            if t < self.hops - way:
                self.copy(way, t - 1).wait_recv()
                self.copy(way, t).start()

    def done(self):
        for way in range(2):
            if self.hops > way:
                self.copy(way, self.hops - way - 1).wait_recv()

    def finish(self):
        for way in range(2):
            for t in range(self.hops - way):
                self.copy(way, t).wait_send()


def placed(rank_col, got):
    tokens = got.shape[0] * got.shape[1] * got.shape[2]
    return mm(picker_cols(rank_col, tokens), got.reshape(tokens, HALF), NN)


class Deal:
    def __init__(self, a, rows, bufs, sems):
        self.a, self.rows = a, rows
        self.xin, self.xout, self.sbuf, self.rbuf = bufs
        self.sib_s, self.sib_r, self.nbr_s, self.nbr_r, self.fwd_s, self.fwd_r, self.row_s, self.row_r, self.sh_s, self.sh_r = sems
        self.r, self.c, self.sib, self.nbr, self.diag = col_peers()
        self.h, self.core = self.c // 2, self.c % 2
        self.tokens = self.xin.shape[2] * 4
        self.slots = self.tokens // rows
        self.own_slots = self.slots // 2

    def to_sib(self):
        v = self.xin.at[self.a, self.c]
        return remote(v, v, self.sib_s.at[self.a], self.sib_r.at[self.a], (self.r, self.sib))

    def to_nbr(self):
        return remote(self.xout.at[self.a], self.xin.at[self.a, self.c], self.nbr_s.at[self.a], self.nbr_r.at[self.a], (self.r, self.nbr))

    def fwd(self):
        v = self.xin.at[self.a, self.nbr]
        return remote(v, v, self.fwd_s.at[self.a], self.fwd_r.at[self.a], (self.r, self.sib))

    def start_split(self):
        self.to_nbr().start()
        self.to_sib().start()

    def split(self, ref):
        self.xout[self.a] = ref[:, half_lanes(1 - self.h)].astype(bf16)
        self.to_nbr().start()
        self.xin[self.a, self.c] = ref[:, half_lanes(self.h)].astype(bf16)
        self.to_sib().start()

    def joined(self):
        self.to_nbr().wait_recv()
        self.fwd().start()
        self.to_sib().wait_recv()
        self.fwd().wait_recv()

    def row_copy(self, i):
        to = (self.r + i) % self.rows
        return remote(
            self.sbuf.at[self.a, i], self.rbuf.at[self.a, self.r, self.core],
            self.row_s.at[self.a, i], self.row_r.at[self.a, i], (to, self.c),
        )

    def share(self, i):
        v = self.rbuf.at[self.a, (self.r + self.rows - i) % self.rows, self.core]
        return remote(v, v, self.sh_s.at[self.a, i], self.sh_r.at[self.a, i], (self.r, self.sib))

    def pick_and_send(self, rank):
        source = self.xin[self.a].reshape(self.tokens, HALF)

        def picked(to):
            return mm(picker_rows(rank, to * self.slots + self.core * self.own_slots, self.own_slots), source, NN).astype(bf16)

        @pl.loop(1, self.rows)
        def _(i):
            self.sbuf[self.a, i] = picked((self.r + i) % self.rows)
            self.row_copy(i).start()

        self.rbuf[self.a, self.r, self.core] = picked(self.r)
        self.share(0).start()

    def shared(self):
        @pl.loop(1, self.rows)
        def _(i):
            self.row_copy(i).wait_recv()
            self.share(i).start()

        @pl.loop(0, self.rows)
        def _(i):
            self.share(i).wait_recv()

    def placed(self, rank_col):
        return placed(rank_col, self.rbuf[self.a])

    def joined_sent(self):
        self.to_sib().wait_send()
        self.to_nbr().wait_send()
        self.fwd().wait_send()

    def rows_sent(self):
        @pl.loop(1, self.rows)
        def _(i):
            self.row_copy(i).wait_send()

        @pl.loop(0, self.rows)
        def _(i):
            self.share(i).wait_send()


def deal_scratch(rows, own_rows, count):
    slots = 4 * own_rows // rows
    return [
        pltpu.VMEM((count, 4, own_rows, HALF), bf16),
        pltpu.VMEM((count, own_rows, HALF), bf16),
        pltpu.VMEM((count, rows, slots // 2, HALF), bf16),
        pltpu.VMEM((count, rows, 2, slots // 2, HALF), bf16),
    ]


def deal_sems(rows, count):
    return [pltpu.SemaphoreType.DMA((count,))] * 6 + [pltpu.SemaphoreType.DMA((count, rows))] * 4


def arrive_body(
    rows, x_ref, g_ref, place_ref, order_ref, vin_ref, part_ref,
    pack_ref, tok_ref, own_ref, cot_ref, cot_send, rank_ref, vec_ref, bqv_ref, bin_ref,
    *scratch,
):
    bufs, sems = scratch[:4], scratch[4:14]
    key_g, key_w, col_g, col_w, vbuf = scratch[14:19]
    an_s, an_r, as_s, as_r, af_s, af_r, vr_s, vr_r, vc_s, vc_r, w_s, w_r = scratch[19:]
    r, c, sib, nbr, diag = col_peers()
    h = c // 2
    own_rows = x_ref.shape[0]
    tokens = 4 * own_rows
    chunks = own_rows // CH
    greet((sib, nbr, diag), rows, r, c)

    first, second = Deal(0, rows, bufs, sems), Deal(1, rows, bufs, sems)
    first.split(x_ref)
    ring = RingGather(rows, lambda b: pack_ref.at[b], (w_s, w_r))
    pack_ref[r] = part_ref[...]
    ring.start()
    second.split(g_ref)

    def vec_row(i):
        v = vbuf.at[c, r]
        return remote(v, v, vr_s.at[i], vr_r.at[i], ((r + i) % rows, c))

    def vec_col(i, peer):
        v = vbuf.at[c]
        return remote(v, v, vc_s.at[i], vc_r.at[i], (r, peer))

    vbuf[c, r] = vin_ref[...]

    @pl.loop(1, rows)
    def _(i):
        vec_row(i).start()

    key_g[...] = place_ref[...].astype(f32)
    source = order_ref[...] // tokens
    key_w[...] = (source * tokens + lax.broadcasted_iota(jnp.int32, (1, tokens), 1)).astype(f32)
    to_col(key_g, col_g)
    to_col(key_w, col_w)
    rank_ref[0:1, :] = rank_row(key_g, col_g)
    if ring.hops > 1:
        ring.hop(1)
    rank_ref[1:2, :] = rank_row(key_w, col_w)
    rank_g = rank_ref[0:1, :]
    key_w[...] = rank_ref[1:2, :]
    to_col(key_w, col_w)
    for t in range(2, ring.hops):
        ring.hop(t)

    first.joined()
    first.pick_and_send(rank_g)

    @pl.loop(1, rows)
    def _(i):
        vec_row(i).wait_recv()

    for i, peer in enumerate((sib, nbr, diag)):
        vec_col(i, peer).start()

    second.joined()
    second.pick_and_send(rank_g)

    for i, peer in enumerate((sib, nbr, diag)):
        vec_col(i, peer).wait_recv()
    width, wide = D // (4 * rows), 4 * D // (4 * rows)
    lane = lax.broadcasted_iota(jnp.int32, (HALF, D), 0)
    feat = lax.broadcasted_iota(jnp.int32, (HALF, D), 1)
    everyone = vbuf[:, :, 0, :].reshape(4 * rows, HALF).astype(bf16)
    mine = vbuf[c][:, 0, :].astype(bf16)
    owner = lax.broadcasted_iota(jnp.int32, (4 * rows, D), 0) == lax.broadcasted_iota(jnp.int32, (4 * rows, D), 1) // width
    vec_ref[...] = jnp.zeros_like(vec_ref)
    for i in range(6):
        hot = jnp.where(lane - (i + 2) * width == feat % width, 1.0, 0.0).astype(bf16)
        vec_ref[i : i + 1, :] = jnp.sum(jnp.where(owner, mm(everyone, hot, NN), 0.0), axis=0, keepdims=True)
    row_owner = lax.broadcasted_iota(jnp.int32, (rows, D), 0)
    row_feat = lax.broadcasted_iota(jnp.int32, (rows, D), 1)
    hot = jnp.where(lane - 8 * width == feat % wide, 1.0, 0.0).astype(bf16)
    bin_ref[...] = jnp.sum(jnp.where(row_owner == row_feat // wide, mm(mine, hot, NN), 0.0), axis=0, keepdims=True)
    bqv_ref[...] = jnp.zeros_like(bqv_ref)
    for i in range(2):
        hot = jnp.where(lane - i * width == feat % width, 1.0, 0.0).astype(bf16)
        whole = jnp.sum(jnp.where(row_owner == row_feat // width, mm(mine, hot, NN), 0.0), axis=0, keepdims=True)
        bqv_ref[i : i + 1, :] = whole[:, :FEAT]

    def piece(q, k, half):
        return tok_ref.at[q, pl.ds(pl.multiple_of(k * CH, CH), CH), half_lanes(half)]

    def tok_copy(qi, q, k, half, s, rr, peer):
        v = piece(q, k, half)
        return remote(v, v, s.at[qi, k], rr.at[qi, k], (r, peer))

    ours = ((0, c), (1, nbr))
    first.shared()

    @pl.loop(0, chunks)
    def _(k):
        at = pl.ds(pl.multiple_of(k * CH, CH), CH)
        for qi, q in ours:
            rank = col_w[pl.ds(pl.multiple_of(q * own_rows + k * CH, CH), CH), :]
            tok_ref[q, at, half_lanes(h)] = first.placed(rank).astype(bf16)
            tok_copy(qi, q, k, h, an_s, an_r, nbr).start()
            tok_copy(qi, q, k, h, as_s, as_r, sib).start()

    def pass_on(k):
        for qi, q in ours:
            tok_copy(1 - qi, q, k, 1 - h, an_s, an_r, nbr).wait_recv()
            tok_copy(qi, q, k, 1 - h, af_s, af_r, sib).start()

    pl.loop(0, chunks // 2)(pass_on)
    second.shared()
    pl.loop(chunks // 2, chunks)(pass_on)
    for q, ref in ((nbr, cot_send), (c, cot_ref)):

        @pl.loop(0, chunks)
        def _(k):
            rank = col_w[pl.ds(pl.multiple_of(q * own_rows + k * CH, CH), CH), :]
            ref[pl.ds(pl.multiple_of(k * CH, CH), CH), :] = second.placed(rank).astype(bf16)

    @pl.loop(0, chunks)
    def _(k):
        for qi, q in ours:
            tok_copy(qi, q, k, h, as_s, as_r, sib).wait_recv()
            tok_copy(qi, q, k, 1 - h, af_s, af_r, sib).wait_recv()
            tok_copy(qi, q, k, h, an_s, an_r, nbr).wait_send()
            tok_copy(qi, q, k, h, as_s, as_r, sib).wait_send()
            tok_copy(qi, q, k, 1 - h, af_s, af_r, sib).wait_send()

    own_ref[...] = tok_ref[c]
    ring.done()
    ring.finish()

    for deal in (first, second):
        deal.joined_sent()
        deal.rows_sent()

    @pl.loop(1, rows)
    def _(i):
        vec_row(i).wait_send()

    for i, peer in enumerate((sib, nbr, diag)):
        vec_col(i, peer).wait_send()


def arrive(rows, x, g, place, order, vin, part):
    own_rows = x.shape[0]
    tokens = 4 * own_rows
    chunks = own_rows // CH
    S, V, DS = jax.ShapeDtypeStruct, pltpu.VMEM, pltpu.SemaphoreType.DMA
    return pl.pallas_call(
        functools.partial(arrive_body, rows),
        out_shape=(
            S((rows, D // rows, D), bf16), S((4, own_rows, D), bf16), S((own_rows, D), bf16),
            S((own_rows, HALF), bf16), S((own_rows, HALF), bf16), S((8, tokens), f32),
            S((8, D), f32), S((8, FEAT), f32), S((1, D), f32),
        ),
        in_specs=[VM] * 6,
        out_specs=(VM,) * 9,
        scratch_shapes=deal_scratch(rows, own_rows, 2)
        + deal_sems(rows, 2)
        + [
            V((1, tokens), f32), V((1, tokens), f32), V((tokens, 1), f32), V((tokens, 1), f32),
            V((4, rows, 8, HALF), f32),
        ]
        + [DS((2, chunks))] * 6
        + [DS((rows,))] * 2
        + [DS((3,))] * 2
        + [DS((2, rows // 2))] * 2,
        name="arrive",
        compiler_params=pltpu.CompilerParams(collective_id=1, has_side_effects=True, vmem_limit_bytes=62 << 20),
        cost_estimate=pl.CostEstimate(flops=60_000_000_000, bytes_accessed=20_000_000, transcendentals=0),
    )(x, g, place, order, vin, part)


class Ring:
    def __init__(self, rows, own, sbuf, rbuf, sems):
        self.rows, self.hops = rows, rows // 2
        self.own = own
        self.sbuf, self.rbuf = sbuf, rbuf
        self.send, self.recv = sems
        self.r, self.c = lax.axis_index("row"), lax.axis_index("col")
        self.spot = ring_spot(self.r, rows)

    def copy(self, way, t):
        to = ring_row(self.spot + (1 if way == 0 else self.rows - 1), self.rows)
        return remote(
            self.sbuf.at[way, t], self.rbuf.at[way, t], self.send.at[way, t], self.recv.at[way, t], (to, self.c)
        )

    def block(self, way, t):
        if way == 0:
            return ring_row(self.spot + self.hops - t, self.rows)
        return ring_row(self.spot + self.rows - (self.hops - 1) + t, self.rows)

    def start(self):
        for way in range(2 if self.hops > 1 else 1):
            self.sbuf[way, 0] = self.own(self.block(way, 0)).astype(bf16)
            self.copy(way, 0).start()

    def hop(self, t):
        for way in range(2):
            if t < self.hops - way:
                self.copy(way, t - 1).wait_recv()
                total = self.own(self.block(way, t)) + self.rbuf[way, t - 1].astype(f32)
                self.sbuf[way, t] = total.astype(bf16)
                self.copy(way, t).start()

    def result(self):
        self.copy(0, self.hops - 1).wait_recv()
        total = self.own(self.r) + self.rbuf[0, self.hops - 1].astype(f32)
        if self.hops > 1:
            self.copy(1, self.hops - 2).wait_recv()
            total = total + self.rbuf[1, self.hops - 2].astype(f32)
        return total

    def finish(self):
        for way in range(2):
            for t in range(self.hops - way):
                self.copy(way, t).wait_send()


def middle_body(
    rows, mixed_ref, tok_ref, cot_own, cot_got, pack_ref, ff_ref, vec_ref, bin_ref, rank_ref,
    back_ref, g1_ref, gmix_ref, dwo_ref, gin_ref, gout_ref, dvec_ref, dbin_ref,
    *scratch,
):
    nfull, hidden, slope, g2full, own, d2ds, d2dr, xs, xr, hat1, inv1, grad2, dwin, dwout = scratch[:14]
    wo_ref, attn_w, ff_all, wide, w_sem, wr_s, wr_r, xin, xout, sbuf, ring_out, ring_in = scratch[14:26]
    ds_s, ds_r, x_s, x_r, asib_s, asib_r, anbr_s, anbr_r, afwd_s, afwd_r, q_s, q_r = scratch[26:38]
    r, c, sib, nbr, diag = col_peers()
    h = c // 2
    chunks = tok_ref.shape[0] // CH
    block = D // rows
    fetch = pltpu.make_async_copy(pack_ref, attn_w, w_sem.at[0])
    fetch.start()
    greet((sib, nbr), rows, r, c)
    ff_ring = RingGather(rows, lambda b: ff_all.at[b], (wr_s, wr_r))
    ff_all[r] = ff_ref[...]
    ff_ring.start()
    fetch.wait()
    wo_ref[...] = attn_w[:, 3 * FEAT :]
    outs = Deal(0, rows, (xin, xout, sbuf, back_ref), scratch[38:])
    ring = Ring(rows, lambda b: jnp.concatenate([dwin[b], dwout[b]], axis=1), ring_out, ring_in, (q_s, q_r))

    bo, g1, s1, b2, g2, s2 = [vec_ref[pl.ds(i, 1), :] for i in range(6)]

    def win():
        return ff_all[:, :, :D].reshape(D, D) if block % 16 == 0 else attn_w[...]

    def wout():
        return ff_all[:, :, D:].reshape(D, D) if block % 16 == 0 else wide[...]

    def d2d(st, k):
        return remote(d2ds.at[k], d2dr.at[k], ds_s.at[st, k], ds_r.at[st, k], (r, sib))

    def xcopy(st, k):
        return remote(xs.at[k], xr.at[k], x_s.at[st, k], x_r.at[st, k], (r, nbr))

    def rs_start(st, k, pair):
        if st > 0:
            d2d(st - 1, k).wait_send()
            xcopy(st - 1, k).wait_send()
        d2ds[k] = pair(sib, diag).astype(bf16).reshape(2, CH, D)
        d2d(st, k).start()
        both = pair(c, nbr)
        d2d(st, k).wait_recv()
        xs[k] = (both[CH:] + d2dr[k, 1].astype(f32)).astype(bf16)
        xcopy(st, k).start()
        own[k] = both[:CH] + d2dr[k, 0].astype(f32)

    def rs_end(st, k):
        xcopy(st, k).wait_recv()
        return own[k] + xr[k].astype(f32)

    gathered = (nfull, g2full, g1_ref)

    def piece(st, q, k):
        return gathered[st].at[q, pl.ds(pl.multiple_of(k * CH, CH), CH), :]

    def ag_copy(st, k, q, sems, target):
        return remote(piece(st, q, k), piece(st, q, k), sems[0].at[st, k], sems[1].at[st, k], (r, target))

    to_sib = functools.partial(ag_copy, sems=(asib_s, asib_r), target=sib)
    to_nbr = functools.partial(ag_copy, sems=(anbr_s, anbr_r), target=nbr)
    fwd = functools.partial(ag_copy, sems=(afwd_s, afwd_r), target=sib)

    def ag_start(st, k, value):
        gathered[st][c, pl.ds(pl.multiple_of(k * CH, CH), CH), :] = value
        to_nbr(st, k, c).start()
        to_sib(st, k, c).start()

    def ag_end(st, k):
        to_nbr(st, k, c).wait_recv()
        fwd(st, k, nbr).start()
        to_sib(st, k, c).wait_recv()
        fwd(st, k, nbr).wait_recv()

    def rows_of(k):
        return pl.ds(pl.multiple_of(k * CH, CH), CH)

    def two_rows(ref, p, q, k):
        return jnp.concatenate([ref[p, rows_of(k), :], ref[q, rows_of(k), :]], axis=0)

    def put_two(ref, p, q, k, value):
        ref[p, rows_of(k), :] = value[:CH]
        ref[q, rows_of(k), :] = value[CH:]

    def all_rows(ref, k):
        return ref[:, rows_of(k), :].reshape(4 * CH, ref.shape[2])

    def ff_hops(part):
        for t in range(1 + part * (ff_ring.hops - 1) // 3, 1 + (part + 1) * (ff_ring.hops - 1) // 3):
            ff_ring.hop(t)

    def mix_heads(k):
        rs_start(0, k, lambda p, q: mm(two_rows(mixed_ref, p, q, k), wo_ref[...], NT))

    def first_norm(k):
        resid = rs_end(0, k) + tok_ref[rows_of(k), :].astype(f32) + bo
        hat, inv = norm_rows(resid)
        hat1[k] = hat
        inv1[k] = inv
        val = hat * g1 + s1
        ag_start(0, k, val.astype(bf16))

    pl.loop(0, chunks // 2)(mix_heads)
    ff_hops(0)
    pl.loop(chunks // 2, chunks)(mix_heads)
    ff_hops(1)
    pl.loop(0, chunks // 2)(first_norm)
    ff_hops(2)
    pl.loop(chunks // 2, chunks)(first_norm)
    ff_ring.done()
    if block % 16 != 0:
        for b in range(rows):
            attn_w[b * block : (b + 1) * block, :] = ff_all[b, :, :D]
            wide[b * block : (b + 1) * block, :] = ff_all[b, :, D:]

    @pl.loop(0, chunks)
    def _(k):
        ag_end(0, k)

        def pair(p, q):
            pre = mm(two_rows(nfull, p, q, k), win(), NN) + bin_ref[...]
            cum = 0.5 * (1.0 + lax.erf(pre * root_half))
            dens = jnp.exp(-0.5 * pre * pre) * inv_root_two_pi
            low = (pre * cum).astype(bf16)
            put_two(hidden, p, q, k, low)
            put_two(slope, p, q, k, cum + pre * dens)
            return mm(low, wout(), NT)

        rs_start(1, k, pair)

    dvec_ref[...] = jnp.zeros_like(dvec_ref)

    @pl.loop(0, chunks)
    def _(k):
        resid = rs_end(1, k) + (hat1[k] * g1 + s1) + b2
        hat, inv = norm_rows(resid)
        low, high = [half.astype(bf16) for half in jnp.split(hat * g2 + s2, 2, axis=1)]
        xin[0, c, rows_of(k), :] = jnp.where(h == 0, low, high)
        xout[0, rows_of(k), :] = jnp.where(h == 0, high, low)
        halves = (cot_own[rows_of(k), :], cot_got[rows_of(k), :])
        low, high = jnp.where(h == 0, halves[0], halves[1]), jnp.where(h == 0, halves[1], halves[0])
        cot = jnp.concatenate([low, high], axis=1).astype(f32)
        grad = norm_back(cot, g2, hat, inv)
        grad2[k] = grad
        ag_start(1, k, grad.astype(bf16))
        dvec_ref[pl.ds(2, 1), :] += jnp.sum(grad, axis=0, keepdims=True)
        dvec_ref[pl.ds(5, 1), :] += jnp.sum(cot * hat, axis=0, keepdims=True)
        dvec_ref[pl.ds(6, 1), :] += jnp.sum(cot, axis=0, keepdims=True)

    outs.start_split()
    dwin[...] = jnp.zeros_like(dwin)
    dwout[...] = jnp.zeros_like(dwout)
    dwo_ref[...] = jnp.zeros_like(dwo_ref)
    dbin_ref[...] = jnp.zeros_like(dbin_ref)

    def add_blocks(ref, value):
        if block % 8 == 0:
            ref[...] += value.reshape(rows, block, D)
        else:
            for b in range(rows):
                ref[b] += value[b * block : (b + 1) * block]

    def back_hidden(k):
        ag_end(1, k)

        def pair(p, q):
            grad_pre = mm(two_rows(g2full, p, q, k), wout(), NN) * two_rows(slope, p, q, k)
            dbin_ref[...] += jnp.sum(grad_pre, axis=0, keepdims=True)
            low = grad_pre.astype(bf16)
            put_two(slope, p, q, k, low.astype(f32))
            return mm(low, win(), NT)

        rs_start(2, k, pair)
        add_blocks(dwout, mm(all_rows(g2full, k), all_rows(hidden, k), TN))
        add_blocks(dwin, mm(all_rows(nfull, k), all_rows(slope, k).astype(bf16), TN))

    pl.loop(0, chunks // 2)(back_hidden)
    outs.joined()
    outs.pick_and_send(rank_ref[1:2, :])
    pl.loop(chunks // 2, chunks)(back_hidden)
    ring.start()

    def hops(part):
        for t in range(1 + part * (ring.hops - 1) // 3, 1 + (part + 1) * (ring.hops - 1) // 3):
            ring.hop(t)

    def back_first(k):
        grad_normed = rs_end(2, k) + grad2[k]
        hat = hat1[k]
        grad = norm_back(grad_normed, g1, hat, inv1[k])
        ag_start(2, k, grad.astype(bf16))
        dvec_ref[pl.ds(1, 1), :] += jnp.sum(grad, axis=0, keepdims=True)
        dvec_ref[pl.ds(3, 1), :] += jnp.sum(grad_normed * hat, axis=0, keepdims=True)
        dvec_ref[pl.ds(4, 1), :] += jnp.sum(grad_normed, axis=0, keepdims=True)

    pl.loop(0, chunks // 2)(back_first)
    hops(0)
    pl.loop(chunks // 2, chunks)(back_first)
    hops(1)

    def back_mixed(k):
        ag_end(2, k)
        g1c = all_rows(g1_ref, k)
        gmix_ref[:, rows_of(k), :] = mm(g1c, wo_ref[...], NN).astype(bf16).reshape(4, CH, FEAT)
        dwo_ref[...] += mm(g1c, all_rows(mixed_ref, k), TN)

    pl.loop(0, chunks // 2)(back_mixed)
    hops(2)
    pl.loop(chunks // 2, chunks)(back_mixed)
    outs.shared()
    total = ring.result()
    gin_ref[...] = total[:, :D]
    gout_ref[...] = total[:, D:].T

    @pl.loop(0, chunks)
    def _(k):
        d2d(2, k).wait_send()
        xcopy(2, k).wait_send()
        for st in range(3):
            to_sib(st, k, c).wait_send()
            to_nbr(st, k, c).wait_send()
            fwd(st, k, nbr).wait_send()

    outs.joined_sent()
    outs.rows_sent()
    ring.finish()
    ff_ring.finish()


def middle(rows, mixed, tok, cot_own, cot_got, pack, ff_part, vec, b_in, rank):
    own_rows = tok.shape[0]
    chunks = own_rows // CH
    block, hops, slots = D // rows, rows // 2, 4 * own_rows // rows
    sem = pltpu.SemaphoreType.DMA((3, chunks))
    S, V = jax.ShapeDtypeStruct, pltpu.VMEM
    return pl.pallas_call(
        functools.partial(middle_body, rows),
        out_shape=(
            S((1, rows, 2, slots // 2, HALF), bf16),
            S((4, own_rows, D), bf16),
            S((4, own_rows, FEAT), bf16),
            S((D, FEAT), f32),
            S((block, D), f32),
            S((D, block), f32),
            S((8, D), f32),
            S((1, D), f32),
        ),
        in_specs=[VM] * 4 + [ANY] + [VM] * 4,
        out_specs=(VM,) * 8,
        scratch_shapes=[
            pltpu.VMEM((4, own_rows, D), bf16),
            pltpu.VMEM((4, own_rows, D), bf16),
            pltpu.VMEM((4, own_rows, D), f32),
            pltpu.VMEM((4, own_rows, D), bf16),
            pltpu.VMEM((chunks, CH, D), f32),
            pltpu.VMEM((chunks, 2, CH, D), bf16),
            pltpu.VMEM((chunks, 2, CH, D), bf16),
            pltpu.VMEM((chunks, CH, D), bf16),
            pltpu.VMEM((chunks, CH, D), bf16),
            pltpu.VMEM((chunks, CH, D), f32),
            pltpu.VMEM((chunks, CH, 1), f32),
            pltpu.VMEM((chunks, CH, D), f32),
            V((rows, block, D), f32),
            V((rows, block, D), f32),
            V((D, FEAT), bf16),
            V((D, D), bf16),
            V((rows, block, 2 * D), bf16),
            V((8, 128) if block % 16 == 0 else (D, D), bf16),
            pltpu.SemaphoreType.DMA((1,)),
            pltpu.SemaphoreType.DMA((2, hops)),
            pltpu.SemaphoreType.DMA((2, hops)),
        ]
        + deal_scratch(rows, own_rows, 1)[:3]
        + [V((2, hops, block, 2 * D), bf16)] * 2
        + [sem] * 10
        + [pltpu.SemaphoreType.DMA((2, hops))] * 2
        + deal_sems(rows, 1),
        name="middle",
        compiler_params=pltpu.CompilerParams(collective_id=2, has_side_effects=True, vmem_limit_bytes=62 << 20),
        cost_estimate=pl.CostEstimate(flops=80_000_000_000, bytes_accessed=20_000_000, transcendentals=4_000_000),
    )(mixed, tok, cot_own, cot_got, pack, ff_part, vec, b_in, rank)


def depart_body(
    rows, back_in, g1_in, dqkv_in, pack_in, tok_in, rank_ref, dwo_ref, dvec_ref, dbin_ref,
    out_ref, grad_ref, gq_ref, gk_ref, gv_ref, go_ref, gvec_ref, gwide_ref,
    *scratch,
):
    bufs, sems = scratch[:4], scratch[4:14]
    key, col_g, sums, dw = scratch[14:18]
    d2ds, d2dr, keep, xs, xr, gsend, grecv, r2s, r2r, vmine, vall, vrow, back_ref, g1_ref, dqkv_ref, w_ref, tok_ref, f_sem = scratch[18:36]
    ds_s, ds_r, x_s, x_r, fin_s, fin_r, q2_s, q2_r, sh_s, sh_r, vc_s, vc_r, vr_s, vr_r = scratch[36:]
    r, c, sib, nbr, diag = col_peers()
    h = c // 2
    own_rows = out_ref.shape[0]
    tokens = 4 * own_rows
    chunks = own_rows // CH
    block = D // rows
    pairs = ((dqkv_in, dqkv_ref), (pack_in, w_ref), (tok_in, tok_ref), (g1_in, g1_ref), (back_in, back_ref))
    fetches = [pltpu.make_async_copy(src, dst, f_sem.at[n]) for n, (src, dst) in enumerate(pairs)]
    for fetch in fetches:
        fetch.start()
    greet((sib, nbr, diag), rows, r, c)

    def rows_of(k):
        return pl.ds(pl.multiple_of(k * CH, CH), CH)

    def token_rows(q, k):
        return pl.ds(pl.multiple_of(q * own_rows + k * CH, CH), CH)

    grads = Deal(0, rows, bufs, sems)
    ring = Ring(rows, lambda b: jnp.concatenate([dw[b], dwo_ref[b]], axis=1), r2s, r2r, (q2_s, q2_r))
    ours = ((0, c), (1, nbr))

    vmine[...] = jnp.zeros_like(vmine)
    vmine[0:8, :] = dvec_ref[...]

    def vec_col(i, peer):
        return remote(vmine, vall.at[c], vc_s.at[i], vc_r.at[i], (r, peer))

    for i, peer in enumerate((sib, nbr, diag)):
        vec_col(i, peer).start()

    def d2d(k):
        return remote(d2ds.at[k], d2dr.at[k], ds_s.at[k], ds_r.at[k], (r, sib))

    def xcopy(k):
        return remote(xs.at[k], xr.at[k], x_s.at[k], x_r.at[k], (r, nbr))

    def part(q, k):
        return mm(dqkv_ref[token_rows(q, k), :], w_ref[:, : 3 * FEAT], NT)

    fetches[0].wait()
    fetches[1].wait()

    def send_parts(k):
        d2ds[k, 0] = part(sib, k).astype(bf16)
        d2ds[k, 1] = part(diag, k).astype(bf16)
        d2d(k).start()
        for i, q in ours:
            keep[k, i] = part(q, k)

    def combine(k):
        d2d(k).wait_recv()
        for i in range(2):
            keep[k, i] = keep[k, i] + d2dr[k, i].astype(f32)
            xs[k, 1 - i] = keep[k, i, :, half_lanes(1 - h)].astype(bf16)
        xcopy(k).start()

    pl.loop(0, chunks // 2)(send_parts)
    pl.loop(0, chunks // 2)(combine)
    fetches[2].wait()
    whole = mm(tok_ref[...].reshape(tokens, D), dqkv_ref[...], TN)
    for b in range(rows):
        dw[b] = whole[b * block : (b + 1) * block]
    ring.start()

    pl.loop(chunks // 2, chunks)(send_parts)
    pl.loop(chunks // 2, chunks)(combine)
    fetches[3].wait()
    if ring.hops > 1:
        ring.hop(1)

    def shared(k, i, q):
        v = grads.xin.at[0, q, rows_of(k)]
        return remote(v, v, sh_s.at[i, k], sh_r.at[i, k], (r, sib))

    def grad_rows(k):
        xcopy(k).wait_recv()
        for i, q in ours:
            total = keep[k, i, :, half_lanes(h)] + xr[k, i].astype(f32) + g1_ref[q, rows_of(k), half_lanes(h)].astype(f32)
            grads.xin[0, q, rows_of(k), :] = total.astype(bf16)
            shared(k, i, q).start()

    pl.loop(0, chunks // 2)(grad_rows)
    if ring.hops > 2:
        ring.hop(2)
    pl.loop(chunks // 2, chunks)(grad_rows)

    @pl.loop(0, chunks)
    def _(k):
        for i, q in ours:
            shared(k, i, q).wait_recv()

    grads.pick_and_send(rank_ref[1:2, :])
    if ring.hops > 3:
        ring.hop(3)

    sums[...] = jnp.zeros_like(sums)

    @pl.loop(0, tokens // QB)
    def _(k):
        part_rows = dqkv_ref[pl.ds(pl.multiple_of(k * QB, QB), QB), :].astype(f32)
        sums[0:1, :] += jnp.sum(part_rows, axis=0, keepdims=True)

    for i, peer in enumerate((sib, nbr, diag)):
        vec_col(i, peer).wait_recv()
    total = vmine[...] + vall[sib] + vall[nbr] + vall[diag]
    vrow[r, 0:8, :] = total[0:8, :]
    vrow[r, 8:9, :] = dbin_ref[...]
    vrow[r, 9:10, :] = jnp.concatenate([sums[0:1, :], jnp.zeros((1, FEAT), f32)], axis=1)

    def vec_row(i):
        v = vrow.at[r]
        return remote(v, v, vr_s.at[i], vr_r.at[i], ((r + i) % rows, c))

    @pl.loop(1, rows)
    def _(i):
        vec_row(i).start()

    key[...] = rank_ref[0:1, :]
    to_col(key, col_g)

    def final(i, k):
        return remote(gsend.at[i, k], grecv.at[i, k], fin_s.at[i, k], fin_r.at[i, k], (r, nbr))

    def send_final(i, got):
        @pl.loop(0, chunks)
        def _(k):
            gsend[i, k] = placed(col_g[token_rows(nbr, k), :], got[0]).astype(bf16)
            final(i, k).start()

    def own_final(got, ref):
        @pl.loop(0, chunks)
        def _(k):
            ref[rows_of(k), half_lanes(h)] = placed(col_g[token_rows(c, k), :], got[0]).astype(bf16)

    def take_final(i, ref):
        @pl.loop(0, chunks)
        def _(k):
            final(i, k).wait_recv()
            ref[rows_of(k), half_lanes(1 - h)] = grecv[i, k]

    fetches[4].wait()
    send_final(0, back_ref)
    own_final(back_ref, out_ref)
    @pl.loop(1, rows)
    def _(i):
        vec_row(i).wait_recv()

    total = vrow[0]
    for i in range(1, rows):
        total = total + vrow[i]
    width, wide = D // (4 * rows), 4 * D // (4 * rows)
    spots = lax.broadcasted_iota(jnp.int32, (D, 128), 0)
    outs_at = lax.broadcasted_iota(jnp.int32, (D, 128), 1)

    def chosen(values, first, size):
        hot = jnp.where((spots - first == outs_at) & (outs_at < size), 1.0, 0.0)
        return lax.dot_general(values, hot, NN, precision=lax.Precision.HIGHEST, preferred_element_type=f32)

    gvec_ref[0:8, :] = chosen(total[0:8, :], (c * rows + r) * width, width)
    gwide_ref[0:1, :] = chosen(total[8:16, :], r * wide, wide)[0:1, :]
    gwide_ref[1:2, :] = chosen(total[8:16, :], r * width, width)[1:2, :]
    gwide_ref[2:3, :] = chosen(total[8:16, :], 2 * FEAT + r * width, width)[1:2, :]
    take_final(0, out_ref)

    grads.shared()
    send_final(1, grads.rbuf)
    for t in range(4, ring.hops):
        ring.hop(t)
    total = ring.result()
    for i, ref in enumerate((gq_ref, gk_ref, gv_ref)):
        ref[...] = total[:, i * FEAT : (i + 1) * FEAT]
    go_ref[...] = total[:, 3 * FEAT :].T

    own_final(grads.rbuf, grad_ref)
    take_final(1, grad_ref)

    grads.rows_sent()

    @pl.loop(0, chunks)
    def _(k):
        for i, q in ours:
            shared(k, i, q).wait_send()
            final(i, k).wait_send()
        d2d(k).wait_send()
        xcopy(k).wait_send()

    ring.finish()
    for i, peer in enumerate((sib, nbr, diag)):
        vec_col(i, peer).wait_send()

    @pl.loop(1, rows)
    def _(i):
        vec_row(i).wait_send()


def depart(rows, back, g1, dqkv, pack, tok, rank, dwo, dvec, dbin):
    own_rows = tok.shape[1]
    tokens = 4 * own_rows
    chunks = own_rows // CH
    block, hops = D // rows, rows // 2
    S, V, DS = jax.ShapeDtypeStruct, pltpu.VMEM, pltpu.SemaphoreType.DMA
    third = S((block, FEAT), f32)
    return pl.pallas_call(
        functools.partial(depart_body, rows),
        out_shape=(
            S((own_rows, D), bf16), S((own_rows, D), bf16), third, third, third, S((FEAT, block), f32),
            S((8, 128), f32), S((8, 128), f32),
        ),
        in_specs=[ANY] * 5 + [VM] * 4,
        out_specs=(VM,) * 8,
        scratch_shapes=deal_scratch(rows, own_rows, 1)
        + deal_sems(rows, 1)
        + [V((1, tokens), f32), V((tokens, 1), f32), V((8, 3 * FEAT), f32), V((rows, block, 3 * FEAT), f32)]
        + [
            V((chunks, 2, CH, D), bf16), V((chunks, 2, CH, D), bf16), V((chunks, 2, CH, D), f32),
            V((chunks, 2, CH, HALF), bf16), V((chunks, 2, CH, HALF), bf16),
            V((2, chunks, CH, HALF), bf16), V((2, chunks, CH, HALF), bf16),
            V((2, hops, block, D), bf16), V((2, hops, block, D), bf16),
            V((16, D), f32), V((4, 16, D), f32), V((rows, 16, D), f32),
            V(back.shape, bf16), V(g1.shape, bf16), V(dqkv.shape, bf16), V((D, D), bf16), V(tok.shape, bf16), DS((5,)),
        ]
        + [DS((chunks,))] * 4
        + [DS((2, chunks))] * 2
        + [DS((2, hops))] * 2
        + [DS((2, chunks))] * 2
        + [DS((3,))] * 2
        + [DS((rows,))] * 2,
        name="depart",
        compiler_params=pltpu.CompilerParams(collective_id=3, has_side_effects=True, vmem_limit_bytes=62 << 20),
        cost_estimate=pl.CostEstimate(flops=60_000_000_000, bytes_accessed=20_000_000, transcendentals=0),
    )(back, g1, dqkv, pack, tok, rank, dwo, dvec, dbin)


def gather_up_body(*refs):
    weights, vectors, (attn_ref, ff_ref, vin_ref) = refs[:6], refs[6:-3], refs[-3:]
    q, k, v, o, inner, outer = weights
    attn_ref[...] = jnp.concatenate([q[...], k[...], v[...], o[...].T], axis=1)
    ff_ref[:, :D] = inner[...]
    ff_ref[:, D:] = outer[...].T
    parts = [ref[...].astype(f32) for ref in vectors]
    left = HALF - sum(part.shape[1] for part in parts)
    row = jnp.concatenate(parts + [jnp.zeros((1, left), f32)], axis=1)
    vin_ref[...] = jnp.broadcast_to(row, vin_ref.shape)


def gather_up(weights, vectors):
    S, block = jax.ShapeDtypeStruct, weights[0].shape[0]
    return pl.pallas_call(
        gather_up_body,
        out_shape=(S((block, D), bf16), S((block, 2 * D), bf16), S((8, HALF), f32)),
        in_specs=[VM] * (len(weights) + len(vectors)),
        out_specs=(VM, VM, VM),
        name="gather_up",
        compiler_params=pltpu.CompilerParams(vmem_limit_bytes=62 << 20),
    )(*weights, *(v[None] for v in vectors))


def hand_out_body(small, wide, *refs):
    arrays, (gvec_ref, gwide_ref) = refs[:8], refs[8:10]
    outs = refs[10:]
    for src, dst in zip(arrays, outs[:8]):
        dst[...] = src[...].astype(f32)
    q, v, o, inner, outer, gain1, shift1, gain2, shift2 = outs[8:]
    q[...] = gwide_ref[1:2, :small]
    v[...] = gwide_ref[2:3, :small]
    inner[...] = gwide_ref[0:1, :wide]
    for i, ref in enumerate((o, outer, gain1, shift1, gain2, shift2)):
        ref[...] = gvec_ref[i + 1 : i + 2, :small]


def hand_out(small, wide, arrays, gvec, gwide):
    S = jax.ShapeDtypeStruct
    one, four = S((1, small), f32), S((1, wide), f32)
    outs = pl.pallas_call(
        functools.partial(hand_out_body, small, wide),
        out_shape=tuple(S(a.shape, f32) for a in arrays) + (one, one, one, four) + (one,) * 5,
        in_specs=[VM] * 10,
        out_specs=(VM,) * 17,
        name="hand_out",
        compiler_params=pltpu.CompilerParams(vmem_limit_bytes=62 << 20),
    )(*arrays, gvec, gwide)
    return outs[:8] + tuple(v.reshape(-1) for v in outs[8:])


def per_device(
    inputs, cotangent, token_order, token_place, seq_lengths,
    query_weight, key_weight, value_weight, output_weight, inner_weight, outer_weight,
    query_bias, value_bias, output_bias, inner_bias, outer_bias,
    first_gain, first_shift, second_gain, second_shift,
):
    rows = lax.axis_size("row")
    own_rows = inputs.shape[0]
    tok_rows = 4 * own_rows

    attn_part, ff_part, vin = gather_up(
        (query_weight, key_weight, value_weight, output_weight, inner_weight, outer_weight),
        (
            query_bias, value_bias, output_bias, first_gain, first_shift, outer_bias, second_gain, second_shift,
            inner_bias,
        ),
    )
    pack, tok, own_tok, cot_own, cot_send, rank, vec, bqv, b_in = arrive(
        rows, inputs, cotangent, token_place[None], token_order[None], vin, attn_part
    )
    pack = pack.reshape(D, D)
    cot_got = lax.ppermute(cot_send, "col", [(i, (i + 2) % 4) for i in range(4)])
    q, k, v, mixed, lse = attend_fwd(seq_lengths, tok.reshape(tok_rows, D), pack, bqv)
    back, g1, gmix, dwo, g_in, g_out, dvec, dbin = middle(
        rows, mixed.reshape(4, own_rows, FEAT), own_tok, cot_own, cot_got, pack, ff_part, vec, b_in, rank
    )
    dqkv = attend_bwd(seq_lengths, q, k, v, mixed, gmix.reshape(tok_rows, FEAT), lse)
    output, input_grad, gq, gk, gv, go, gvec, gwide = depart(
        rows, back, g1, dqkv, pack, tok, rank, dwo.reshape(rows, -1, FEAT), dvec, dbin
    )
    return hand_out(
        query_bias.shape[0], inner_bias.shape[0], (output, input_grad, gq, gk, gv, go, g_in, g_out), gvec, gwide
    )


def solution(mesh):
    tok = P(("row", "col"), None)
    rc, cr, vec = P("row", "col"), P("col", "row"), P(("col", "row"))
    in_specs = (tok, tok, P("row"), P("row"), P("row", None), rc, rc, rc, cr, rc, cr) + (vec,) * 9
    out_specs = (tok, tok, rc, rc, rc, cr, rc, cr) + (vec,) * 9
    return jax.shard_map(per_device, mesh=mesh, in_specs=in_specs, out_specs=out_specs, check_vma=False)
```

```python
import functools

import jax
import jax.numpy as jnp
from jax import lax
from jax.experimental import pallas as pl
from jax.experimental.pallas import tpu as pltpu
from jax.sharding import PartitionSpec as P

D = 768
HD = 64
FEAT = 192
HEADS = 3
QB = 256
WINS = (384, 512, 640, 768, 1024, 1408)

norm_eps = 1e-12
root_half = 0.7071067811865476
inv_root_two_pi = 0.3989422804014327
NN = (((1,), (0,)), ((), ()))
NT = (((1,), (1,)), ((), ()))
TN = (((0,), (0,)), ((), ()))
MESH = pl.DeviceIdType.MESH
f32 = jnp.float32
bf16 = jnp.bfloat16
VM = pl.BlockSpec(memory_space=pltpu.VMEM)
SM = pl.BlockSpec(memory_space=pltpu.SMEM)
ANY = pl.BlockSpec(memory_space=pl.ANY)


def mm(a, b, dims):
    return lax.dot_general(a, b, dims, preferred_element_type=f32)


def lane_head(rows):
    return lax.broadcasted_iota(jnp.int32, (rows, FEAT), 1) // HD


def sequence_of(lens_ref, pos):
    start, end, run = jnp.zeros_like(pos), jnp.zeros_like(pos), 0
    for i in range(lens_ref.shape[1]):
        length = lens_ref[0, i]
        end = end + jnp.where(pos >= run, length, 0)
        run = run + length
        start = start + jnp.where(pos >= run, length, 0)
    return start, end


def for_window(lens_ref, qb, rows, body):
    first = sequence_of(lens_ref, qb * QB)[0] // 128 * 128
    span = sequence_of(lens_ref, qb * QB + QB - 1)[1] - first
    for less, win in zip((0,) + WINS, WINS):

        @pl.when((span > less) & (span <= win))
        def _():
            body(pl.multiple_of(jnp.minimum(first, rows - win), 128), win)


def attend_fwd_body(
    lens_ref, tok_in, pack_ref, b_ref, q_out, k_out, v_out, mix_ref, lse_ref, q_ref, k_ref, v_ref, tok_ref, w_ref, sem,
):
    step = 2 * QB
    steps = tok_ref.shape[0] // step
    fetch = pltpu.make_async_copy(pack_ref, w_ref, sem.at[0])
    fetch.start()

    def tokens(i):
        at = pl.ds(pl.multiple_of(i * step, step), step)
        return pltpu.make_async_copy(tok_in.at[at], tok_ref.at[at], sem.at[4 + i])

    pl.loop(0, steps)(lambda i: tokens(i).start())
    scale = HD ** (-0.5)
    total_rows = q_ref.shape[0]
    heads = lane_head(QB)
    lanes = lax.broadcasted_iota(jnp.int32, (QB, 128), 1)
    b_q, b_v = b_ref[0:1, :], b_ref[1:2, :]
    fetch.wait()

    @pl.loop(0, steps)
    def _(i):
        tokens(i).wait()
        rows = pl.ds(pl.multiple_of(i * step, step), step)
        out = mm(tok_ref[rows, :], w_ref[:, : 3 * FEAT], NN)
        q_ref[rows, :] = (out[:, :FEAT] + b_q).astype(bf16)
        k_ref[rows, :] = out[:, FEAT : 2 * FEAT].astype(bf16)
        v_ref[rows, :] = (out[:, 2 * FEAT :] + b_v).astype(bf16)

    leaving = [
        pltpu.make_async_copy(src, dst, sem.at[n + 1])
        for n, (src, dst) in enumerate(((q_ref, q_out), (k_ref, k_out), (v_ref, v_out)))
    ]
    for copy in leaving:
        copy.start()

    def by_head(parts):
        return jnp.where(heads == 0, parts[0], jnp.where(heads == 1, parts[1], parts[2]))

    @pl.loop(0, total_rows // QB)
    def _(qb):
        rows = pl.ds(pl.multiple_of(qb * QB, QB), QB)
        start, end = sequence_of(lens_ref, lax.broadcasted_iota(jnp.int32, (QB, 1), 0) + qb * QB)

        def window(at, win):
            qv = q_ref[rows, :] * scale
            kv, vv = k_ref[pl.ds(at, win), :], v_ref[pl.ds(at, win), :]
            pos = lax.broadcasted_iota(jnp.int32, (QB, win), 1) + at
            allowed = (pos >= start) & (pos < end)
            scores = [
                jnp.where(allowed, mm(jnp.where(heads == h, qv, jnp.zeros_like(qv)), kv, NT), -1e30)
                for h in range(HEADS)
            ]
            tops = [jnp.max(s, axis=1, keepdims=True) for s in scores]
            weights = [jnp.exp(scores[h] - tops[h]) for h in range(HEADS)]
            totals = [jnp.sum(e, axis=1, keepdims=True) for e in weights]
            mixed = by_head([mm(weights[h].astype(bf16), vv, NN) for h in range(HEADS)])
            mix_ref[rows, :] = (mixed / by_head(totals)).astype(bf16)
            lse = jnp.zeros((QB, 128), f32)
            for h in range(HEADS):
                lse = jnp.where(lanes == h, tops[h] + jnp.log(totals[h]), lse)
            lse_ref[:, rows] = lse.T[:8]

        for_window(lens_ref, qb, total_rows, window)

    for copy in leaving:
        copy.wait()


def attend_fwd(lens, tokens, pack, bias):
    rows = tokens.shape[0]
    part = jax.ShapeDtypeStruct((rows, FEAT), bf16)
    return pl.pallas_call(
        attend_fwd_body,
        out_shape=(part, part, part, part, jax.ShapeDtypeStruct((8, rows), f32)),
        in_specs=[SM, ANY, ANY, VM],
        out_specs=(ANY, ANY, ANY, VM, VM),
        scratch_shapes=[pltpu.VMEM((rows, FEAT), bf16)] * 3
        + [
            pltpu.VMEM((rows, D), bf16),
            pltpu.VMEM((D, D), bf16),
            pltpu.SemaphoreType.DMA((4 + rows // (2 * QB),)),
        ],
        name="attend_fwd",
        compiler_params=pltpu.CompilerParams(vmem_limit_bytes=62 << 20),
        cost_estimate=pl.CostEstimate(flops=8_000_000_000, bytes_accessed=8_000_000, transcendentals=4_000_000),
    )(lens, tokens, pack, bias)


def attend_bwd_body(
    lens_ref, q_in, k_in, v_in, mix_in, lse_in, do_ref, dqkv_ref,
    k_ref, q_ref, v_ref, mix_ref, lse_ref, k_turned, dq_acc, dk_acc, dv_acc, fetch_sem,
):
    fetches = [
        pltpu.make_async_copy(src, dst, fetch_sem.at[i])
        for i, (src, dst) in enumerate(
            ((k_in, k_ref), (q_in, q_ref), (v_in, v_ref), (mix_in, mix_ref), (lse_in, lse_ref))
        )
    ]
    for fetch in fetches:
        fetch.start()
    scale = HD ** (-0.5)
    total_rows = q_ref.shape[0]
    blocks = total_rows // QB
    heads = lane_head(QB)
    dk_acc[...] = jnp.zeros_like(dk_acc)
    dv_acc[...] = jnp.zeros_like(dv_acc)
    fetches[0].wait()

    @pl.loop(0, blocks)
    def _(qb):
        rows = pl.ds(pl.multiple_of(qb * QB, QB), QB)
        k_turned[:, rows] = k_ref[rows, :].T

    for fetch in fetches[1:]:
        fetch.wait()

    @pl.loop(0, blocks)
    def _(qb):
        rows = pl.ds(pl.multiple_of(qb * QB, QB), QB)
        start, end = sequence_of(lens_ref, lax.broadcasted_iota(jnp.int32, (1, QB), 1) + qb * QB)

        def window(at, win):
            qv = q_ref[rows, :] * scale
            do = do_ref[rows, :]
            along = (do.astype(f32) * mix_ref[rows, :].astype(f32)).T
            keys = pl.ds(at, win)
            kv, vv = k_ref[keys, :], v_ref[keys, :]
            pos = lax.broadcasted_iota(jnp.int32, (win, QB), 0) + at
            allowed = (pos >= start) & (pos < end)
            each = range(HEADS)
            qs = [jnp.where(heads == h, qv, jnp.zeros_like(qv)) for h in each]
            dos = [jnp.where(heads == h, do, jnp.zeros_like(do)) for h in each]
            inner = [jnp.sum(along[h * HD : (h + 1) * HD], axis=0, keepdims=True) for h in each]
            scores = [mm(kv, qs[h], NT) for h in each]
            probs = [jnp.where(allowed, jnp.exp(scores[h] - lse_ref[h : h + 1, rows]), 0.0) for h in each]
            dps = [mm(vv, dos[h], NT) for h in each]
            lows = [p.astype(bf16) for p in probs]
            dss = [(probs[h] * (dps[h] - inner[h])).astype(bf16) for h in each]
            grad_v = sum([mm(lows[h], dos[h], NN) for h in each])
            grad_k = sum([mm(dss[h], qs[h], NN) for h in each])
            grad_q = [mm(k_turned[h * HD : (h + 1) * HD, keys], dss[h], NN) for h in each]
            dk_acc[keys, :] += grad_k
            dv_acc[keys, :] += grad_v
            dq_acc[rows, :] = jnp.concatenate(grad_q, axis=0).T

        for_window(lens_ref, qb, total_rows, window)

    @pl.loop(0, blocks)
    def _(qb):
        rows = pl.ds(pl.multiple_of(qb * QB, QB), QB)
        parts = [dq_acc[rows, :] * scale, dk_acc[rows, :], dv_acc[rows, :]]
        dqkv_ref[rows, :] = jnp.concatenate([p.astype(bf16) for p in parts], axis=1)


def attend_bwd(lens, q, k, v, mixed, do, lse):
    rows = q.shape[0]
    return pl.pallas_call(
        attend_bwd_body,
        out_shape=jax.ShapeDtypeStruct((rows, 3 * FEAT), bf16),
        in_specs=[SM] + [ANY] * 5 + [VM],
        out_specs=VM,
        scratch_shapes=[pltpu.VMEM((rows, FEAT), bf16)] * 4
        + [
            pltpu.VMEM((8, rows), f32),
            pltpu.VMEM((FEAT, rows), bf16),
            pltpu.VMEM((rows, FEAT), f32),
            pltpu.VMEM((rows, FEAT), f32),
            pltpu.VMEM((rows, FEAT), f32),
            pltpu.SemaphoreType.DMA((5,)),
        ],
        name="attend_bwd",
        compiler_params=pltpu.CompilerParams(vmem_limit_bytes=62 << 20),
        cost_estimate=pl.CostEstimate(flops=20_000_000_000, bytes_accessed=6_000_000, transcendentals=4_000_000),
    )(lens, q, k, v, mixed, lse, do)


def remote(src, dst, send_sem, recv_sem, device):
    return pltpu.make_async_remote_copy(
        src_ref=src, dst_ref=dst, send_sem=send_sem, recv_sem=recv_sem,
        device_id=device, device_id_type=MESH,
    )


def col_peers():
    r, c = lax.axis_index("row"), lax.axis_index("col")
    sib, nbr, diag = c + 1 - 2 * (c % 2), (c + 2) % 4, 3 - c
    return r, c, sib, nbr, diag


def norm_rows(x):
    mean = jnp.mean(x, axis=1, keepdims=True)
    center = x - mean
    var = jnp.mean(center * center, axis=1, keepdims=True)
    inv = lax.rsqrt(var + norm_eps)
    return center * inv, inv


def norm_back(grad, gain, hat, inv):
    e = grad * gain
    mean_e = jnp.mean(e, axis=1, keepdims=True)
    mean_c = jnp.mean(e * hat, axis=1, keepdims=True)
    return inv * (e - mean_e - hat * mean_c)


CH = 128


HALF = 384
PARTS = 3
WIDE = HALF // PARTS


def half_lanes(h):
    return pl.ds(pl.multiple_of(h * HALF, HALF), HALF)


def greet(peers, rows, row, c):
    barrier = pltpu.get_barrier_semaphore()
    for peer in peers:
        pl.semaphore_signal(barrier, inc=1, device_id=(row, peer), device_id_type=MESH)

    @pl.loop(1, rows)
    def _(i):
        pl.semaphore_signal(barrier, inc=1, device_id=((row + i) % rows, c), device_id_type=MESH)

    pl.semaphore_wait(barrier, len(peers) + rows - 1)


def to_col(src, dst):
    eye = lax.broadcasted_iota(jnp.int32, (128, 128), 0) == lax.broadcasted_iota(jnp.int32, (128, 128), 1)

    @pl.loop(0, dst.shape[0] // 128)
    def _(t):
        at = pl.ds(pl.multiple_of(t * 128, 128), 128)
        dst[at, :] = jnp.sum(jnp.where(eye, src[:, at], 0.0), axis=1, keepdims=True)


def rank_row(row_ref, col_ref):
    keys = row_ref[...]
    size = keys.shape[1]

    def step(t, acc):
        col = col_ref[pl.ds(pl.multiple_of(t * 128, 128), 128), :]
        less = jnp.where(col < keys, 1.0, 0.0)
        return acc + jnp.sum(less.reshape(16, 8, size), axis=0)

    acc = lax.fori_loop(0, size // 128, step, jnp.zeros((8, size), f32))
    return jnp.sum(acc, axis=0, keepdims=True)


def picker_rows(rank, first, count):
    want = (lax.broadcasted_iota(jnp.int32, (count, rank.shape[1]), 0) + first).astype(f32)
    return jnp.where(rank == want, 1.0, 0.0).astype(bf16)


def picker_cols(rank, count):
    have = lax.broadcasted_iota(jnp.int32, (rank.shape[0], count), 1).astype(f32)
    return jnp.where(rank == have, 1.0, 0.0).astype(bf16)


def ring_spot(row, rows):
    return jnp.where(row % 2 == 0, row // 2, rows - 1 - row // 2)


def ring_row(spot, rows):
    spot = (spot + rows) % rows
    return jnp.where(spot < rows // 2, 2 * spot, 2 * (rows - 1 - spot) + 1)


class RingGather:
    def __init__(self, rows, place, sems):
        self.rows, self.hops, self.place = rows, rows // 2, place
        self.send, self.recv = sems
        self.r, self.c = lax.axis_index("row"), lax.axis_index("col")
        self.spot = ring_spot(self.r, rows)

    def copy(self, way, t):
        step, to = (self.rows - t, 1) if way == 0 else (t, self.rows - 1)
        v = self.place(ring_row(self.spot + step, self.rows))
        return remote(v, v, self.send.at[way, t], self.recv.at[way, t], (ring_row(self.spot + to, self.rows), self.c))

    def start(self):
        for way in range(2):
            if self.hops > way:
                self.copy(way, 0).start()

    def hop(self, t):
        for way in range(2):
            if t < self.hops - way:
                self.copy(way, t - 1).wait_recv()
                self.copy(way, t).start()

    def done(self):
        for way in range(2):
            if self.hops > way:
                self.copy(way, self.hops - way - 1).wait_recv()

    def finish(self):
        for way in range(2):
            for t in range(self.hops - way):
                self.copy(way, t).wait_send()


def placed(rank_col, got):
    tokens = got.shape[0] * got.shape[1] * got.shape[2]
    return mm(picker_cols(rank_col, tokens), got.reshape(tokens, got.shape[-1]), NN)


class Deal:
    def __init__(self, a, rows, bufs, sems):
        self.a, self.rows = a, rows
        self.xin, self.xout, self.sbuf, self.rbuf = bufs
        self.sib_s, self.sib_r, self.nbr_s, self.nbr_r, self.fwd_s, self.fwd_r, self.row_s, self.row_r, self.sh_s, self.sh_r = sems
        self.r, self.c, self.sib, self.nbr, self.diag = col_peers()
        self.h, self.core = self.c // 2, self.c % 2
        self.tokens = self.xin.shape[2] * 4
        self.slots = self.tokens // rows
        self.own_slots = self.slots // 2

    def to_sib(self):
        v = self.xin.at[self.a, self.c]
        return remote(v, v, self.sib_s.at[self.a], self.sib_r.at[self.a], (self.r, self.sib))

    def to_nbr(self):
        return remote(self.xout.at[self.a], self.xin.at[self.a, self.c], self.nbr_s.at[self.a], self.nbr_r.at[self.a], (self.r, self.nbr))

    def fwd(self):
        v = self.xin.at[self.a, self.nbr]
        return remote(v, v, self.fwd_s.at[self.a], self.fwd_r.at[self.a], (self.r, self.sib))

    def start_split(self):
        self.to_nbr().start()
        self.to_sib().start()

    def split(self, ref):
        self.xout[self.a] = ref[:, half_lanes(1 - self.h)].astype(bf16)
        self.to_nbr().start()
        self.xin[self.a, self.c] = ref[:, half_lanes(self.h)].astype(bf16)
        self.to_sib().start()

    def joined(self):
        self.to_nbr().wait_recv()
        self.fwd().start()
        self.to_sib().wait_recv()
        self.fwd().wait_recv()

    def row_copy(self, i):
        to = (self.r + i) % self.rows
        return remote(
            self.sbuf.at[self.a, i], self.rbuf.at[self.a, self.r, self.core],
            self.row_s.at[self.a, i], self.row_r.at[self.a, i], (to, self.c),
        )

    def share(self, i):
        v = self.rbuf.at[self.a, (self.r + self.rows - i) % self.rows, self.core]
        return remote(v, v, self.sh_s.at[self.a, i], self.sh_r.at[self.a, i], (self.r, self.sib))

    def pick_and_send(self, rank):
        source = self.xin[self.a].reshape(self.tokens, self.xin.shape[-1])

        def picked(to):
            return mm(picker_rows(rank, to * self.slots + self.core * self.own_slots, self.own_slots), source, NN).astype(bf16)

        @pl.loop(1, self.rows)
        def _(i):
            self.sbuf[self.a, i] = picked((self.r + i) % self.rows)
            self.row_copy(i).start()

        self.rbuf[self.a, self.r, self.core] = picked(self.r)
        self.share(0).start()

    def shared(self):
        @pl.loop(1, self.rows)
        def _(i):
            self.row_copy(i).wait_recv()
            self.share(i).start()

        @pl.loop(0, self.rows)
        def _(i):
            self.share(i).wait_recv()

    def placed(self, rank_col):
        return placed(rank_col, self.rbuf[self.a])

    def joined_sent(self):
        self.to_sib().wait_send()
        self.to_nbr().wait_send()
        self.fwd().wait_send()

    def rows_sent(self):
        @pl.loop(1, self.rows)
        def _(i):
            self.row_copy(i).wait_send()

        @pl.loop(0, self.rows)
        def _(i):
            self.share(i).wait_send()


def deal_scratch(rows, own_rows, count, width=HALF):
    slots = 4 * own_rows // rows
    return [
        pltpu.VMEM((count, 4, own_rows, width), bf16),
        pltpu.VMEM((count, own_rows, width), bf16),
        pltpu.VMEM((count, rows, slots // 2, width), bf16),
        pltpu.VMEM((count, rows, 2, slots // 2, width), bf16),
    ]


def deal_sems(rows, count):
    return [pltpu.SemaphoreType.DMA((count,))] * 6 + [pltpu.SemaphoreType.DMA((count, rows))] * 4


def arrive_body(
    rows, x_ref, g_ref, place_ref, order_ref, vin_ref, part_ref,
    pack_ref, tok_ref, own_ref, cot_ref, cot_send, rank_ref, vec_ref, bqv_ref, bin_ref,
    *scratch,
):
    bufs, sems = scratch[:4], scratch[4:14]
    key_g, key_w, col_g, col_w, vbuf = scratch[14:19]
    an_s, an_r, as_s, as_r, af_s, af_r, vr_s, vr_r, vc_s, vc_r, w_s, w_r = scratch[19:]
    r, c, sib, nbr, diag = col_peers()
    h = c // 2
    own_rows = x_ref.shape[0]
    tokens = 4 * own_rows
    chunks = own_rows // CH
    greet((sib, nbr, diag), rows, r, c)

    first, second = Deal(0, rows, bufs, sems), Deal(1, rows, bufs, sems)
    first.split(x_ref)
    ring = RingGather(rows, lambda b: pack_ref.at[b], (w_s, w_r))
    pack_ref[r] = part_ref[...]
    ring.start()
    second.split(g_ref)

    def vec_row(i):
        v = vbuf.at[c, r]
        return remote(v, v, vr_s.at[i], vr_r.at[i], ((r + i) % rows, c))

    def vec_col(i, peer):
        v = vbuf.at[c]
        return remote(v, v, vc_s.at[i], vc_r.at[i], (r, peer))

    vbuf[c, r] = vin_ref[...]

    @pl.loop(1, rows)
    def _(i):
        vec_row(i).start()

    key_g[...] = place_ref[...].astype(f32)
    source = order_ref[...] // tokens
    key_w[...] = (source * tokens + lax.broadcasted_iota(jnp.int32, (1, tokens), 1)).astype(f32)
    to_col(key_g, col_g)
    to_col(key_w, col_w)
    rank_ref[0:1, :] = rank_row(key_g, col_g)
    if ring.hops > 1:
        ring.hop(1)
    rank_ref[1:2, :] = rank_row(key_w, col_w)
    rank_g = rank_ref[0:1, :]
    key_w[...] = rank_ref[1:2, :]
    to_col(key_w, col_w)
    for t in range(2, ring.hops):
        ring.hop(t)

    first.joined()
    first.pick_and_send(rank_g)

    @pl.loop(1, rows)
    def _(i):
        vec_row(i).wait_recv()

    for i, peer in enumerate((sib, nbr, diag)):
        vec_col(i, peer).start()

    second.joined()
    second.pick_and_send(rank_g)

    for i, peer in enumerate((sib, nbr, diag)):
        vec_col(i, peer).wait_recv()
    width, wide = D // (4 * rows), 4 * D // (4 * rows)
    lane = lax.broadcasted_iota(jnp.int32, (HALF, D), 0)
    feat = lax.broadcasted_iota(jnp.int32, (HALF, D), 1)
    everyone = vbuf[:, :, 0, :].reshape(4 * rows, HALF).astype(bf16)
    mine = vbuf[c][:, 0, :].astype(bf16)
    owner = lax.broadcasted_iota(jnp.int32, (4 * rows, D), 0) == lax.broadcasted_iota(jnp.int32, (4 * rows, D), 1) // width
    vec_ref[...] = jnp.zeros_like(vec_ref)
    for i in range(6):
        hot = jnp.where(lane - (i + 2) * width == feat % width, 1.0, 0.0).astype(bf16)
        vec_ref[i : i + 1, :] = jnp.sum(jnp.where(owner, mm(everyone, hot, NN), 0.0), axis=0, keepdims=True)
    row_owner = lax.broadcasted_iota(jnp.int32, (rows, D), 0)
    row_feat = lax.broadcasted_iota(jnp.int32, (rows, D), 1)
    hot = jnp.where(lane - 8 * width == feat % wide, 1.0, 0.0).astype(bf16)
    bin_ref[...] = jnp.sum(jnp.where(row_owner == row_feat // wide, mm(mine, hot, NN), 0.0), axis=0, keepdims=True)
    bqv_ref[...] = jnp.zeros_like(bqv_ref)
    for i in range(2):
        hot = jnp.where(lane - i * width == feat % width, 1.0, 0.0).astype(bf16)
        whole = jnp.sum(jnp.where(row_owner == row_feat // width, mm(mine, hot, NN), 0.0), axis=0, keepdims=True)
        bqv_ref[i : i + 1, :] = whole[:, :FEAT]

    def piece(q, k, half):
        return tok_ref.at[q, pl.ds(pl.multiple_of(k * CH, CH), CH), half_lanes(half)]

    def tok_copy(qi, q, k, half, s, rr, peer):
        v = piece(q, k, half)
        return remote(v, v, s.at[qi, k], rr.at[qi, k], (r, peer))

    ours = ((0, c), (1, nbr))
    first.shared()

    @pl.loop(0, chunks)
    def _(k):
        at = pl.ds(pl.multiple_of(k * CH, CH), CH)
        for qi, q in ours:
            rank = col_w[pl.ds(pl.multiple_of(q * own_rows + k * CH, CH), CH), :]
            tok_ref[q, at, half_lanes(h)] = first.placed(rank).astype(bf16)
            tok_copy(qi, q, k, h, an_s, an_r, nbr).start()
            tok_copy(qi, q, k, h, as_s, as_r, sib).start()

    def pass_on(k):
        for qi, q in ours:
            tok_copy(1 - qi, q, k, 1 - h, an_s, an_r, nbr).wait_recv()
            tok_copy(qi, q, k, 1 - h, af_s, af_r, sib).start()

    pl.loop(0, chunks // 2)(pass_on)
    second.shared()
    pl.loop(chunks // 2, chunks)(pass_on)
    for q, ref in ((nbr, cot_send), (c, cot_ref)):

        @pl.loop(0, chunks)
        def _(k):
            rank = col_w[pl.ds(pl.multiple_of(q * own_rows + k * CH, CH), CH), :]
            ref[pl.ds(pl.multiple_of(k * CH, CH), CH), :] = second.placed(rank).astype(bf16)

    @pl.loop(0, chunks)
    def _(k):
        for qi, q in ours:
            tok_copy(qi, q, k, h, as_s, as_r, sib).wait_recv()
            tok_copy(qi, q, k, 1 - h, af_s, af_r, sib).wait_recv()
            tok_copy(qi, q, k, h, an_s, an_r, nbr).wait_send()
            tok_copy(qi, q, k, h, as_s, as_r, sib).wait_send()
            tok_copy(qi, q, k, 1 - h, af_s, af_r, sib).wait_send()

    own_ref[...] = tok_ref[c]
    ring.done()
    ring.finish()

    for deal in (first, second):
        deal.joined_sent()
        deal.rows_sent()

    @pl.loop(1, rows)
    def _(i):
        vec_row(i).wait_send()

    for i, peer in enumerate((sib, nbr, diag)):
        vec_col(i, peer).wait_send()


def arrive(rows, x, g, place, order, vin, part):
    own_rows = x.shape[0]
    tokens = 4 * own_rows
    chunks = own_rows // CH
    S, V, DS = jax.ShapeDtypeStruct, pltpu.VMEM, pltpu.SemaphoreType.DMA
    return pl.pallas_call(
        functools.partial(arrive_body, rows),
        out_shape=(
            S((rows, D // rows, D), bf16), S((4, own_rows, D), bf16), S((own_rows, D), bf16),
            S((own_rows, HALF), bf16), S((own_rows, HALF), bf16), S((8, tokens), f32),
            S((8, D), f32), S((8, FEAT), f32), S((1, D), f32),
        ),
        in_specs=[VM] * 6,
        out_specs=(VM,) * 9,
        scratch_shapes=deal_scratch(rows, own_rows, 2)
        + deal_sems(rows, 2)
        + [
            V((1, tokens), f32), V((1, tokens), f32), V((tokens, 1), f32), V((tokens, 1), f32),
            V((4, rows, 8, HALF), f32),
        ]
        + [DS((2, chunks))] * 6
        + [DS((rows,))] * 2
        + [DS((3,))] * 2
        + [DS((2, rows // 2))] * 2,
        name="arrive",
        compiler_params=pltpu.CompilerParams(collective_id=1, has_side_effects=True, vmem_limit_bytes=62 << 20),
        cost_estimate=pl.CostEstimate(flops=60_000_000_000, bytes_accessed=20_000_000, transcendentals=0),
    )(x, g, place, order, vin, part)


class Ring:
    def __init__(self, rows, own, sbuf, rbuf, sems):
        self.rows, self.hops = rows, rows // 2
        self.own = own
        self.sbuf, self.rbuf = sbuf, rbuf
        self.send, self.recv = sems
        self.r, self.c = lax.axis_index("row"), lax.axis_index("col")
        self.spot = ring_spot(self.r, rows)

    def copy(self, way, t):
        to = ring_row(self.spot + (1 if way == 0 else self.rows - 1), self.rows)
        return remote(
            self.sbuf.at[way, t], self.rbuf.at[way, t], self.send.at[way, t], self.recv.at[way, t], (to, self.c)
        )

    def block(self, way, t):
        if way == 0:
            return ring_row(self.spot + self.hops - t, self.rows)
        return ring_row(self.spot + self.rows - (self.hops - 1) + t, self.rows)

    def start(self):
        for way in range(2 if self.hops > 1 else 1):
            self.sbuf[way, 0] = self.own(self.block(way, 0)).astype(bf16)
            self.copy(way, 0).start()

    def hop(self, t):
        for way in range(2):
            if t < self.hops - way:
                self.copy(way, t - 1).wait_recv()
                total = self.own(self.block(way, t)) + self.rbuf[way, t - 1].astype(f32)
                self.sbuf[way, t] = total.astype(bf16)
                self.copy(way, t).start()

    def result(self):
        self.copy(0, self.hops - 1).wait_recv()
        total = self.own(self.r) + self.rbuf[0, self.hops - 1].astype(f32)
        if self.hops > 1:
            self.copy(1, self.hops - 2).wait_recv()
            total = total + self.rbuf[1, self.hops - 2].astype(f32)
        return total

    def finish(self):
        for way in range(2):
            for t in range(self.hops - way):
                self.copy(way, t).wait_send()


def middle_body(
    rows, mixed_ref, tok_ref, cot_own, cot_got, pack_ref, ff_ref, vec_ref, bin_ref, rank_ref,
    back_ref, g1_ref, gmix_ref, dwo_ref, gin_ref, gout_ref, dvec_ref, dbin_ref,
    *scratch,
):
    nfull, hidden, slope, g2full, own, d2ds, d2dr, xs, xr, hat1, inv1, grad2, dwin, dwout = scratch[:14]
    wo_ref, attn_w, ff_all, wide, w_sem, wr_s, wr_r, xin, xout, sbuf, ring_out, ring_in = scratch[14:26]
    ds_s, ds_r, x_s, x_r, asib_s, asib_r, anbr_s, anbr_r, afwd_s, afwd_r, q_s, q_r = scratch[26:38]
    r, c, sib, nbr, diag = col_peers()
    h = c // 2
    chunks = tok_ref.shape[0] // CH
    block = D // rows
    fetch = pltpu.make_async_copy(pack_ref, attn_w, w_sem.at[0])
    fetch.start()
    greet((sib, nbr), rows, r, c)
    ff_ring = RingGather(rows, lambda b: ff_all.at[b], (wr_s, wr_r))
    ff_all[r] = ff_ref[...]
    ff_ring.start()
    fetch.wait()
    wo_ref[...] = attn_w[:, 3 * FEAT :]
    outs = Deal(0, rows, (xin, xout, sbuf, back_ref), scratch[38:])
    ring = Ring(rows, lambda b: jnp.concatenate([dwin[b], dwout[b]], axis=1), ring_out, ring_in, (q_s, q_r))

    bo, g1, s1, b2, g2, s2 = [vec_ref[pl.ds(i, 1), :] for i in range(6)]

    def win():
        return ff_all[:, :, :D].reshape(D, D) if block % 16 == 0 else attn_w[...]

    def wout():
        return ff_all[:, :, D:].reshape(D, D) if block % 16 == 0 else wide[...]

    def d2d(st, k):
        return remote(d2ds.at[k], d2dr.at[k], ds_s.at[st, k], ds_r.at[st, k], (r, sib))

    def xcopy(st, k):
        return remote(xs.at[k], xr.at[k], x_s.at[st, k], x_r.at[st, k], (r, nbr))

    def rs_start(st, k, pair):
        if st > 0:
            d2d(st - 1, k).wait_send()
            xcopy(st - 1, k).wait_send()
        d2ds[k] = pair(sib, diag).astype(bf16).reshape(2, CH, D)
        d2d(st, k).start()
        both = pair(c, nbr)
        d2d(st, k).wait_recv()
        xs[k] = (both[CH:] + d2dr[k, 1].astype(f32)).astype(bf16)
        xcopy(st, k).start()
        own[k] = both[:CH] + d2dr[k, 0].astype(f32)

    def rs_end(st, k):
        xcopy(st, k).wait_recv()
        return own[k] + xr[k].astype(f32)

    gathered = (nfull, g2full, g1_ref)

    def piece(st, q, k):
        return gathered[st].at[q, pl.ds(pl.multiple_of(k * CH, CH), CH), :]

    def ag_copy(st, k, q, sems, target):
        return remote(piece(st, q, k), piece(st, q, k), sems[0].at[st, k], sems[1].at[st, k], (r, target))

    to_sib = functools.partial(ag_copy, sems=(asib_s, asib_r), target=sib)
    to_nbr = functools.partial(ag_copy, sems=(anbr_s, anbr_r), target=nbr)
    fwd = functools.partial(ag_copy, sems=(afwd_s, afwd_r), target=sib)

    def ag_start(st, k, value):
        gathered[st][c, pl.ds(pl.multiple_of(k * CH, CH), CH), :] = value
        to_nbr(st, k, c).start()
        to_sib(st, k, c).start()

    def ag_end(st, k):
        to_nbr(st, k, c).wait_recv()
        fwd(st, k, nbr).start()
        to_sib(st, k, c).wait_recv()
        fwd(st, k, nbr).wait_recv()

    def rows_of(k):
        return pl.ds(pl.multiple_of(k * CH, CH), CH)

    def two_rows(ref, p, q, k):
        return jnp.concatenate([ref[p, rows_of(k), :], ref[q, rows_of(k), :]], axis=0)

    def put_two(ref, p, q, k, value):
        ref[p, rows_of(k), :] = value[:CH]
        ref[q, rows_of(k), :] = value[CH:]

    def all_rows(ref, k):
        return ref[:, rows_of(k), :].reshape(4 * CH, ref.shape[2])

    def ff_hops(part):
        for t in range(1 + part * (ff_ring.hops - 1) // 3, 1 + (part + 1) * (ff_ring.hops - 1) // 3):
            ff_ring.hop(t)

    def mix_heads(k):
        rs_start(0, k, lambda p, q: mm(two_rows(mixed_ref, p, q, k), wo_ref[...], NT))

    def first_norm(k):
        resid = rs_end(0, k) + tok_ref[rows_of(k), :].astype(f32) + bo
        hat, inv = norm_rows(resid)
        hat1[k] = hat
        inv1[k] = inv
        val = hat * g1 + s1
        ag_start(0, k, val.astype(bf16))

    pl.loop(0, chunks // 2)(mix_heads)
    ff_hops(0)
    pl.loop(chunks // 2, chunks)(mix_heads)
    ff_hops(1)
    pl.loop(0, chunks // 2)(first_norm)
    ff_hops(2)
    pl.loop(chunks // 2, chunks)(first_norm)
    ff_ring.done()
    if block % 16 != 0:
        for b in range(rows):
            attn_w[b * block : (b + 1) * block, :] = ff_all[b, :, :D]
            wide[b * block : (b + 1) * block, :] = ff_all[b, :, D:]

    @pl.loop(0, chunks)
    def _(k):
        ag_end(0, k)

        def pair(p, q):
            pre = mm(two_rows(nfull, p, q, k), win(), NN) + bin_ref[...]
            cum = 0.5 * (1.0 + lax.erf(pre * root_half))
            dens = jnp.exp(-0.5 * pre * pre) * inv_root_two_pi
            low = (pre * cum).astype(bf16)
            put_two(hidden, p, q, k, low)
            put_two(slope, p, q, k, cum + pre * dens)
            return mm(low, wout(), NT)

        rs_start(1, k, pair)

    dvec_ref[...] = jnp.zeros_like(dvec_ref)

    @pl.loop(0, chunks)
    def _(k):
        resid = rs_end(1, k) + (hat1[k] * g1 + s1) + b2
        hat, inv = norm_rows(resid)
        low, high = [half.astype(bf16) for half in jnp.split(hat * g2 + s2, 2, axis=1)]
        xin[0, c, rows_of(k), :] = jnp.where(h == 0, low, high)
        xout[0, rows_of(k), :] = jnp.where(h == 0, high, low)
        halves = (cot_own[rows_of(k), :], cot_got[rows_of(k), :])
        low, high = jnp.where(h == 0, halves[0], halves[1]), jnp.where(h == 0, halves[1], halves[0])
        cot = jnp.concatenate([low, high], axis=1).astype(f32)
        grad = norm_back(cot, g2, hat, inv)
        grad2[k] = grad
        ag_start(1, k, grad.astype(bf16))
        dvec_ref[pl.ds(2, 1), :] += jnp.sum(grad, axis=0, keepdims=True)
        dvec_ref[pl.ds(5, 1), :] += jnp.sum(cot * hat, axis=0, keepdims=True)
        dvec_ref[pl.ds(6, 1), :] += jnp.sum(cot, axis=0, keepdims=True)

    outs.start_split()
    dwin[...] = jnp.zeros_like(dwin)
    dwout[...] = jnp.zeros_like(dwout)
    dwo_ref[...] = jnp.zeros_like(dwo_ref)
    dbin_ref[...] = jnp.zeros_like(dbin_ref)

    def add_blocks(ref, value):
        if block % 8 == 0:
            ref[...] += value.reshape(rows, block, D)
        else:
            for b in range(rows):
                ref[b] += value[b * block : (b + 1) * block]

    def back_hidden(k):
        ag_end(1, k)

        def pair(p, q):
            grad_pre = mm(two_rows(g2full, p, q, k), wout(), NN) * two_rows(slope, p, q, k)
            dbin_ref[...] += jnp.sum(grad_pre, axis=0, keepdims=True)
            low = grad_pre.astype(bf16)
            put_two(slope, p, q, k, low.astype(f32))
            return mm(low, win(), NT)

        rs_start(2, k, pair)
        add_blocks(dwout, mm(all_rows(g2full, k), all_rows(hidden, k), TN))
        add_blocks(dwin, mm(all_rows(nfull, k), all_rows(slope, k).astype(bf16), TN))

    pl.loop(0, chunks // 2)(back_hidden)
    outs.joined()
    outs.pick_and_send(rank_ref[1:2, :])
    pl.loop(chunks // 2, chunks)(back_hidden)
    ring.start()

    def hops(part):
        for t in range(1 + part * (ring.hops - 1) // 3, 1 + (part + 1) * (ring.hops - 1) // 3):
            ring.hop(t)

    def back_first(k):
        grad_normed = rs_end(2, k) + grad2[k]
        hat = hat1[k]
        grad = norm_back(grad_normed, g1, hat, inv1[k])
        ag_start(2, k, grad.astype(bf16))
        dvec_ref[pl.ds(1, 1), :] += jnp.sum(grad, axis=0, keepdims=True)
        dvec_ref[pl.ds(3, 1), :] += jnp.sum(grad_normed * hat, axis=0, keepdims=True)
        dvec_ref[pl.ds(4, 1), :] += jnp.sum(grad_normed, axis=0, keepdims=True)

    pl.loop(0, chunks // 2)(back_first)
    hops(0)
    pl.loop(chunks // 2, chunks)(back_first)
    hops(1)

    def back_mixed(k):
        ag_end(2, k)
        g1c = all_rows(g1_ref, k)
        gmix_ref[:, rows_of(k), :] = mm(g1c, wo_ref[...], NN).astype(bf16).reshape(4, CH, FEAT)
        dwo_ref[...] += mm(g1c, all_rows(mixed_ref, k), TN)

    pl.loop(0, chunks // 2)(back_mixed)
    hops(2)
    pl.loop(chunks // 2, chunks)(back_mixed)
    outs.shared()
    total = ring.result()
    gin_ref[...] = total[:, :D]
    gout_ref[...] = total[:, D:].T

    @pl.loop(0, chunks)
    def _(k):
        d2d(2, k).wait_send()
        xcopy(2, k).wait_send()
        for st in range(3):
            to_sib(st, k, c).wait_send()
            to_nbr(st, k, c).wait_send()
            fwd(st, k, nbr).wait_send()

    outs.joined_sent()
    outs.rows_sent()
    ring.finish()
    ff_ring.finish()


def middle(rows, mixed, tok, cot_own, cot_got, pack, ff_part, vec, b_in, rank):
    own_rows = tok.shape[0]
    chunks = own_rows // CH
    block, hops, slots = D // rows, rows // 2, 4 * own_rows // rows
    sem = pltpu.SemaphoreType.DMA((3, chunks))
    S, V = jax.ShapeDtypeStruct, pltpu.VMEM
    return pl.pallas_call(
        functools.partial(middle_body, rows),
        out_shape=(
            S((1, rows, 2, slots // 2, HALF), bf16),
            S((4, own_rows, D), bf16),
            S((4, own_rows, FEAT), bf16),
            S((D, FEAT), f32),
            S((block, D), f32),
            S((D, block), f32),
            S((8, D), f32),
            S((1, D), f32),
        ),
        in_specs=[VM] * 4 + [ANY] + [VM] * 4,
        out_specs=(VM,) * 8,
        scratch_shapes=[
            pltpu.VMEM((4, own_rows, D), bf16),
            pltpu.VMEM((4, own_rows, D), bf16),
            pltpu.VMEM((4, own_rows, D), f32),
            pltpu.VMEM((4, own_rows, D), bf16),
            pltpu.VMEM((chunks, CH, D), f32),
            pltpu.VMEM((chunks, 2, CH, D), bf16),
            pltpu.VMEM((chunks, 2, CH, D), bf16),
            pltpu.VMEM((chunks, CH, D), bf16),
            pltpu.VMEM((chunks, CH, D), bf16),
            pltpu.VMEM((chunks, CH, D), f32),
            pltpu.VMEM((chunks, CH, 1), f32),
            pltpu.VMEM((chunks, CH, D), f32),
            V((rows, block, D), f32),
            V((rows, block, D), f32),
            V((D, FEAT), bf16),
            V((D, D), bf16),
            V((rows, block, 2 * D), bf16),
            V((8, 128) if block % 16 == 0 else (D, D), bf16),
            pltpu.SemaphoreType.DMA((1,)),
            pltpu.SemaphoreType.DMA((2, hops)),
            pltpu.SemaphoreType.DMA((2, hops)),
        ]
        + deal_scratch(rows, own_rows, 1)[:3]
        + [V((2, hops, block, 2 * D), bf16)] * 2
        + [sem] * 10
        + [pltpu.SemaphoreType.DMA((2, hops))] * 2
        + deal_sems(rows, 1),
        name="middle",
        compiler_params=pltpu.CompilerParams(collective_id=2, has_side_effects=True, vmem_limit_bytes=62 << 20),
        cost_estimate=pl.CostEstimate(flops=80_000_000_000, bytes_accessed=20_000_000, transcendentals=4_000_000),
    )(mixed, tok, cot_own, cot_got, pack, ff_part, vec, b_in, rank)


def depart_body(
    rows, back_in, g1_in, dqkv_in, pack_in, tok_in, rank_ref, dwo_ref, dvec_ref, dbin_ref,
    out_ref, grad_ref, gq_ref, gk_ref, gv_ref, go_ref, gvec_ref, gwide_ref,
    *scratch,
):
    bufs, sems = scratch[:4], scratch[4:14]
    key, col_g, sums, dw = scratch[14:18]
    d2ds, d2dr, keep, xs, xr, gsend, grecv, r2s, r2r, vmine, vall, vrow, back_ref, g1_ref, dqkv_ref, w_ref, tok_ref, f_sem, psend, precv = scratch[18:38]
    ds_s, ds_r, x_s, x_r, fin_s, fin_r, q2_s, q2_r, sh_s, sh_r, vc_s, vc_r, vr_s, vr_r, pf_s, pf_r = scratch[38:]
    r, c, sib, nbr, diag = col_peers()
    h = c // 2
    own_rows = out_ref.shape[0]
    tokens = 4 * own_rows
    chunks = own_rows // CH
    block = D // rows
    pairs = ((dqkv_in, dqkv_ref), (pack_in, w_ref), (tok_in, tok_ref), (g1_in, g1_ref), (back_in, back_ref))
    fetches = [pltpu.make_async_copy(src, dst, f_sem.at[n]) for n, (src, dst) in enumerate(pairs)]
    for fetch in fetches:
        fetch.start()
    greet((sib, nbr, diag), rows, r, c)

    def rows_of(k):
        return pl.ds(pl.multiple_of(k * CH, CH), CH)

    def token_rows(q, k):
        return pl.ds(pl.multiple_of(q * own_rows + k * CH, CH), CH)

    grads = [Deal(f, rows, bufs, sems) for f in range(PARTS)]
    ring = Ring(rows, lambda b: jnp.concatenate([dw[b], dwo_ref[b]], axis=1), r2s, r2r, (q2_s, q2_r))
    ours = ((0, c), (1, nbr))

    vmine[...] = jnp.zeros_like(vmine)
    vmine[0:8, :] = dvec_ref[...]

    def vec_col(i, peer):
        return remote(vmine, vall.at[c], vc_s.at[i], vc_r.at[i], (r, peer))

    for i, peer in enumerate((sib, nbr, diag)):
        vec_col(i, peer).start()

    def d2d(k):
        return remote(d2ds.at[k], d2dr.at[k], ds_s.at[k], ds_r.at[k], (r, sib))

    def xcopy(k):
        return remote(xs.at[k], xr.at[k], x_s.at[k], x_r.at[k], (r, nbr))

    def lanes_of(half, f):
        return pl.ds(pl.multiple_of(half * HALF + f * WIDE, WIDE), WIDE)

    def send_parts(f):
        w = jnp.concatenate([w_ref[lanes_of(h, f), : 3 * FEAT], w_ref[lanes_of(1 - h, f), : 3 * FEAT]], axis=0)

        def part(q):
            return mm(dqkv_ref[pl.ds(pl.multiple_of(q * own_rows, own_rows), own_rows), :], w, NT)

        d2ds[f, 0] = part(sib).astype(bf16)
        d2ds[f, 1] = part(diag).astype(bf16)
        d2d(f).start()
        for i, q in ours:
            keep[f, i] = part(q)
        d2d(f).wait_recv()
        for i in range(2):
            keep[f, i] = keep[f, i] + d2dr[f, i].astype(f32)
            xs[f, 1 - i] = keep[f, i, :, WIDE:].astype(bf16)
        xcopy(f).start()

    def shared(f, i, q):
        v = grads[f].xin.at[f, q]
        return remote(v, v, sh_s.at[i, f], sh_r.at[i, f], (r, sib))

    def grad_rows(f):
        xcopy(f).wait_recv()
        for i, q in ours:
            total = keep[f, i, :, :WIDE] + xr[f, i].astype(f32) + g1_ref[q, :, lanes_of(h, f)].astype(f32)
            grads[f].xin[f, q] = total.astype(bf16)
            shared(f, i, q).start()
        for i, q in ours:
            shared(f, i, q).wait_recv()
        grads[f].pick_and_send(rank_ref[1:2, :])

    fetches[0].wait()
    fetches[1].wait()
    send_parts(0)
    send_parts(1)
    fetches[2].wait()
    whole = mm(tok_ref[...].reshape(tokens, D), dqkv_ref[...], TN)
    for b in range(rows):
        dw[b] = whole[b * block : (b + 1) * block]
    ring.start()
    for f in range(2, PARTS):
        send_parts(f)
    fetches[3].wait()
    grad_rows(0)
    grad_rows(1)
    if ring.hops > 1:
        ring.hop(1)
    grad_rows(2)
    if ring.hops > 2:
        ring.hop(2)
    if ring.hops > 3:
        ring.hop(3)

    sums[...] = jnp.zeros_like(sums)

    @pl.loop(0, tokens // QB)
    def _(k):
        part_rows = dqkv_ref[pl.ds(pl.multiple_of(k * QB, QB), QB), :].astype(f32)
        sums[0:1, :] += jnp.sum(part_rows, axis=0, keepdims=True)

    for i, peer in enumerate((sib, nbr, diag)):
        vec_col(i, peer).wait_recv()
    total = vmine[...] + vall[sib] + vall[nbr] + vall[diag]
    vrow[r, 0:8, :] = total[0:8, :]
    vrow[r, 8:9, :] = dbin_ref[...]
    vrow[r, 9:10, :] = jnp.concatenate([sums[0:1, :], jnp.zeros((1, FEAT), f32)], axis=1)

    def vec_row(i):
        v = vrow.at[r]
        return remote(v, v, vr_s.at[i], vr_r.at[i], ((r + i) % rows, c))

    @pl.loop(1, rows)
    def _(i):
        vec_row(i).start()

    key[...] = rank_ref[0:1, :]
    to_col(key, col_g)

    def final(i, k):
        return remote(gsend.at[i, k], grecv.at[i, k], fin_s.at[i, k], fin_r.at[i, k], (r, nbr))

    def send_final(i, got):
        @pl.loop(0, chunks)
        def _(k):
            gsend[i, k] = placed(col_g[token_rows(nbr, k), :], got[0]).astype(bf16)
            final(i, k).start()

    def own_final(got, ref):
        @pl.loop(0, chunks)
        def _(k):
            ref[rows_of(k), half_lanes(h)] = placed(col_g[token_rows(c, k), :], got[0]).astype(bf16)

    def take_final(i, ref):
        @pl.loop(0, chunks)
        def _(k):
            final(i, k).wait_recv()
            ref[rows_of(k), half_lanes(1 - h)] = grecv[i, k]

    fetches[4].wait()
    send_final(0, back_ref)
    own_final(back_ref, out_ref)
    @pl.loop(1, rows)
    def _(i):
        vec_row(i).wait_recv()

    total = vrow[0]
    for i in range(1, rows):
        total = total + vrow[i]
    width, wide = D // (4 * rows), 4 * D // (4 * rows)
    spots = lax.broadcasted_iota(jnp.int32, (D, 128), 0)
    outs_at = lax.broadcasted_iota(jnp.int32, (D, 128), 1)

    def chosen(values, first, size):
        hot = jnp.where((spots - first == outs_at) & (outs_at < size), 1.0, 0.0)
        return lax.dot_general(values, hot, NN, precision=lax.Precision.HIGHEST, preferred_element_type=f32)

    gvec_ref[0:8, :] = chosen(total[0:8, :], (c * rows + r) * width, width)
    gwide_ref[0:1, :] = chosen(total[8:16, :], r * wide, wide)[0:1, :]
    gwide_ref[1:2, :] = chosen(total[8:16, :], r * width, width)[1:2, :]
    gwide_ref[2:3, :] = chosen(total[8:16, :], 2 * FEAT + r * width, width)[1:2, :]
    take_final(0, out_ref)

    def grad_final(f):
        return remote(psend.at[f], precv.at[f], pf_s.at[f], pf_r.at[f], (r, nbr))

    for f in range(PARTS):
        grads[f].shared()

        @pl.loop(0, chunks)
        def _(k):
            psend[f, rows_of(k), :] = placed(col_g[token_rows(nbr, k), :], grads[f].rbuf[f]).astype(bf16)

        grad_final(f).start()

    for f in range(PARTS):

        @pl.loop(0, chunks)
        def _(k):
            grad_ref[rows_of(k), lanes_of(h, f)] = placed(col_g[token_rows(c, k), :], grads[f].rbuf[f]).astype(bf16)

    for t in range(4, ring.hops):
        ring.hop(t)
    total = ring.result()
    for i, ref in enumerate((gq_ref, gk_ref, gv_ref)):
        ref[...] = total[:, i * FEAT : (i + 1) * FEAT]
    go_ref[...] = total[:, 3 * FEAT :].T

    for f in range(PARTS):
        grad_final(f).wait()
        grad_ref[:, lanes_of(1 - h, f)] = precv[f]
        grads[f].rows_sent()
        d2d(f).wait_send()
        xcopy(f).wait_send()
        for i, q in ours:
            shared(f, i, q).wait_send()

    @pl.loop(0, chunks)
    def _(k):
        final(0, k).wait_send()

    ring.finish()
    for i, peer in enumerate((sib, nbr, diag)):
        vec_col(i, peer).wait_send()

    @pl.loop(1, rows)
    def _(i):
        vec_row(i).wait_send()


def depart(rows, back, g1, dqkv, pack, tok, rank, dwo, dvec, dbin):
    own_rows = tok.shape[1]
    tokens = 4 * own_rows
    chunks = own_rows // CH
    block, hops = D // rows, rows // 2
    S, V, DS = jax.ShapeDtypeStruct, pltpu.VMEM, pltpu.SemaphoreType.DMA
    third = S((block, FEAT), f32)
    return pl.pallas_call(
        functools.partial(depart_body, rows),
        out_shape=(
            S((own_rows, D), bf16), S((own_rows, D), bf16), third, third, third, S((FEAT, block), f32),
            S((8, 128), f32), S((8, 128), f32),
        ),
        in_specs=[ANY] * 5 + [VM] * 4,
        out_specs=(VM,) * 8,
        scratch_shapes=deal_scratch(rows, own_rows, PARTS, WIDE)
        + deal_sems(rows, PARTS)
        + [V((1, tokens), f32), V((tokens, 1), f32), V((8, 3 * FEAT), f32), V((rows, block, 3 * FEAT), f32)]
        + [
            V((PARTS, 2, own_rows, 2 * WIDE), bf16), V((PARTS, 2, own_rows, 2 * WIDE), bf16),
            V((PARTS, 2, own_rows, 2 * WIDE), f32),
            V((PARTS, 2, own_rows, WIDE), bf16), V((PARTS, 2, own_rows, WIDE), bf16),
            V((1, chunks, CH, HALF), bf16), V((1, chunks, CH, HALF), bf16),
            V((2, hops, block, D), bf16), V((2, hops, block, D), bf16),
            V((16, D), f32), V((4, 16, D), f32), V((rows, 16, D), f32),
            V(back.shape, bf16), V(g1.shape, bf16), V(dqkv.shape, bf16), V((D, D), bf16), V(tok.shape, bf16), DS((5,)),
            V((PARTS, own_rows, WIDE), bf16), V((PARTS, own_rows, WIDE), bf16),
        ]
        + [DS((PARTS,))] * 4
        + [DS((1, chunks))] * 2
        + [DS((2, hops))] * 2
        + [DS((2, PARTS))] * 2
        + [DS((3,))] * 2
        + [DS((rows,))] * 2
        + [DS((PARTS,))] * 2,
        name="depart",
        compiler_params=pltpu.CompilerParams(collective_id=3, has_side_effects=True, vmem_limit_bytes=62 << 20),
        cost_estimate=pl.CostEstimate(flops=60_000_000_000, bytes_accessed=20_000_000, transcendentals=0),
    )(back, g1, dqkv, pack, tok, rank, dwo, dvec, dbin)


def gather_up_body(*refs):
    weights, vectors, (attn_ref, ff_ref, vin_ref) = refs[:6], refs[6:-3], refs[-3:]
    q, k, v, o, inner, outer = weights
    attn_ref[...] = jnp.concatenate([q[...], k[...], v[...], o[...].T], axis=1)
    ff_ref[:, :D] = inner[...]
    ff_ref[:, D:] = outer[...].T
    parts = [ref[...].astype(f32) for ref in vectors]
    left = HALF - sum(part.shape[1] for part in parts)
    row = jnp.concatenate(parts + [jnp.zeros((1, left), f32)], axis=1)
    vin_ref[...] = jnp.broadcast_to(row, vin_ref.shape)


def gather_up(weights, vectors):
    S, block = jax.ShapeDtypeStruct, weights[0].shape[0]
    return pl.pallas_call(
        gather_up_body,
        out_shape=(S((block, D), bf16), S((block, 2 * D), bf16), S((8, HALF), f32)),
        in_specs=[VM] * (len(weights) + len(vectors)),
        out_specs=(VM, VM, VM),
        name="gather_up",
        compiler_params=pltpu.CompilerParams(vmem_limit_bytes=62 << 20),
    )(*weights, *(v[None] for v in vectors))


def hand_out_body(small, wide, *refs):
    arrays, (gvec_ref, gwide_ref) = refs[:8], refs[8:10]
    outs = refs[10:]
    for src, dst in zip(arrays, outs[:8]):
        dst[...] = src[...].astype(f32)
    q, v, o, inner, outer, gain1, shift1, gain2, shift2 = outs[8:]
    q[...] = gwide_ref[1:2, :small]
    v[...] = gwide_ref[2:3, :small]
    inner[...] = gwide_ref[0:1, :wide]
    for i, ref in enumerate((o, outer, gain1, shift1, gain2, shift2)):
        ref[...] = gvec_ref[i + 1 : i + 2, :small]


def hand_out(small, wide, arrays, gvec, gwide):
    S = jax.ShapeDtypeStruct
    one, four = S((1, small), f32), S((1, wide), f32)
    outs = pl.pallas_call(
        functools.partial(hand_out_body, small, wide),
        out_shape=tuple(S(a.shape, f32) for a in arrays) + (one, one, one, four) + (one,) * 5,
        in_specs=[VM] * 10,
        out_specs=(VM,) * 17,
        name="hand_out",
        compiler_params=pltpu.CompilerParams(vmem_limit_bytes=62 << 20),
    )(*arrays, gvec, gwide)
    return outs[:8] + tuple(v.reshape(-1) for v in outs[8:])


def per_device(
    inputs, cotangent, token_order, token_place, seq_lengths,
    query_weight, key_weight, value_weight, output_weight, inner_weight, outer_weight,
    query_bias, value_bias, output_bias, inner_bias, outer_bias,
    first_gain, first_shift, second_gain, second_shift,
):
    rows = lax.axis_size("row")
    own_rows = inputs.shape[0]
    tok_rows = 4 * own_rows

    attn_part, ff_part, vin = gather_up(
        (query_weight, key_weight, value_weight, output_weight, inner_weight, outer_weight),
        (
            query_bias, value_bias, output_bias, first_gain, first_shift, outer_bias, second_gain, second_shift,
            inner_bias,
        ),
    )
    pack, tok, own_tok, cot_own, cot_send, rank, vec, bqv, b_in = arrive(
        rows, inputs, cotangent, token_place[None], token_order[None], vin, attn_part
    )
    pack = pack.reshape(D, D)
    cot_got = lax.ppermute(cot_send, "col", [(i, (i + 2) % 4) for i in range(4)])
    q, k, v, mixed, lse = attend_fwd(seq_lengths, tok.reshape(tok_rows, D), pack, bqv)
    back, g1, gmix, dwo, g_in, g_out, dvec, dbin = middle(
        rows, mixed.reshape(4, own_rows, FEAT), own_tok, cot_own, cot_got, pack, ff_part, vec, b_in, rank
    )
    dqkv = attend_bwd(seq_lengths, q, k, v, mixed, gmix.reshape(tok_rows, FEAT), lse)
    output, input_grad, gq, gk, gv, go, gvec, gwide = depart(
        rows, back, g1, dqkv, pack, tok, rank, dwo.reshape(rows, -1, FEAT), dvec, dbin
    )
    return hand_out(
        query_bias.shape[0], inner_bias.shape[0], (output, input_grad, gq, gk, gv, go, g_in, g_out), gvec, gwide
    )


def solution(mesh):
    tok = P(("row", "col"), None)
    rc, cr, vec = P("row", "col"), P("col", "row"), P(("col", "row"))
    in_specs = (tok, tok, P("row"), P("row"), P("row", None), rc, rc, rc, cr, rc, cr) + (vec,) * 9
    out_specs = (tok, tok, rc, rc, rc, cr, rc, cr) + (vec,) * 9
    return jax.shard_map(per_device, mesh=mesh, in_specs=in_specs, out_specs=out_specs, check_vma=False)
```
